32 devices in a mesh: det: 4 (over y, x), tm: 8 (over z, core).
Axes of the slice: x: 2, y: 2, z: 4, core: 2. Of those that a mesh axis runs over, the one named last changes fastest.
Arguments:
- timestream: float32 [2048, 4096], P('det', 'tm'), may hold values from -18 to 18
- sample_flags: int32 [2048, 4096], P('det', 'tm'), may hold values 0 or 1
- pointing: bfloat16 [32, 4, 128, 128], P('tm'), may hold values from -0.5 to 0.5
- tile_ids: int32 [32, 4], P('tm'), may hold values from 0 to 31
- block_offsets: int32 [32, 4], P('tm'), may hold values from 0 to 127
- tile_owner: int32 [32], replicated, may hold values from 0 to 31, each once
- det_gains: float32 [2048], P('det'), may hold values from 0.5 to 2
- mode_vectors: float32 [2048, 32], P('det'), may hold values from -0.125 to 0.125
- filter_gain: float32 [257], replicated, may hold values from 0.05 to 1
Outputs:
- tile_snr: float32 [32, 128, 128], P(('det', 'tm'))
- cleaned: bfloat16 [2048, 4096], P('det', 'tm')
The draws below stay inside these ranges and needn't reach their ends.
Inputs may be any that keep to these rules, and one draw needn't show every extreme that they name: Tile t is held in slot tile_owner[t]; slot q belongs to device q of det+tm in mesh order (one tile per device).
All inputs are finite; a program needn't handle non-finite values. No bound on the sum of `sample_flags` on one device may be relied on, other than what follows from the above.
Results may differ from the reference program's by a relative error of at most 0.0085.
Values may be sent and summed in bfloat16 or wider, within the bound.
No kernel may reach another device: no remote copies, remote signals or barrier semaphores. Data moves between devices by JAX's collectives and lax.ppermute only.
A program may use at most 64 MiB of HBM per device.

```python
import math
import jax
import jax.numpy as jnp
import numpy as np
from jax import lax

DET_DEV = 512
SAMP_DEV = 512
FLEN = 512
FBINS = 257
SEGLEN = 128
TILE = 128
BLOCKS_TILE = 128
KBLK = 4
MODES = 32
DETS = 2048
SAMPLES = 4096
SEG_DEV = 4
SEGMENTS = 32
NTILES = 32
N_DET = 4
N_TM = 8


def draw_timestream(key, part):
    common_key = jax.random.fold_in(key, 101)
    coupling_key = jax.random.fold_in(key, 202)
    noise_key = jax.random.fold_in(key, 303)
    common = jnp.clip(jax.random.normal(common_key, (SAMPLES,), jnp.float32), -6.0, 6.0)
    coupling = jnp.exp(jax.random.uniform(coupling_key, (DETS,), jnp.float32, math.log(0.5), math.log(2.0)))
    noise = jnp.clip(jax.random.normal(noise_key, (DETS, SAMPLES), jnp.float32), -6.0, 6.0)
    return coupling[:, None] * common[None, :] + noise


def with_ends(values, stream_key, least, largest):
    longest = values.shape.index(max(values.shape))
    spots = []
    for shift in (0, 1):
        where = [jax.random.randint(jax.random.fold_in(stream_key, axis), (), 0, length) for axis, length in enumerate(values.shape)]
        where[longest] = (where[longest] + shift) % values.shape[longest]
        spots.append(tuple(where))
    return values.at[spots[0]].set(least).at[spots[1]].set(largest)


def shard_levels(key, shape, cuts, smallest, high):
    factor_of, own = 1.0, jax.random.fold_in(key, 6)
    for dim, parts in cuts:
        steps = jnp.exp(jax.random.uniform(jax.random.fold_in(own, dim), (parts,), jnp.float32, smallest / len(cuts), high / len(cuts)))
        factor_of = factor_of * jnp.repeat(steps, shape[dim] // parts).reshape([-1 if axis == dim else 1 for axis in range(len(shape))])
    return factor_of


def cumulative_ranks(amount, skew):
    loads = [(1 << 20) // math.isqrt(rank ** skew) + 1 for rank in range(1, amount + 1)]
    deviation = 1 + sum(loads) // (1 << 30)
    return np.cumsum(np.array([max(1, weight // deviation) for weight in loads]))


def skewed_ids(rng, extent, amount, skew):
    listing = cumulative_ranks(amount, skew)
    ticket = jax.random.randint(jax.random.fold_in(rng, 1), extent, 0, int(listing[amount - 1]))
    rank = jnp.searchsorted(jnp.asarray(listing, jnp.int32), ticket, side="right")
    return jax.random.permutation(jax.random.fold_in(rng, 2), amount)[rank].astype(jnp.int32)


def centred(rng, dims, scale, bound, cuts=(), held_as=jnp.bfloat16):
    level = shard_levels(rng, dims, cuts, -0.22, 0.18) if cuts else 1.0
    array = jax.random.normal(rng, dims, jnp.float32) * scale * level
    return jnp.minimum(jnp.maximum(array, -bound), bound).astype(held_as)


def setup_inputs(seed: int = 0) -> dict:
    streams_of = jax.random.split(jax.random.key(seed), 10)
    timestream = draw_timestream(jax.random.fold_in(streams_of[9], 71), 0)
    sample_flags = with_ends((jax.random.randint(streams_of[1], (DETS, SAMPLES), 0, 8) < 1).astype(jnp.int32), jax.random.fold_in(streams_of[1], 1), 0, 1)
    pointing = centred(streams_of[2], (SEGMENTS, KBLK, SEGLEN, TILE), SEGLEN ** -0.5, 0.5, ((0, 8),))
    tile_ids = with_ends(skewed_ids(streams_of[3], (SEGMENTS, KBLK), NTILES, 2), jax.random.fold_in(streams_of[3], 3), 0, NTILES - 1).astype(jnp.int32)
    block_offsets = with_ends(jax.random.randint(streams_of[4], (SEGMENTS, KBLK), 0, BLOCKS_TILE), jax.random.fold_in(streams_of[4], 1), 0, BLOCKS_TILE - 1).astype(jnp.int32)
    tile_owner = jax.random.permutation(streams_of[5], NTILES).astype(jnp.int32)
    det_gains = jnp.clip(jnp.exp(math.log(2.0) - 1.3862944 * jax.random.uniform(streams_of[6], (DETS,), jnp.float32) ** shard_levels(streams_of[6], (DETS,), ((0, 4),), -0.2, 0.2)), 0.5, 2.0)
    mode_vectors = centred(streams_of[7], (DETS, MODES), DETS ** -0.5, 0.125, ((0, 4),), jnp.float32)
    filter_gain = jnp.clip(jnp.exp(jax.random.uniform(streams_of[8], (FBINS,), jnp.float32, math.log(0.05), math.log(1.0))), 0.05, 1.0)
    return dict(timestream=timestream, sample_flags=sample_flags, pointing=pointing, tile_ids=tile_ids, block_offsets=block_offsets, tile_owner=tile_owner, det_gains=det_gains, mode_vectors=mode_vectors, filter_gain=filter_gain)


def spectral_tables():
    position = lax.iota(jnp.int32, FLEN)
    phase_index = position[:, None] * position[None, :] % FLEN
    angles = phase_index.astype(jnp.float32) * (2.0 * math.pi / FLEN)
    return (jnp.cos(angles).astype(jnp.bfloat16), jnp.sin(angles).astype(jnp.bfloat16))

def filter_rows(residual, response, forward, inverse):
    sample_rows = residual.astype(jnp.bfloat16).reshape(-1, FLEN)
    spectrum = jnp.dot(sample_rows, forward, preferred_element_type=jnp.float32)
    shaped = (spectrum * response[None, :]).astype(jnp.bfloat16)
    filtered = jnp.dot(shaped, inverse, preferred_element_type=jnp.float32) / FLEN
    return filtered.reshape(residual.shape)

def reference(timestream, sample_flags, pointing, tile_ids, block_offsets, tile_owner, det_gains, mode_vectors, filter_gain):
    hi = lax.Precision.HIGHEST
    cosine, sine = spectral_tables()
    forward = jnp.concatenate([cosine, sine], axis=1)
    inverse = jnp.concatenate([cosine, sine], axis=0)
    full_gain = jnp.concatenate([filter_gain, filter_gain[1:FLEN // 2][::-1]])
    response = jnp.concatenate([full_gain, full_gain])
    keep = (1 - sample_flags).astype(jnp.float32)
    target_rows = (tile_owner[tile_ids].astype(jnp.int32) * BLOCKS_TILE + block_offsets).reshape(-1).astype(jnp.int32)
    point_float = pointing.astype(jnp.float32)
    squares = lax.optimization_barrier(jnp.sum(point_float * point_float, axis=2))
    weights = (jnp.sum(det_gains * det_gains) * squares).reshape(-1, TILE)
    tod_blocks = timestream.reshape(DETS, N_TM, SAMP_DEV).transpose(1, 0, 2)
    keep_blocks = keep.reshape(DETS, N_TM, SAMP_DEV).transpose(1, 0, 2)
    point_blocks = point_float.reshape(N_TM, SEG_DEV, KBLK, SEGLEN, TILE)
    group_gains = det_gains.reshape(N_DET, DET_DEV)
    total_rows = NTILES * BLOCKS_TILE

    def one_block(inputs):
        tod_part, keep_part, point_part, signal_part = inputs
        residual = (tod_part - det_gains[:, None] * signal_part[None, :]) * keep_part
        filtered = filter_rows(residual, response, forward, inverse)
        amplitudes = jnp.dot(mode_vectors.T, filtered, precision=hi)
        clean = filtered - jnp.dot(mode_vectors, amplitudes, precision=hi)
        summed = jnp.einsum('gd,gds->gs', group_gains, clean.reshape(N_DET, DET_DEV, SAMP_DEV), precision=hi)
        summed = summed.astype(jnp.bfloat16).astype(jnp.float32).reshape(N_DET, SEG_DEV, SEGLEN)
        projected = jnp.einsum('sktp,gst->skp', point_part, summed, precision=hi).reshape(-1, TILE)
        return (projected, clean.astype(jnp.bfloat16))
    zero_signal = jnp.zeros((N_TM, SAMP_DEV), jnp.float32)
    first_proj, unused_clean = lax.map(one_block, (tod_blocks, keep_blocks, point_blocks, zero_signal))
    psum = jnp.zeros((total_rows, TILE), jnp.float32).at[target_rows].add(first_proj.reshape(-1, TILE))
    wsum = jnp.zeros((total_rows, TILE), jnp.float32).at[target_rows].add(weights) + 1.0
    map_rows = psum / wsum
    map_half = map_rows.astype(jnp.bfloat16)
    fetched = map_half[target_rows].astype(jnp.float32).reshape(SEGMENTS, KBLK, TILE)
    signal = jnp.einsum('sktp,skp->st', point_float, fetched, precision=hi).reshape(N_TM, SAMP_DEV)
    second_proj, second_clean = lax.map(one_block, (tod_blocks, keep_blocks, point_blocks, signal))
    psum = jnp.zeros((total_rows, TILE), jnp.float32).at[target_rows].add(second_proj.reshape(-1, TILE))
    map_rows = map_rows + psum / wsum
    tile_snr = (map_rows * jnp.sqrt(wsum)).reshape(NTILES, BLOCKS_TILE, TILE)
    cleaned = second_clean.transpose(1, 0, 2).reshape(DETS, SAMPLES)
    return (tile_snr, cleaned)
```

```python
import functools
import math

import jax
import jax.numpy as jnp
import numpy as np
from jax import lax
from jax.experimental import pallas as pl
from jax.experimental.pallas import tpu as pltpu
from jax.sharding import PartitionSpec as P

F32 = jnp.float32
BF16 = jnp.bfloat16
LANES = 128
BASE = 128
DIGITS = 3
EXT = 16
NN = (((1,), (0,)), ((), ()))
NT = (((1,), (1,)), ((), ()))


def mm(a, b, dims=NN):
    return lax.dot_general(a, b, dims, preferred_element_type=F32)


def split(x):
    hi = x.astype(BF16)
    return hi, (x - hi.astype(F32)).astype(BF16)


def iota(shape, axis):
    return lax.broadcasted_iota(jnp.int32, shape, axis)


def cosine_table(flen, rows):
    f = np.arange(rows)[:, None]
    n = np.arange(flen)[None, :]
    scale = np.where((f == 0) | (f == flen // 2), 1.0, 2.0) / flen
    scale = np.where(f <= flen // 2, scale, 0.0)
    return (scale * np.cos(2.0 * math.pi * ((f * n) % flen) / flen)).astype(np.float32)


def sums_kernel(modes, ts_ref, flag_ref, v_ref, g_ref, msg_ref, acc1, acc2, small):
    step = pl.program_id(0)
    chunk, samples = ts_ref.shape
    keep = (1 - flag_ref[...]).astype(F32)
    x_hi, x_lo = split(ts_ref[...] * keep)
    v = v_ref[...]
    vt = v.T
    g = g_ref[...]
    row = iota((EXT, chunk), 0)
    left1 = jnp.concatenate([vt, jnp.where(row < 2, g, 0.0)], axis=0)
    left2 = jnp.concatenate([vt * g, jnp.where((row >= 2) & (row < 4), g * g, 0.0)], axis=0)
    hi1, lo1 = split(left1)
    hi2, lo2 = split(left2)
    n = modes + EXT
    both = mm(jnp.concatenate([hi1, lo1], axis=0), x_hi)
    part1 = both[:n] + both[n:] + mm(hi1, x_lo)
    both = mm(jnp.concatenate([hi2, lo2], axis=0), keep.astype(BF16))
    part2 = both[:n] + both[n:]
    u_row = (row >= 4) & (row < 6)
    v_wide = jnp.concatenate([v, jnp.zeros((chunk, LANES - modes), F32)], axis=1)
    u_part = lax.dot_general(
        jnp.where(u_row, g, 0.0), v_wide, NN, precision=lax.Precision.HIGHEST, preferred_element_type=F32
    )
    square = jnp.sum(g * g, axis=1, keepdims=True)
    r = iota((EXT, LANES), 0)
    here = (r >= 4) & (r < 6) & (iota((EXT, LANES), 1) == modes)
    u_part = u_part + jnp.where(here, square, 0.0)

    @pl.when(step == 0)
    def _():
        acc1[...] = part1
        acc2[...] = part2
        small[...] = u_part

    @pl.when(step > 0)
    def _():
        acc1[...] += part1
        acc2[...] += part2
        small[...] += u_part

    @pl.when(step == pl.num_programs(0) - 1)
    def _():
        msg_ref[0:modes] = acc1[0:modes].astype(BF16)
        msg_ref[modes : 2 * modes] = acc2[0:modes].astype(BF16)
        wide = jnp.concatenate([small[...], jnp.zeros((EXT, samples - LANES), F32)], axis=1)
        ext = acc1[modes:] + acc2[modes:] + wide
        hi = ext.astype(BF16).astype(F32)
        odd = iota((EXT, samples), 0) % 2 == 1
        msg_ref[2 * modes :] = jnp.where(odd, ext - hi, hi).astype(BF16)


def prep_kernel(seg, kblk, tids_ref, offs_ref, owner_ref, pos_ref, gain_ref, cos_ref, point_ref, v_ref,
                hhi_ref, hlo_ref, v3_ref, geo_ref, own_ref):
    flen = cos_ref.shape[1]
    gain8 = jnp.broadcast_to(gain_ref[...], (8, gain_ref.shape[1]))
    h = lax.dot_general(gain8, cos_ref[...], NN, precision=lax.Precision.HIGHEST, preferred_element_type=F32)
    base = jnp.broadcast_to(h[0:1], (LANES, flen))
    base = pltpu.roll(base, 0, 1, stride=1, stride_axis=0)
    base_hi, base_lo = split(base)
    blocks = flen // LANES
    for a in range(blocks):
        for b in range(blocks):
            c = (b - a) % blocks
            to = (slice(a * LANES, (a + 1) * LANES), slice(b * LANES, (b + 1) * LANES))
            hhi_ref[to] = base_hi[:, c * LANES : (c + 1) * LANES]
            hlo_ref[to] = base_lo[:, c * LANES : (c + 1) * LANES]
    vt = v_ref[...].T
    vhi = vt.astype(BF16).astype(F32)
    pad = jnp.zeros((LANES - 3 * vt.shape[0], vt.shape[1]), F32)
    v3_ref[...] = jnp.concatenate([vhi, vhi, vt - vhi, pad], axis=0).T.astype(BF16)
    listed = seg * kblk
    row16 = iota((listed, LANES), 0)
    lane16 = iota((listed, LANES), 1)
    first = pos_ref[0] * listed
    lane_blocks = pos_ref[1]
    squares = jnp.zeros((listed, LANES), F32)
    ids = jnp.zeros((listed, LANES), F32)
    own = jnp.zeros((listed, LANES), F32)
    for k in range(kblk):
        for s in range(seg):
            j = k * seg + s
            p = point_ref[s, k].astype(F32)
            squares = jnp.where(row16 == j, jnp.sum(p * p, axis=0, keepdims=True), squares)
            target = owner_ref[tids_ref[s, k]] * LANES + offs_ref[s, k]
            own = jnp.where(row16 == j, target.astype(F32), own)
            place = first + j
            digit = target
            for d in range(DIGITS):
                at = (row16 == d * lane_blocks + place // LANES) & (lane16 == place % LANES)
                ids = jnp.where(at, (digit % BASE).astype(F32), ids)
                digit = digit // BASE
    geo_ref[0:listed] = squares.astype(BF16)
    geo_ref[listed:] = ids.astype(BF16)
    own_ref[...] = own


def matvec(b, hhi, hlo):
    hi, lo = split(b)
    row = iota((EXT, b.shape[1]), 0)
    left = jnp.where(row == 0, hi.astype(F32), jnp.where(row == 1, lo.astype(F32), 0.0)).astype(BF16)
    z = mm(left, hhi) + mm(left, hlo)
    return z[0:1] + z[1:2]


def project(z, point_ref, seg, kblk):
    samples = z.shape[1]
    listed = seg * kblk
    hi, lo = split(z)
    row = iota((2 * listed, samples), 0)
    lane = iota((2 * listed, samples), 1)
    wide = jnp.where(row < listed, hi.astype(F32), lo.astype(F32))
    wide = jnp.where(lane // (samples // seg) == row % seg, wide, 0.0)
    out = jnp.zeros((2 * listed, point_ref.shape[3]), F32)
    for k in range(kblk):
        left = jnp.where((row % listed) // seg == k, wide, 0.0).astype(BF16)
        out = out + mm(left, point_ref[:, k].reshape(samples, -1))
    return out[:listed] + out[listed:]


def first_kernel(modes, seg, kblk, m0, m1, m2, m3, hhi_ref, hlo_ref, point_ref, geo_ref,
                 bq_ref, vec_ref, send_ref):
    tot = m0[...].astype(F32) + m1[...].astype(F32) + m2[...].astype(F32) + m3[...].astype(F32)
    bq_ref[...] = tot[0 : 2 * modes]
    ext = tot[2 * modes :]
    u_row = ext[4:5, 0:LANES] + ext[5:6, 0:LANES]
    u_col = jnp.sum(jnp.where(iota((modes, LANES), 0) == iota((modes, LANES), 1), u_row, 0.0), axis=1, keepdims=True)
    square = jnp.sum(jnp.where(iota((1, LANES), 1) == modes, u_row, 0.0), axis=1, keepdims=True)
    b1 = ext[0:1] + ext[1:2] - jnp.sum(u_col * tot[0:modes], axis=0, keepdims=True)
    b2 = ext[2:3] + ext[3:4] - jnp.sum(u_col * tot[modes : 2 * modes], axis=0, keepdims=True)
    row = iota((8, b1.shape[1]), 0)
    vec_ref[...] = jnp.where(row == 0, b1, jnp.where(row == 1, b2, jnp.where(row == 2, square, 0.0)))
    z = matvec(b1, hhi_ref[...], hlo_ref[...])
    proj = project(z, point_ref, seg, kblk).astype(BF16)
    geo = geo_ref[...]
    listed = seg * kblk
    for t in range(send_ref.shape[0]):
        send_ref[t, 0:listed] = proj
        send_ref[t, listed:] = geo


def lane_ids(all_ref, listed, blocks, b):
    ids = jnp.sum(all_ref[:, 2 * listed :].astype(F32), axis=0)
    out = ids[b : b + 1]
    for d in range(1, DIGITS):
        out = out + float(BASE**d) * ids[d * blocks + b : d * blocks + b + 1]
    return out


def second_kernel(seg, kblk, all_ref, own_ref, vec_ref, hhi_ref, hlo_ref, point_ref, sig_ref, send_ref):
    listed = seg * kblk
    blocks = all_ref.shape[0] * listed // LANES
    samples = vec_ref.shape[1]
    per = LANES // listed
    own = own_ref[...]
    psum = jnp.zeros((listed, LANES), F32)
    wsum = jnp.zeros((listed, LANES), F32)
    for b in range(blocks):
        same = (own == lane_ids(all_ref, listed, blocks, b)).astype(F32).astype(BF16)
        part = all_ref[b * per : (b + 1) * per]
        psum = psum + mm(same, part[:, 0:listed].reshape(LANES, LANES))
        wsum = wsum + mm(same, part[:, listed : 2 * listed].reshape(LANES, LANES))
    square = vec_ref[2:3, 0:LANES]
    fetched = (psum / (1.0 + square * wsum)).astype(BF16)
    row = iota((listed, samples), 0)
    lane = iota((listed, samples), 1)
    spread = jnp.zeros((listed, samples), F32)
    for k in range(kblk):
        out = mm(fetched, point_ref[:, k].reshape(samples, -1), NT)
        spread = spread + jnp.where((row // seg == k) & (lane // (samples // seg) == row % seg), out, 0.0)
    sig = jnp.sum(spread, axis=0, keepdims=True)
    sig_ref[...] = jnp.broadcast_to(sig, sig_ref.shape)
    z = matvec(vec_ref[0:1] - vec_ref[1:2] * sig, hhi_ref[...], hlo_ref[...])
    proj = project(z, point_ref, seg, kblk).astype(BF16)
    for t in range(send_ref.shape[0]):
        send_ref[t] = proj


def clean_kernel(modes, ts_ref, flag_ref, g_ref, v3_ref, bq_ref, sig_ref, hhi_ref, hlo_ref, out_ref):
    chunk = ts_ref.shape[0]
    sig = sig_ref[0:1]
    q_hi, q_lo = split(bq_ref[0:modes] - bq_ref[modes : 2 * modes] * sig)
    pad = jnp.zeros((LANES - 3 * modes, q_hi.shape[1]), BF16)
    q3 = jnp.concatenate([q_hi, q_lo, q_hi, pad], axis=0)
    eye = iota((chunk, chunk), 0) == iota((chunk, chunk), 1)
    g_col = jnp.sum(jnp.where(eye, g_ref[...], 0.0), axis=1, keepdims=True)
    keep = (1 - flag_ref[...]).astype(F32)
    rest = (ts_ref[...] - g_col * sig) * keep - mm(v3_ref[...], q3)
    rest = rest.astype(BF16)
    out_ref[...] = (mm(rest, hhi_ref[...]) + mm(rest, hlo_ref[...])).astype(BF16)


def tile_kernel(seg, kblk, first_ref, all_ref, all2_ref, vec_ref, out_ref):
    listed = seg * kblk
    blocks = all_ref.shape[0] * listed // LANES
    per = LANES // listed
    psum1 = jnp.zeros((LANES, LANES), F32)
    psum2 = jnp.zeros((LANES, LANES), F32)
    wsum = jnp.zeros((LANES, LANES), F32)
    mine = (iota((LANES, LANES), 0) + first_ref[0]).astype(F32)
    for b in range(blocks):
        same = (mine == lane_ids(all_ref, listed, blocks, b)).astype(F32).astype(BF16)
        part = all_ref[b * per : (b + 1) * per]
        psum1 = psum1 + mm(same, part[:, 0:listed].reshape(LANES, LANES))
        wsum = wsum + mm(same, part[:, listed : 2 * listed].reshape(LANES, LANES))
        psum2 = psum2 + mm(same, all2_ref[b * per : (b + 1) * per].reshape(LANES, LANES))
    wsum = 1.0 + vec_ref[2:3, 0:LANES] * wsum
    out_ref[0] = (psum1 / wsum + psum2 / wsum) * jnp.sqrt(wsum)


VM = pl.BlockSpec(memory_space=pltpu.VMEM)
SM = pl.BlockSpec(memory_space=pltpu.SMEM)


def shape(dims, dtype=F32):
    return jax.ShapeDtypeStruct(dims, dtype)


def others(x, axis, n):
    if n & (n - 1) == 0:
        pairs = [[(i, i ^ k) for i in range(n)] for k in range(1, n)]
    else:
        pairs = [[(i, (i + k) % n) for i in range(n)] for k in range(1, n)]
    return [lax.ppermute(x, axis, p) for p in pairs]


def shards(n_det, n_tm, timestream, sample_flags, pointing, tile_ids, block_offsets, tile_owner, det_gains,
           mode_vectors, filter_gain):
    dets, samples = timestream.shape
    modes = mode_vectors.shape[1]
    seg, kblk = tile_ids.shape
    listed = seg * kblk
    chunk = LANES
    grid = (dets // chunk,)
    g = det_gains.reshape(1, dets)
    msg = pl.pallas_call(
        functools.partial(sums_kernel, modes),
        grid=grid,
        in_specs=[
            pl.BlockSpec((chunk, samples), lambda i: (i, 0)),
            pl.BlockSpec((chunk, samples), lambda i: (i, 0)),
            pl.BlockSpec((chunk, modes), lambda i: (i, 0)),
            pl.BlockSpec((1, chunk), lambda i: (0, i)),
        ],
        out_specs=pl.BlockSpec((2 * modes + EXT, samples), lambda i: (0, 0)),
        out_shape=shape((2 * modes + EXT, samples), BF16),
        scratch_shapes=[
            pltpu.VMEM((modes + EXT, samples), F32),
            pltpu.VMEM((modes + EXT, samples), F32),
            pltpu.VMEM((EXT, LANES), F32),
        ],
        name="sums",
    )(timestream, sample_flags, mode_vectors, g)
    parts = [msg] + others(msg, "det", n_det)

    rows = -(-filter_gain.shape[0] // LANES) * LANES
    gain = jnp.pad(filter_gain, (0, rows - filter_gain.shape[0])).reshape(1, rows)
    tm_at = lax.axis_index("tm")
    place = jnp.stack([tm_at, jnp.int32(n_tm * listed // LANES)]).astype(jnp.int32)
    hhi, hlo, v3, geo, own = pl.pallas_call(
        functools.partial(prep_kernel, seg, kblk),
        in_specs=[SM, SM, SM, SM, VM, VM, VM, VM],
        out_specs=[VM] * 5,
        out_shape=[
            shape((samples, samples), BF16),
            shape((samples, samples), BF16),
            shape((dets, LANES), BF16),
            shape((2 * listed, LANES), BF16),
            shape((listed, LANES)),
        ],
        cost_estimate=pl.CostEstimate(flops=10**8, bytes_accessed=3 * 10**6, transcendentals=0),
        name="prep",
    )(tile_ids, block_offsets, tile_owner, place, gain, jnp.asarray(cosine_table(samples, rows)), pointing,
      mode_vectors)

    bq, vec, send = pl.pallas_call(
        functools.partial(first_kernel, modes, seg, kblk),
        in_specs=[VM] * 8,
        out_specs=[VM] * 3,
        out_shape=[
            shape((2 * modes, samples)),
            shape((8, samples)),
            shape((n_tm, 3 * listed, LANES), BF16),
        ],
        name="first",
    )(*parts, hhi, hlo, pointing, geo)
    everyone = lax.all_to_all(send, "tm", 0, 0)

    sig, send = pl.pallas_call(
        functools.partial(second_kernel, seg, kblk),
        in_specs=[VM] * 6,
        out_specs=[VM] * 2,
        out_shape=[shape((8, samples)), shape((n_tm, listed, LANES), BF16)],
        name="second",
    )(everyone, own, vec, hhi, hlo, pointing)
    everyone2 = lax.all_to_all(send, "tm", 0, 0)

    cleaned = pl.pallas_call(
        functools.partial(clean_kernel, modes),
        grid=grid,
        in_specs=[
            pl.BlockSpec((chunk, samples), lambda i: (i, 0)),
            pl.BlockSpec((chunk, samples), lambda i: (i, 0)),
            pl.BlockSpec((1, chunk), lambda i: (0, i)),
            pl.BlockSpec((chunk, LANES), lambda i: (i, 0)),
            pl.BlockSpec((2 * modes, samples), lambda i: (0, 0)),
            pl.BlockSpec((8, samples), lambda i: (0, 0)),
            pl.BlockSpec((samples, samples), lambda i: (0, 0)),
            pl.BlockSpec((samples, samples), lambda i: (0, 0)),
        ],
        out_specs=pl.BlockSpec((chunk, samples), lambda i: (i, 0)),
        out_shape=shape((dets, samples), BF16),
        cost_estimate=pl.CostEstimate(flops=10**9, bytes_accessed=4 * 10**6, transcendentals=0),
        name="clean",
    )(timestream, sample_flags, g, v3, bq, sig, hhi, hlo)

    first_row = (lax.axis_index(("det", "tm")) * LANES).reshape(1).astype(jnp.int32)
    tile = pl.pallas_call(
        functools.partial(tile_kernel, seg, kblk),
        in_specs=[SM, VM, VM, VM],
        out_specs=VM,
        out_shape=shape((1, LANES, LANES)),
        name="tile",
    )(first_row, everyone, everyone2, vec)
    return tile, cleaned


def solution(mesh):
    return jax.shard_map(
        functools.partial(shards, mesh.shape["det"], mesh.shape["tm"]),
        mesh=mesh,
        in_specs=(
            P("det", "tm"),
            P("det", "tm"),
            P("tm", None, None, None),
            P("tm", None),
            P("tm", None),
            P(),
            P("det"),
            P("det", None),
            P(),
        ),
        out_specs=(P(("det", "tm"), None, None), P("det", "tm")),
        check_vma=False,
    )
```

```python
import functools
import math

import jax
import jax.numpy as jnp
import numpy as np
from jax import lax
from jax.experimental import pallas as pl
from jax.experimental.pallas import tpu as pltpu
from jax.sharding import PartitionSpec as P

F32 = jnp.float32
BF16 = jnp.bfloat16
LANES = 128
BASE = 128
EXT = 16
NN = (((1,), (0,)), ((), ()))
NT = (((1,), (1,)), ((), ()))


def mm(a, b, dims=NN):
    return lax.dot_general(a, b, dims, preferred_element_type=F32)


def split(x):
    hi = x.astype(BF16)
    return hi, (x - hi.astype(F32)).astype(BF16)


def iota(shape, axis):
    return lax.broadcasted_iota(jnp.int32, shape, axis)


def cosine_table(flen, rows):
    f = np.arange(rows)[:, None]
    n = np.arange(flen)[None, :]
    scale = np.where((f == 0) | (f == flen // 2), 1.0, 2.0) / flen
    scale = np.where(f <= flen // 2, scale, 0.0)
    return (scale * np.cos(2.0 * math.pi * ((f * n) % flen) / flen)).astype(np.float32)


def sums_kernel(modes, parts, ts_hbm, flag_hbm, v_hbm, g_hbm, msg_ref, ts_ref, keep_ref, v_ref, g_ref, flag_ref, sem,
                small_sem):
    dets, samples = ts_ref.shape
    chunk = dets // parts
    smalls = [
        pltpu.make_async_copy(v_hbm, v_ref, small_sem.at[0]),
        pltpu.make_async_copy(g_hbm, g_ref, small_sem.at[1]),
    ]
    for copy in smalls:
        copy.start()
    pairs = []
    for i in range(parts):
        rows = pl.ds(i * chunk, chunk)
        pairs.append(
            (
                pltpu.make_async_copy(ts_hbm.at[rows], ts_ref.at[rows], sem.at[0, i]),
                pltpu.make_async_copy(flag_hbm.at[rows], flag_ref.at[rows], sem.at[1, i]),
            )
        )
    for pair in pairs:
        for copy in pair:
            copy.start()
    for copy in smalls:
        copy.wait()
    vt = v_ref[...]
    g = g_ref[...]
    row = iota((EXT, dets), 0)
    left1 = jnp.concatenate([vt, jnp.where(row < 2, g, 0.0)], axis=0)
    left2 = jnp.concatenate([vt * g, jnp.where((row >= 2) & (row < 4), g * g, 0.0)], axis=0)
    hi1, lo1 = split(left1)
    hi2, lo2 = split(left2)
    left1 = jnp.concatenate([hi1, lo1], axis=0)
    left2 = jnp.concatenate([hi2, lo2], axis=0)
    u = jnp.sum(vt * g, axis=1, keepdims=True)
    square = jnp.sum(g * g, axis=1, keepdims=True)
    lane = iota((modes, samples), 1)
    u = jnp.sum(jnp.where(lane == iota((modes, samples), 0), u, 0.0), axis=0, keepdims=True)
    u = jnp.where(iota((1, samples), 1) == modes, square, u)
    n = modes + EXT
    acc1 = jnp.zeros((n, samples), F32)
    acc2 = jnp.zeros((n, samples), F32)
    for i in range(parts):
        for copy in pairs[i]:
            copy.wait()
        at = slice(i * chunk, (i + 1) * chunk)
        keep = (1 - flag_ref[at]).astype(F32)
        keep_ref[at] = keep.astype(BF16)
        x_hi, x_lo = split(ts_ref[at] * keep)
        both = mm(left1[:, at], x_hi)
        acc1 = acc1 + (both[:n] + both[n:]) + mm(hi1[:, at], x_lo)
        both = mm(left2[:, at], keep.astype(BF16))
        acc2 = acc2 + (both[:n] + both[n:])
    msg_ref[0:modes] = acc1[0:modes].astype(BF16)
    msg_ref[modes : 2 * modes] = acc2[0:modes].astype(BF16)
    row = iota((EXT, samples), 0)
    ext = acc1[modes:] + acc2[modes:] + jnp.where((row >= 4) & (row < 6), u, 0.0)
    hi = ext.astype(BF16).astype(F32)
    msg_ref[2 * modes :] = jnp.where(row % 2 == 1, ext - hi, hi).astype(BF16)


def prep_kernel(seg, kblk, lane_blocks, digits, tids_ref, offs_ref, owner_ref, gain_ref, cos_ref, point_ref, v_ref,
                h2_ref, pn_ref, pt_ref, v3_ref, geo_ref, own_ref, wide_ref):
    flen = cos_ref.shape[1]
    wide_ref[...] = jnp.zeros_like(wide_ref)
    wide_ref[0:1, 0 : gain_ref.shape[1]] = gain_ref[...]
    h = lax.dot_general(wide_ref[...], cos_ref[...], NN, precision=lax.Precision.HIGHEST, preferred_element_type=F32)
    base = jnp.broadcast_to(h[0:1], (LANES, flen))
    base = pltpu.roll(base, 0, 1, stride=1, stride_axis=0)
    base_hi, base_lo = split(base)
    blocks = flen // LANES
    for a in range(blocks):
        for b in range(blocks):
            c = (b - a) % blocks
            to = slice(b * LANES, (b + 1) * LANES)
            h2_ref[a * LANES : (a + 1) * LANES, to] = base_hi[:, c * LANES : (c + 1) * LANES]
            h2_ref[flen + a * LANES : flen + (a + 1) * LANES, to] = base_lo[:, c * LANES : (c + 1) * LANES]
    vt = v_ref[...]
    vhi = vt.astype(BF16).astype(F32)
    pad = jnp.zeros((LANES - 3 * vt.shape[0], vt.shape[1]), F32)
    v3_ref[...] = jnp.concatenate([vhi, vhi, vt - vhi, pad], axis=0).T.astype(BF16)
    listed = seg * kblk
    row16 = iota((listed, LANES), 0)
    first = lax.axis_index("tm") * listed
    squares = jnp.zeros((listed, LANES), F32)
    ext = geo_ref.shape[0] - listed
    row_x = iota((ext, LANES), 0)
    lane_x = iota((ext, LANES), 1)
    ids = jnp.zeros((ext, LANES), F32)
    own = jnp.zeros((listed, LANES), F32)
    for k in range(kblk):
        for s in range(seg):
            j = k * seg + s
            p = point_ref[s, k]
            span, tile = p.shape
            pn_ref[s * span : (s + 1) * span, k * tile : (k + 1) * tile] = p
            pt_ref[k * tile : (k + 1) * tile, s * span : (s + 1) * span] = p.T
            p = p.astype(F32)
            squares = jnp.where(row16 == j, jnp.sum(p * p, axis=0, keepdims=True), squares)
            target = owner_ref[tids_ref[s, k]] * LANES + offs_ref[s, k]
            own = jnp.where(row16 == j, target.astype(F32), own)
            place = first + j
            digit = target
            for d in range(digits):
                at = (row_x == d * lane_blocks + place // LANES) & (lane_x == place % LANES)
                ids = jnp.where(at, (digit % BASE).astype(F32), ids)
                digit = digit // BASE
    geo_ref[0:listed] = squares.astype(BF16)
    geo_ref[listed:] = ids.astype(BF16)
    own_ref[...] = own


def filtered(b, h2_ref):
    flen = b.shape[1]
    hi, lo = split(b)
    row = iota((EXT, flen), 0)
    left = jnp.where(row == 0, hi.astype(F32), jnp.where(row == 1, lo.astype(F32), 0.0)).astype(BF16)
    z = mm(left, h2_ref[0:flen]) + mm(left, h2_ref[flen:])
    return z[0:1] + z[1:2]


def project(z, pn_ref, seg, kblk):
    samples = z.shape[1]
    listed = seg * kblk
    hi, lo = split(z)
    row = iota((2 * listed, samples), 0)
    lane = iota((2 * listed, samples), 1)
    wide = jnp.where(row < listed, hi.astype(F32), lo.astype(F32))
    wide = jnp.where(lane // (samples // seg) == row % seg, wide, 0.0).astype(BF16)
    out = mm(wide, pn_ref[...])
    out = out[:listed] + out[listed:]
    row = iota((listed, LANES), 0)
    proj = out[:, 0:LANES]
    for k in range(1, kblk):
        proj = jnp.where(row // seg == k, out[:, k * LANES : (k + 1) * LANES], proj)
    return proj


def first_kernel(modes, seg, kblk, m0, m1, m2, m3, h2_ref, pn_ref, geo_ref,
                 bq_ref, vec_ref, send_ref):
    tot = m0[...].astype(F32) + m1[...].astype(F32) + m2[...].astype(F32) + m3[...].astype(F32)
    bq_ref[...] = tot[0 : 2 * modes]
    ext = tot[2 * modes :]
    u_row = ext[4:5, 0:LANES] + ext[5:6, 0:LANES]
    u_col = jnp.sum(jnp.where(iota((modes, LANES), 0) == iota((modes, LANES), 1), u_row, 0.0), axis=1, keepdims=True)
    square = jnp.sum(jnp.where(iota((1, LANES), 1) == modes, u_row, 0.0), axis=1, keepdims=True)
    b1 = ext[0:1] + ext[1:2] - jnp.sum(u_col * tot[0:modes], axis=0, keepdims=True)
    b2 = ext[2:3] + ext[3:4] - jnp.sum(u_col * tot[modes : 2 * modes], axis=0, keepdims=True)
    row = iota((8, b1.shape[1]), 0)
    vec_ref[...] = jnp.where(row == 0, b1, jnp.where(row == 1, b2, jnp.where(row == 2, square, 0.0)))
    z = filtered(b1, h2_ref)
    proj = project(z, pn_ref, seg, kblk).astype(BF16)
    geo = geo_ref[...]
    listed = seg * kblk
    for t in range(send_ref.shape[0]):
        send_ref[t, 0:listed] = proj
        send_ref[t, listed:] = geo


def lane_ids(all_ref, listed, blocks, digits, b):
    ids = jnp.sum(all_ref[:, 2 * listed :].astype(F32), axis=0)
    out = ids[b : b + 1]
    for d in range(1, digits):
        out = out + float(BASE**d) * ids[d * blocks + b : d * blocks + b + 1]
    return out


def second_kernel(seg, kblk, digits, all_ref, own_ref, vec_ref, h2_ref, pn_ref, pt_ref, sig_ref, send_ref):
    listed = seg * kblk
    blocks = all_ref.shape[0] * listed // LANES
    samples = vec_ref.shape[1]
    per = LANES // listed
    own = own_ref[...]
    psum = jnp.zeros((listed, LANES), F32)
    wsum = jnp.zeros((listed, LANES), F32)
    for b in range(blocks):
        same = (own == lane_ids(all_ref, listed, blocks, digits, b)).astype(F32).astype(BF16)
        part = all_ref[b * per : (b + 1) * per]
        psum = psum + mm(same, part[:, 0:listed].reshape(LANES, LANES))
        wsum = wsum + mm(same, part[:, listed : 2 * listed].reshape(LANES, LANES))
    square = vec_ref[2:3, 0:LANES]
    fetched = (psum / (1.0 + square * wsum)).astype(BF16)
    row = iota((listed, LANES), 0)
    wide = [jnp.where(row // seg == k, fetched.astype(F32), 0.0).astype(BF16) for k in range(kblk)]
    spread = mm(jnp.concatenate(wide, axis=1), pt_ref[...])
    row = iota((listed, samples), 0)
    lane = iota((listed, samples), 1)
    sig = jnp.sum(jnp.where(lane // (samples // seg) == row % seg, spread, 0.0), axis=0, keepdims=True)
    sig_ref[...] = jnp.broadcast_to(sig, sig_ref.shape)
    z = filtered(vec_ref[0:1] - vec_ref[1:2] * sig, h2_ref)
    proj = project(z, pn_ref, seg, kblk).astype(BF16)
    for t in range(send_ref.shape[0]):
        send_ref[t] = proj


def clean_kernel(seg, kblk, digits, modes, parts, ts_ref, keep_ref, g_ref, v3_ref, bq_ref, sig_ref, h2_ref,
                 all_ref, vec_ref, out_hbm, base_ref, scale_ref, same_ref, out_ref, sem):
    dets, samples = ts_ref.shape
    chunk = dets // parts
    sig = sig_ref[0:1]
    q_hi, q_lo = split(bq_ref[0:modes] - bq_ref[modes : 2 * modes] * sig)
    pad = jnp.zeros((LANES - 3 * modes, samples), BF16)
    q3 = jnp.concatenate([q_hi, q_lo, q_hi, pad], axis=0)
    eye = iota((chunk, chunk), 0) == iota((chunk, chunk), 1)
    copies = []
    for i in range(parts):
        at = slice(i * chunk, (i + 1) * chunk)
        g_col = jnp.sum(jnp.where(eye, g_ref[:, at], 0.0), axis=1, keepdims=True)
        rest = (ts_ref[at] - g_col * sig) * keep_ref[at].astype(F32) - mm(v3_ref[at], q3)
        rest = rest.astype(BF16)
        out_ref[at] = (mm(rest, h2_ref[0:samples]) + mm(rest, h2_ref[samples:])).astype(BF16)
        rows = pl.ds(i * chunk, chunk)
        copy = pltpu.make_async_copy(out_ref.at[rows], out_hbm.at[rows], sem.at[i])
        copy.start()
        copies.append(copy)
    listed = seg * kblk
    blocks = all_ref.shape[0] * listed // LANES
    per = LANES // listed
    psum = jnp.zeros((LANES, LANES), F32)
    wsum = jnp.zeros((LANES, LANES), F32)
    first = (lax.axis_index("det") * lax.axis_size("tm") + lax.axis_index("tm")) * LANES
    mine = (iota((LANES, LANES), 0) + first).astype(F32)
    for b in range(blocks):
        same = (mine == lane_ids(all_ref, listed, blocks, digits, b)).astype(F32).astype(BF16)
        same_ref[b] = same
        part = all_ref[b * per : (b + 1) * per]
        psum = psum + mm(same, part[:, 0:listed].reshape(LANES, LANES))
        wsum = wsum + mm(same, part[:, listed : 2 * listed].reshape(LANES, LANES))
    wsum = 1.0 + vec_ref[2:3, 0:LANES] * wsum
    scale = jnp.sqrt(wsum) / wsum
    scale_ref[...] = scale
    base_ref[...] = psum * scale
    for copy in copies:
        copy.wait()


def tile_kernel(all2_ref, base_ref, scale_ref, same_ref, out_ref):
    per = LANES // all2_ref.shape[1]
    psum = jnp.zeros((LANES, LANES), F32)
    for b in range(same_ref.shape[0]):
        psum = psum + mm(same_ref[b], all2_ref[b * per : (b + 1) * per].reshape(LANES, LANES))
    out_ref[0] = base_ref[...] + psum * scale_ref[...]


VM = pl.BlockSpec(memory_space=pltpu.VMEM)
HB = pl.BlockSpec(memory_space=pltpu.HBM)
SM = pl.BlockSpec(memory_space=pltpu.SMEM)
GRANT = pltpu.CompilerParams(vmem_limit_bytes=12 * 2**20)


def shape(dims, dtype=F32):
    return jax.ShapeDtypeStruct(dims, dtype)


def others(x, axis, n):
    if n & (n - 1) == 0:
        pairs = [[(i, i ^ k) for i in range(n)] for k in range(1, n)]
    else:
        pairs = [[(i, (i + k) % n) for i in range(n)] for k in range(1, n)]
    return [lax.ppermute(x, axis, p) for p in pairs]


def shards(n_det, n_tm, timestream, sample_flags, pointing, tile_ids, block_offsets, tile_owner, det_gains,
           mode_vectors, filter_gain):
    dets, samples = timestream.shape
    modes = mode_vectors.shape[1]
    seg, kblk = tile_ids.shape
    listed = seg * kblk
    parts = dets // LANES
    lane_blocks = n_tm * listed // LANES
    digits = -(-int(tile_owner.shape[0] * LANES - 1).bit_length() // 7)
    id_rows = -(-digits * lane_blocks // 8) * 8
    inputs = (timestream, sample_flags, mode_vectors.T, det_gains.reshape(1, dets))
    msg, ts, keep, vt, g = pl.pallas_call(
        functools.partial(sums_kernel, modes, parts),
        in_specs=[HB] * 4,
        out_specs=[VM] * 5,
        out_shape=[
            shape((2 * modes + EXT, samples), BF16),
            shape((dets, samples)),
            shape((dets, samples), BF16),
            shape((modes, dets)),
            shape((1, dets)),
        ],
        scratch_shapes=[
            pltpu.VMEM((dets, samples), jnp.int32),
            pltpu.SemaphoreType.DMA((2, parts)),
            pltpu.SemaphoreType.DMA((2,)),
        ],
        compiler_params=GRANT,
        name="sums",
    )(*(pltpu.with_memory_space_constraint(x, pltpu.HBM) for x in inputs))
    parts_of_all = [msg] + others(msg, "det", n_det)

    rows = -(-filter_gain.shape[0] // LANES) * LANES
    h2, pn, pt, v3, geo, own = pl.pallas_call(
        functools.partial(prep_kernel, seg, kblk, lane_blocks, digits),
        in_specs=[SM, SM, SM, VM, VM, VM, VM],
        out_specs=[VM] * 6,
        out_shape=[
            shape((2 * samples, samples), BF16),
            shape((samples, kblk * LANES), BF16),
            shape((kblk * LANES, samples), BF16),
            shape((dets, LANES), BF16),
            shape((listed + id_rows, LANES), BF16),
            shape((listed, LANES)),
        ],
        scratch_shapes=[pltpu.VMEM((8, rows), F32)],
        cost_estimate=pl.CostEstimate(flops=10**8, bytes_accessed=3 * 10**6, transcendentals=0),
        compiler_params=GRANT,
        name="prep",
    )(tile_ids, block_offsets, tile_owner, filter_gain.reshape(1, -1), jnp.asarray(cosine_table(samples, rows)),
      pointing, vt)

    bq, vec, send = pl.pallas_call(
        functools.partial(first_kernel, modes, seg, kblk),
        in_specs=[VM] * 7,
        out_specs=[VM] * 3,
        out_shape=[
            shape((2 * modes, samples)),
            shape((8, samples)),
            shape((n_tm, 2 * listed + id_rows, LANES), BF16),
        ],
        compiler_params=GRANT,
        name="first",
    )(*parts_of_all, h2, pn, geo)
    everyone = lax.all_to_all(send, "tm", 0, 0)

    sig, send = pl.pallas_call(
        functools.partial(second_kernel, seg, kblk, digits),
        in_specs=[VM] * 6,
        out_specs=[VM] * 2,
        out_shape=[shape((8, samples)), shape((n_tm, listed, LANES), BF16)],
        compiler_params=GRANT,
        name="second",
    )(everyone, own, vec, h2, pn, pt)
    everyone2 = lax.all_to_all(send, "tm", 0, 0)

    cleaned, base, scale, same = pl.pallas_call(
        functools.partial(clean_kernel, seg, kblk, digits, modes, parts),
        in_specs=[VM] * 9,
        out_specs=[HB, VM, VM, VM],
        out_shape=[
            shape((dets, samples), BF16),
            shape((LANES, LANES)),
            shape((LANES, LANES)),
            shape((lane_blocks, LANES, LANES), BF16),
        ],
        scratch_shapes=[pltpu.VMEM((dets, samples), BF16), pltpu.SemaphoreType.DMA((parts,))],
        cost_estimate=pl.CostEstimate(flops=10**9, bytes_accessed=4 * 10**6, transcendentals=0),
        compiler_params=GRANT,
        name="clean",
    )(ts, keep, g, v3, bq, sig, h2, everyone, vec)

    tile = pl.pallas_call(
        tile_kernel,
        in_specs=[VM] * 4,
        out_specs=VM,
        out_shape=shape((1, LANES, LANES)),
        compiler_params=GRANT,
        name="tile",
    )(everyone2, base, scale, same)
    return tile, cleaned


def solution(mesh):
    return jax.shard_map(
        functools.partial(shards, mesh.shape["det"], mesh.shape["tm"]),
        mesh=mesh,
        in_specs=(
            P("det", "tm"),
            P("det", "tm"),
            P("tm", None, None, None),
            P("tm", None),
            P("tm", None),
            P(),
            P("det"),
            P("det", None),
            P(),
        ),
        out_specs=(P(("det", "tm"), None, None), P("det", "tm")),
        check_vma=False,
    )
```

```python
import functools
import math

import jax
import jax.numpy as jnp
import numpy as np
from jax import lax
from jax.experimental import pallas as pl
from jax.experimental.pallas import tpu as pltpu
from jax.sharding import PartitionSpec as P

F32 = jnp.float32
BF16 = jnp.bfloat16
LANES = 128
BASE = 128
EXT = 16
MORE = 8
NN = (((1,), (0,)), ((), ()))
NT = (((1,), (1,)), ((), ()))


def mm(a, b, dims=NN):
    return lax.dot_general(a, b, dims, preferred_element_type=F32)


def split(x):
    hi = x.astype(BF16)
    return hi, (x - hi.astype(F32)).astype(BF16)


def iota(shape, axis):
    return lax.broadcasted_iota(jnp.int32, shape, axis)


def cosine_table(flen, rows):
    f = np.arange(rows)[:, None]
    n = np.arange(flen)[None, :]
    scale = np.where((f == 0) | (f == flen // 2), 1.0, 2.0) / flen
    scale = np.where(f <= flen // 2, scale, 0.0)
    return (scale * np.cos(2.0 * math.pi * ((f * n) % flen) / flen)).astype(np.float32)


def sums_kernel(modes, ts_hbm, flag_hbm, v_hbm, g_hbm, msg_ref, ts_ref, keep_ref, v_ref, g_ref, flag_ref, sem):
    dets, samples = ts_ref.shape
    streams = [(v_hbm, v_ref), (g_hbm, g_ref), (flag_hbm, flag_ref), (ts_hbm, ts_ref)]
    copies = [pltpu.make_async_copy(a, b, sem.at[i]) for i, (a, b) in enumerate(streams)]
    for copy in copies:
        copy.start()
    copies[0].wait()
    copies[1].wait()
    vt = v_ref[...]
    g = g_ref[...]
    row = iota((EXT, dets), 0)
    left1 = jnp.concatenate([vt, jnp.where(row < 2, g, 0.0)], axis=0)
    left2 = jnp.concatenate([vt * g, jnp.where((row >= 2) & (row < 4), g * g, 0.0)], axis=0)
    hi1, lo1 = split(left1)
    hi2, lo2 = split(left2)
    left1 = jnp.concatenate([hi1, lo1], axis=0)
    left2 = jnp.concatenate([hi2, lo2], axis=0)
    u = jnp.sum(vt * g, axis=1, keepdims=True)
    square = jnp.sum(g * g, axis=1, keepdims=True)
    lane = iota((modes, samples), 1)
    u = jnp.sum(jnp.where(lane == iota((modes, samples), 0), u, 0.0), axis=0, keepdims=True)
    u = jnp.where(iota((1, samples), 1) == modes, square, u)
    n = modes + EXT
    copies[2].wait()
    keep = (1 - flag_ref[...]).astype(F32)
    keep_ref[...] = keep.astype(BF16)
    both = mm(left2, keep.astype(BF16))
    acc2 = both[:n] + both[n:]
    copies[3].wait()
    x_hi, x_lo = split(ts_ref[...] * keep_ref[...].astype(F32))
    both = mm(left1, x_hi)
    acc1 = both[:n] + both[n:] + mm(hi1, x_lo)
    msg_ref[0:modes] = acc1[0:modes].astype(BF16)
    msg_ref[modes : 2 * modes] = acc2[0:modes].astype(BF16)
    row = iota((MORE, samples), 0)
    ext = acc1[modes : modes + MORE] + acc2[modes : modes + MORE] + jnp.where((row >= 4) & (row < 6), u, 0.0)
    hi = ext.astype(BF16).astype(F32)
    msg_ref[2 * modes :] = jnp.where(row % 2 == 1, ext - hi, hi).astype(BF16)


def prep_kernel(seg, kblk, lane_blocks, digits, tids_hbm, offs_hbm, owner_hbm, cos_hbm, point_hbm, gain_ref, v_ref,
                h2_ref, toep_ref, pn_ref, pt_ref, v3_ref, geo_ref, own_ref,
                tids_ref, offs_ref, owner_ref, cos_ref, point_ref, wide_ref, sem):
    streams = [(cos_hbm, cos_ref), (point_hbm, point_ref), (tids_hbm, tids_ref), (offs_hbm, offs_ref),
               (owner_hbm, owner_ref)]
    copies = [pltpu.make_async_copy(a, b, sem.at[i]) for i, (a, b) in enumerate(streams)]
    for copy in copies:
        copy.start()
    flen = cos_ref.shape[1]
    vt = v_ref[...]
    vhi = vt.astype(BF16).astype(F32)
    pad = jnp.zeros((LANES - 3 * vt.shape[0], vt.shape[1]), F32)
    v3_ref[...] = jnp.concatenate([vhi, vhi, vt - vhi, pad], axis=0).T.astype(BF16)
    copies[0].wait()
    wide_ref[...] = jnp.zeros_like(wide_ref)
    wide_ref[0:1, 0 : gain_ref.shape[1]] = gain_ref[...]
    h = lax.dot_general(wide_ref[...], cos_ref[...], NN, precision=lax.Precision.HIGHEST, preferred_element_type=F32)
    base = jnp.broadcast_to(h[0:1], (LANES, flen))
    base = pltpu.roll(base, 0, 1, stride=1, stride_axis=0)
    base_hi, base_lo = split(base)
    blocks = flen // LANES
    for a in range(blocks):
        for b in range(blocks):
            c = (b - a) % blocks
            to = slice(b * LANES, (b + 1) * LANES)
            h2_ref[a * LANES : (a + 1) * LANES, to] = base_hi[:, c * LANES : (c + 1) * LANES]
            h2_ref[flen + a * LANES : flen + (a + 1) * LANES, to] = base_lo[:, c * LANES : (c + 1) * LANES]
    for c in range(blocks):
        at = slice(c * LANES, (c + 1) * LANES)
        toep_ref[at, 0:LANES] = base_hi[:, at]
        toep_ref[at, LANES : 2 * LANES] = base_lo[:, at]
    for copy in copies[1:]:
        copy.wait()
    listed = seg * kblk
    row16 = iota((listed, LANES), 0)
    first = lax.axis_index("tm") * listed
    squares = jnp.zeros((listed, LANES), F32)
    ext = geo_ref.shape[0] - listed
    row_x = iota((ext, LANES), 0)
    lane_x = iota((ext, LANES), 1)
    ids = jnp.zeros((ext, LANES), F32)
    own = jnp.zeros((listed, LANES), F32)
    for k in range(kblk):
        for s in range(seg):
            j = k * seg + s
            p = point_ref[s, k]
            span, tile = p.shape
            pn_ref[s * span : (s + 1) * span, k * tile : (k + 1) * tile] = p
            pt_ref[k * tile : (k + 1) * tile, s * span : (s + 1) * span] = p.T
            p = p.astype(F32)
            squares = jnp.where(row16 == j, jnp.sum(p * p, axis=0, keepdims=True), squares)
            target = owner_ref[tids_ref[s, k]] * LANES + offs_ref[s, k]
            own = jnp.where(row16 == j, target.astype(F32), own)
            place = first + j
            digit = target
            for d in range(digits):
                at = (row_x == d * lane_blocks + place // LANES) & (lane_x == place % LANES)
                ids = jnp.where(at, (digit % BASE).astype(F32), ids)
                digit = digit // BASE
    geo_ref[0:listed] = squares.astype(BF16)
    geo_ref[listed:] = ids.astype(BF16)
    own_ref[...] = own


def filtered(b, toep_ref):
    flen = b.shape[1]
    blocks = flen // LANES
    rows = -(-2 * blocks // EXT) * EXT
    hi, lo = split(b)
    hi, lo = hi.astype(F32), lo.astype(F32)
    row = iota((rows, LANES), 0)
    left = []
    for c in range(blocks):
        block = jnp.zeros((rows, LANES), F32)
        for m in range(blocks):
            at = slice(m * LANES, (m + 1) * LANES)
            a = (m + c) % blocks
            block = jnp.where(row == a, hi[:, at], jnp.where(row == blocks + a, lo[:, at], block))
        left.append(block.astype(BF16))
    z = mm(jnp.concatenate(left, axis=1), toep_ref[...])
    z = z[:, 0:LANES] + z[:, LANES:]
    return z[0:blocks] + z[blocks : 2 * blocks]


def project(z, pn_ref, seg, kblk):
    listed = seg * kblk
    hi, lo = split(z)
    hi, lo = hi.astype(F32), lo.astype(F32)
    row = iota((2 * listed, LANES), 0)
    left = []
    for s in range(seg):
        value = jnp.where(row < listed, hi[s : s + 1], lo[s : s + 1])
        left.append(jnp.where(row % seg == s, value, 0.0).astype(BF16))
    out = mm(jnp.concatenate(left, axis=1), pn_ref[...])
    out = out[:listed] + out[listed:]
    row = iota((listed, LANES), 0)
    proj = out[:, 0:LANES]
    for k in range(1, kblk):
        proj = jnp.where(row // seg == k, out[:, k * LANES : (k + 1) * LANES], proj)
    return proj


def first_kernel(modes, seg, kblk, m0, m1, m2, m3, toep_ref, pn_ref, geo_ref,
                 bq_ref, vec_ref, send_ref):
    tot = m0[...].astype(F32) + m1[...].astype(F32) + m2[...].astype(F32) + m3[...].astype(F32)
    bq_ref[...] = tot[0 : 2 * modes]
    ext = tot[2 * modes :]
    u_row = ext[4:5, 0:LANES] + ext[5:6, 0:LANES]
    u_col = jnp.sum(jnp.where(iota((modes, LANES), 0) == iota((modes, LANES), 1), u_row, 0.0), axis=1, keepdims=True)
    square = jnp.sum(jnp.where(iota((1, LANES), 1) == modes, u_row, 0.0), axis=1, keepdims=True)
    b1 = ext[0:1] + ext[1:2] - jnp.sum(u_col * tot[0:modes], axis=0, keepdims=True)
    b2 = ext[2:3] + ext[3:4] - jnp.sum(u_col * tot[modes : 2 * modes], axis=0, keepdims=True)
    row = iota((8, b1.shape[1]), 0)
    vec_ref[...] = jnp.where(row == 0, b1, jnp.where(row == 1, b2, jnp.where(row == 2, square, 0.0)))
    z = filtered(b1, toep_ref)
    proj = project(z, pn_ref, seg, kblk).astype(BF16)
    geo = geo_ref[...]
    listed = seg * kblk
    for t in range(send_ref.shape[0]):
        send_ref[t, 0:listed] = proj
        send_ref[t, listed:] = geo


def lane_ids(all_ref, listed, blocks, digits, b):
    ids = jnp.sum(all_ref[:, 2 * listed :].astype(F32), axis=0)
    out = ids[b : b + 1]
    for d in range(1, digits):
        out = out + float(BASE**d) * ids[d * blocks + b : d * blocks + b + 1]
    return out


def second_kernel(seg, kblk, digits, all_ref, own_ref, vec_ref, toep_ref, pn_ref, pt_ref, sig_ref, send_ref):
    listed = seg * kblk
    blocks = all_ref.shape[0] * listed // LANES
    samples = vec_ref.shape[1]
    per = LANES // listed
    own = own_ref[...]
    psum = jnp.zeros((listed, LANES), F32)
    wsum = jnp.zeros((listed, LANES), F32)
    for b in range(blocks):
        same = (own == lane_ids(all_ref, listed, blocks, digits, b)).astype(F32).astype(BF16)
        part = all_ref[b * per : (b + 1) * per]
        psum = psum + mm(same, part[:, 0:listed].reshape(LANES, LANES))
        wsum = wsum + mm(same, part[:, listed : 2 * listed].reshape(LANES, LANES))
    square = vec_ref[2:3, 0:LANES]
    fetched = (psum / (1.0 + square * wsum)).astype(BF16)
    row = iota((listed, LANES), 0)
    wide = [jnp.where(row // seg == k, fetched.astype(F32), 0.0).astype(BF16) for k in range(kblk)]
    spread = mm(jnp.concatenate(wide, axis=1), pt_ref[...])
    row = iota((listed, samples), 0)
    lane = iota((listed, samples), 1)
    sig = jnp.sum(jnp.where(lane // (samples // seg) == row % seg, spread, 0.0), axis=0, keepdims=True)
    sig_ref[...] = jnp.broadcast_to(sig, sig_ref.shape)
    z = filtered(vec_ref[0:1] - vec_ref[1:2] * sig, toep_ref)
    proj = project(z, pn_ref, seg, kblk).astype(BF16)
    for t in range(send_ref.shape[0]):
        send_ref[t] = proj


def clean_kernel(seg, kblk, digits, modes, parts, ts_ref, keep_ref, g_ref, v3_ref, bq_ref, sig_ref, h2_ref,
                 all_ref, vec_ref, out_hbm, base_ref, scale_ref, same_ref, out_ref, sem):
    dets, samples = ts_ref.shape
    chunk = dets // parts
    sig = sig_ref[0:1]
    q_hi, q_lo = split(bq_ref[0:modes] - bq_ref[modes : 2 * modes] * sig)
    pad = jnp.zeros((LANES - 3 * modes, samples), BF16)
    q3 = jnp.concatenate([q_hi, q_lo, q_hi, pad], axis=0)
    eye = iota((chunk, chunk), 0) == iota((chunk, chunk), 1)
    copies = []
    for i in range(parts):
        at = slice(i * chunk, (i + 1) * chunk)
        g_col = jnp.sum(jnp.where(eye, g_ref[:, at], 0.0), axis=1, keepdims=True)
        rest = (ts_ref[at] - g_col * sig) * keep_ref[at].astype(F32) - mm(v3_ref[at], q3)
        rest = rest.astype(BF16)
        out_ref[at] = (mm(rest, h2_ref[0:samples]) + mm(rest, h2_ref[samples:])).astype(BF16)
        rows = pl.ds(i * chunk, chunk)
        copy = pltpu.make_async_copy(out_ref.at[rows], out_hbm.at[rows], sem.at[i])
        copy.start()
        copies.append(copy)
    listed = seg * kblk
    blocks = all_ref.shape[0] * listed // LANES
    per = LANES // listed
    psum = jnp.zeros((LANES, LANES), F32)
    wsum = jnp.zeros((LANES, LANES), F32)
    first = (lax.axis_index("det") * lax.axis_size("tm") + lax.axis_index("tm")) * LANES
    mine = (iota((LANES, LANES), 0) + first).astype(F32)
    for b in range(blocks):
        same = (mine == lane_ids(all_ref, listed, blocks, digits, b)).astype(F32).astype(BF16)
        same_ref[b] = same
        part = all_ref[b * per : (b + 1) * per]
        psum = psum + mm(same, part[:, 0:listed].reshape(LANES, LANES))
        wsum = wsum + mm(same, part[:, listed : 2 * listed].reshape(LANES, LANES))
    wsum = 1.0 + vec_ref[2:3, 0:LANES] * wsum
    scale = jnp.sqrt(wsum) / wsum
    scale_ref[...] = scale
    base_ref[...] = psum * scale
    for copy in copies:
        copy.wait()


def tile_kernel(all2_ref, base_ref, scale_ref, same_ref, out_ref):
    per = LANES // all2_ref.shape[1]
    psum = jnp.zeros((LANES, LANES), F32)
    for b in range(same_ref.shape[0]):
        psum = psum + mm(same_ref[b], all2_ref[b * per : (b + 1) * per].reshape(LANES, LANES))
    out_ref[0] = base_ref[...] + psum * scale_ref[...]


VM = pl.BlockSpec(memory_space=pltpu.VMEM)
HB = pl.BlockSpec(memory_space=pltpu.HBM)
SM = pl.BlockSpec(memory_space=pltpu.SMEM)
GRANT = pltpu.CompilerParams(vmem_limit_bytes=12 * 2**20)


def shape(dims, dtype=F32):
    return jax.ShapeDtypeStruct(dims, dtype)


def others(x, axis, n):
    if n & (n - 1) == 0:
        pairs = [[(i, i ^ k) for i in range(n)] for k in range(1, n)]
    else:
        pairs = [[(i, (i + k) % n) for i in range(n)] for k in range(1, n)]
    return [lax.ppermute(x, axis, p) for p in pairs]


def shards(n_det, n_tm, timestream, sample_flags, pointing, tile_ids, block_offsets, tile_owner, det_gains,
           mode_vectors, filter_gain):
    dets, samples = timestream.shape
    modes = mode_vectors.shape[1]
    seg, kblk = tile_ids.shape
    listed = seg * kblk
    parts = 2
    lane_blocks = n_tm * listed // LANES
    digits = -(-int(tile_owner.shape[0] * LANES - 1).bit_length() // 7)
    id_rows = -(-digits * lane_blocks // 8) * 8
    inputs = (timestream, sample_flags, mode_vectors.T, det_gains.reshape(1, dets))
    msg, ts, keep, vt, g = pl.pallas_call(
        functools.partial(sums_kernel, modes),
        in_specs=[HB] * 4,
        out_specs=[VM] * 5,
        out_shape=[
            shape((2 * modes + MORE, samples), BF16),
            shape((dets, samples)),
            shape((dets, samples), BF16),
            shape((modes, dets)),
            shape((1, dets)),
        ],
        scratch_shapes=[
            pltpu.VMEM((dets, samples), jnp.int32),
            pltpu.SemaphoreType.DMA((4,)),
        ],
        compiler_params=GRANT,
        name="sums",
    )(*(pltpu.with_memory_space_constraint(x, pltpu.HBM) for x in inputs))
    parts_of_all = [msg] + others(msg, "det", n_det)

    rows = -(-filter_gain.shape[0] // LANES) * LANES
    inputs = (tile_ids, block_offsets, tile_owner, jnp.asarray(cosine_table(samples, rows)), pointing)
    h2, toep, pn, pt, v3, geo, own = pl.pallas_call(
        functools.partial(prep_kernel, seg, kblk, lane_blocks, digits),
        in_specs=[HB] * 5 + [VM] * 2,
        out_specs=[VM] * 7,
        out_shape=[
            shape((2 * samples, samples), BF16),
            shape((samples, 2 * LANES), BF16),
            shape((samples, kblk * LANES), BF16),
            shape((kblk * LANES, samples), BF16),
            shape((dets, LANES), BF16),
            shape((listed + id_rows, LANES), BF16),
            shape((listed, LANES)),
        ],
        scratch_shapes=[
            pltpu.SMEM(tile_ids.shape, jnp.int32),
            pltpu.SMEM(block_offsets.shape, jnp.int32),
            pltpu.SMEM(tile_owner.shape, jnp.int32),
            pltpu.VMEM((rows, samples), F32),
            pltpu.VMEM(pointing.shape, BF16),
            pltpu.VMEM((8, rows), F32),
            pltpu.SemaphoreType.DMA((5,)),
        ],
        cost_estimate=pl.CostEstimate(flops=10**8, bytes_accessed=3 * 10**6, transcendentals=0),
        compiler_params=GRANT,
        name="prep",
    )(*(pltpu.with_memory_space_constraint(x, pltpu.HBM) for x in inputs), filter_gain.reshape(1, -1), vt)

    bq, vec, send = pl.pallas_call(
        functools.partial(first_kernel, modes, seg, kblk),
        in_specs=[VM] * 7,
        out_specs=[VM] * 3,
        out_shape=[
            shape((2 * modes, samples)),
            shape((8, samples)),
            shape((n_tm, 2 * listed + id_rows, LANES), BF16),
        ],
        compiler_params=GRANT,
        name="first",
    )(*parts_of_all, toep, pn, geo)
    everyone = lax.all_to_all(send, "tm", 0, 0)

    sig, send = pl.pallas_call(
        functools.partial(second_kernel, seg, kblk, digits),
        in_specs=[VM] * 6,
        out_specs=[VM] * 2,
        out_shape=[shape((8, samples)), shape((n_tm, listed, LANES), BF16)],
        compiler_params=GRANT,
        name="second",
    )(everyone, own, vec, toep, pn, pt)
    everyone2 = lax.all_to_all(send, "tm", 0, 0)

    cleaned, base, scale, same = pl.pallas_call(
        functools.partial(clean_kernel, seg, kblk, digits, modes, parts),
        in_specs=[VM] * 9,
        out_specs=[HB, VM, VM, VM],
        out_shape=[
            shape((dets, samples), BF16),
            shape((LANES, LANES)),
            shape((LANES, LANES)),
            shape((lane_blocks, LANES, LANES), BF16),
        ],
        scratch_shapes=[pltpu.VMEM((dets, samples), BF16), pltpu.SemaphoreType.DMA((parts,))],
        cost_estimate=pl.CostEstimate(flops=10**9, bytes_accessed=4 * 10**6, transcendentals=0),
        compiler_params=GRANT,
        name="clean",
    )(ts, keep, g, v3, bq, sig, h2, everyone, vec)

    tile = pl.pallas_call(
        tile_kernel,
        in_specs=[VM] * 4,
        out_specs=VM,
        out_shape=shape((1, LANES, LANES)),
        compiler_params=GRANT,
        name="tile",
    )(everyone2, base, scale, same)
    return tile, cleaned


def solution(mesh):
    return jax.shard_map(
        functools.partial(shards, mesh.shape["det"], mesh.shape["tm"]),
        mesh=mesh,
        in_specs=(
            P("det", "tm"),
            P("det", "tm"),
            P("tm", None, None, None),
            P("tm", None),
            P("tm", None),
            P(),
            P("det"),
            P("det", None),
            P(),
        ),
        out_specs=(P(("det", "tm"), None, None), P("det", "tm")),
        check_vma=False,
    )
```

```python
import functools
import math

import jax
import jax.numpy as jnp
import numpy as np
from jax import lax
from jax.experimental import pallas as pl
from jax.experimental.pallas import tpu as pltpu
from jax.sharding import PartitionSpec as P

F32 = jnp.float32
BF16 = jnp.bfloat16
LANES = 128
BASE = 128
EXT = 16
EARLY = 2
MORE = 8
NN = (((1,), (0,)), ((), ()))
NT = (((1,), (1,)), ((), ()))


def mm(a, b, dims=NN):
    return lax.dot_general(a, b, dims, preferred_element_type=F32)


def split(x):
    hi = x.astype(BF16)
    return hi, (x - hi.astype(F32)).astype(BF16)


def iota(shape, axis):
    return lax.broadcasted_iota(jnp.int32, shape, axis)


def cosine_table(flen, rows):
    f = np.arange(rows)[:, None]
    n = np.arange(flen)[None, :]
    scale = np.where((f == 0) | (f == flen // 2), 1.0, 2.0) / flen
    scale = np.where(f <= flen // 2, scale, 0.0)
    return (scale * np.cos(2.0 * math.pi * ((f * n) % flen) / flen)).astype(np.float32)


def sums_kernel(modes, ts_hbm, flag_hbm, v_hbm, g_hbm, msg_ref, ts_ref, keep_ref, v_ref, g_ref, flag_ref, sem):
    dets, samples = ts_ref.shape
    streams = [(v_hbm, v_ref), (g_hbm, g_ref), (flag_hbm, flag_ref), (ts_hbm, ts_ref)]
    copies = [pltpu.make_async_copy(a, b, sem.at[i]) for i, (a, b) in enumerate(streams)]
    for copy in copies:
        copy.start()
    copies[0].wait()
    copies[1].wait()
    vt = v_ref[...]
    g = g_ref[...]
    row = iota((EXT, dets), 0)
    left1 = jnp.concatenate([vt, jnp.where(row < 2, g, 0.0)], axis=0)
    left2 = jnp.concatenate([vt * g, jnp.where((row >= 2) & (row < 4), g * g, 0.0)], axis=0)
    hi1, lo1 = split(left1)
    hi2, lo2 = split(left2)
    left1 = jnp.concatenate([hi1, lo1], axis=0)
    left2 = jnp.concatenate([hi2, lo2], axis=0)
    u = jnp.sum(vt * g, axis=1, keepdims=True)
    square = jnp.sum(g * g, axis=1, keepdims=True)
    lane = iota((modes, samples), 1)
    u = jnp.sum(jnp.where(lane == iota((modes, samples), 0), u, 0.0), axis=0, keepdims=True)
    u = jnp.where(iota((1, samples), 1) == modes, square, u)
    n = modes + EXT
    copies[2].wait()
    keep = (1 - flag_ref[...]).astype(F32)
    keep_ref[...] = keep.astype(BF16)
    both = mm(left2, keep.astype(BF16))
    acc2 = both[:n] + both[n:]
    copies[3].wait()
    x_hi, x_lo = split(ts_ref[...] * keep_ref[...].astype(F32))
    both = mm(left1, x_hi)
    acc1 = both[:n] + both[n:] + mm(hi1, x_lo)
    msg_ref[0:modes] = acc1[0:modes].astype(BF16)
    msg_ref[modes : 2 * modes] = acc2[0:modes].astype(BF16)
    row = iota((MORE, samples), 0)
    ext = acc1[modes : modes + MORE] + acc2[modes : modes + MORE] + jnp.where((row >= 4) & (row < 6), u, 0.0)
    hi = ext.astype(BF16).astype(F32)
    msg_ref[2 * modes :] = jnp.where(row % 2 == 1, ext - hi, hi).astype(BF16)


def prep_kernel(seg, kblk, lane_blocks, digits, tids_hbm, offs_hbm, owner_hbm, cos_hbm, point_hbm, gain_ref, v_ref,
                h2_ref, toep_ref, pn_ref, pt_ref, v3_ref, geo_ref, own_ref,
                tids_ref, offs_ref, owner_ref, cos_ref, point_ref, wide_ref, sem):
    streams = [(cos_hbm, cos_ref), (point_hbm, point_ref), (tids_hbm, tids_ref), (offs_hbm, offs_ref),
               (owner_hbm, owner_ref)]
    copies = [pltpu.make_async_copy(a, b, sem.at[i]) for i, (a, b) in enumerate(streams)]
    for copy in copies:
        copy.start()
    flen = cos_ref.shape[1]
    vt = v_ref[...]
    vhi = vt.astype(BF16).astype(F32)
    pad = jnp.zeros((LANES - 3 * vt.shape[0], vt.shape[1]), F32)
    v3_ref[...] = jnp.concatenate([vhi, vhi, vt - vhi, pad], axis=0).T.astype(BF16)
    copies[0].wait()
    wide_ref[...] = jnp.zeros_like(wide_ref)
    wide_ref[0:1, 0 : gain_ref.shape[1]] = gain_ref[...]
    h = lax.dot_general(wide_ref[...], cos_ref[...], NN, precision=lax.Precision.HIGHEST, preferred_element_type=F32)
    base = jnp.broadcast_to(h[0:1], (LANES, flen))
    base = pltpu.roll(base, 0, 1, stride=1, stride_axis=0)
    base_hi, base_lo = split(base)
    blocks = flen // LANES
    for a in range(blocks):
        for b in range(blocks):
            c = (b - a) % blocks
            to = slice(b * LANES, (b + 1) * LANES)
            h2_ref[a * LANES : (a + 1) * LANES, to] = base_hi[:, c * LANES : (c + 1) * LANES]
            h2_ref[flen + a * LANES : flen + (a + 1) * LANES, to] = base_lo[:, c * LANES : (c + 1) * LANES]
    for c in range(blocks):
        at = slice(c * LANES, (c + 1) * LANES)
        toep_ref[at, 0:LANES] = base_hi[:, at]
        toep_ref[at, LANES : 2 * LANES] = base_lo[:, at]
    for copy in copies[1:]:
        copy.wait()
    listed = seg * kblk
    row16 = iota((listed, LANES), 0)
    first = lax.axis_index("tm") * listed
    squares = jnp.zeros((listed, LANES), F32)
    ext = geo_ref.shape[0] - listed
    row_x = iota((ext, LANES), 0)
    lane_x = iota((ext, LANES), 1)
    ids = jnp.zeros((ext, LANES), F32)
    own = jnp.zeros((listed, LANES), F32)
    for k in range(kblk):
        for s in range(seg):
            j = k * seg + s
            p = point_ref[s, k]
            span, tile = p.shape
            pn_ref[s * span : (s + 1) * span, k * tile : (k + 1) * tile] = p
            pt_ref[k * tile : (k + 1) * tile, s * span : (s + 1) * span] = p.T
            p = p.astype(F32)
            squares = jnp.where(row16 == j, jnp.sum(p * p, axis=0, keepdims=True), squares)
            target = owner_ref[tids_ref[s, k]] * LANES + offs_ref[s, k]
            own = jnp.where(row16 == j, target.astype(F32), own)
            place = first + j
            digit = target
            for d in range(digits):
                at = (row_x == d * lane_blocks + place // LANES) & (lane_x == place % LANES)
                ids = jnp.where(at, (digit % BASE).astype(F32), ids)
                digit = digit // BASE
    geo_ref[0:listed] = squares.astype(BF16)
    geo_ref[listed:] = ids.astype(BF16)
    own_ref[...] = own


def filtered(b, toep_ref):
    flen = b.shape[1]
    blocks = flen // LANES
    rows = -(-2 * blocks // EXT) * EXT
    hi, lo = split(b)
    hi, lo = hi.astype(F32), lo.astype(F32)
    row = iota((rows, LANES), 0)
    left = []
    for c in range(blocks):
        block = jnp.zeros((rows, LANES), F32)
        for m in range(blocks):
            at = slice(m * LANES, (m + 1) * LANES)
            a = (m + c) % blocks
            block = jnp.where(row == a, hi[:, at], jnp.where(row == blocks + a, lo[:, at], block))
        left.append(block.astype(BF16))
    z = mm(jnp.concatenate(left, axis=1), toep_ref[...])
    z = z[:, 0:LANES] + z[:, LANES:]
    return z[0:blocks] + z[blocks : 2 * blocks]


def project(z, pn_ref, seg, kblk):
    listed = seg * kblk
    hi, lo = split(z)
    hi, lo = hi.astype(F32), lo.astype(F32)
    row = iota((2 * listed, LANES), 0)
    left = []
    for s in range(seg):
        value = jnp.where(row < listed, hi[s : s + 1], lo[s : s + 1])
        left.append(jnp.where(row % seg == s, value, 0.0).astype(BF16))
    out = mm(jnp.concatenate(left, axis=1), pn_ref[...])
    out = out[:listed] + out[listed:]
    row = iota((listed, LANES), 0)
    proj = out[:, 0:LANES]
    for k in range(1, kblk):
        proj = jnp.where(row // seg == k, out[:, k * LANES : (k + 1) * LANES], proj)
    return proj


def first_kernel(modes, seg, kblk, m0, m1, m2, m3, toep_ref, pn_ref, geo_ref,
                 bq_ref, vec_ref, send_ref):
    tot = m0[...].astype(F32) + m1[...].astype(F32) + m2[...].astype(F32) + m3[...].astype(F32)
    bq_ref[...] = tot[0 : 2 * modes]
    ext = tot[2 * modes :]
    u_row = ext[4:5, 0:LANES] + ext[5:6, 0:LANES]
    u_col = jnp.sum(jnp.where(iota((modes, LANES), 0) == iota((modes, LANES), 1), u_row, 0.0), axis=1, keepdims=True)
    square = jnp.sum(jnp.where(iota((1, LANES), 1) == modes, u_row, 0.0), axis=1, keepdims=True)
    b1 = ext[0:1] + ext[1:2] - jnp.sum(u_col * tot[0:modes], axis=0, keepdims=True)
    b2 = ext[2:3] + ext[3:4] - jnp.sum(u_col * tot[modes : 2 * modes], axis=0, keepdims=True)
    row = iota((8, b1.shape[1]), 0)
    vec_ref[...] = jnp.where(row == 0, b1, jnp.where(row == 1, b2, jnp.where(row == 2, square, 0.0)))
    z = filtered(b1, toep_ref)
    proj = project(z, pn_ref, seg, kblk).astype(BF16)
    geo = geo_ref[...]
    listed = seg * kblk
    for t in range(send_ref.shape[0]):
        send_ref[t, 0:listed] = proj
        send_ref[t, listed:] = geo


def lane_ids(all_ref, listed, blocks, digits, b):
    ids = jnp.sum(all_ref[:, 2 * listed :].astype(F32), axis=0)
    out = ids[b : b + 1]
    for d in range(1, digits):
        out = out + float(BASE**d) * ids[d * blocks + b : d * blocks + b + 1]
    return out


def second_kernel(seg, kblk, digits, all_ref, own_ref, vec_ref, toep_ref, pn_ref, pt_ref, sig_ref, send_ref):
    listed = seg * kblk
    blocks = all_ref.shape[0] * listed // LANES
    samples = vec_ref.shape[1]
    per = LANES // listed
    own = own_ref[...]
    psum = jnp.zeros((listed, LANES), F32)
    wsum = jnp.zeros((listed, LANES), F32)
    for b in range(blocks):
        same = (own == lane_ids(all_ref, listed, blocks, digits, b)).astype(F32).astype(BF16)
        part = all_ref[b * per : (b + 1) * per]
        psum = psum + mm(same, part[:, 0:listed].reshape(LANES, LANES))
        wsum = wsum + mm(same, part[:, listed : 2 * listed].reshape(LANES, LANES))
    square = vec_ref[2:3, 0:LANES]
    fetched = (psum / (1.0 + square * wsum)).astype(BF16)
    row = iota((listed, LANES), 0)
    wide = [jnp.where(row // seg == k, fetched.astype(F32), 0.0).astype(BF16) for k in range(kblk)]
    spread = mm(jnp.concatenate(wide, axis=1), pt_ref[...])
    row = iota((listed, samples), 0)
    lane = iota((listed, samples), 1)
    sig = jnp.sum(jnp.where(lane // (samples // seg) == row % seg, spread, 0.0), axis=0, keepdims=True)
    sig_ref[...] = jnp.broadcast_to(sig, sig_ref.shape)
    z = filtered(vec_ref[0:1] - vec_ref[1:2] * sig, toep_ref)
    proj = project(z, pn_ref, seg, kblk).astype(BF16)
    for t in range(send_ref.shape[0]):
        send_ref[t] = proj


def clean_rows(modes, at, ts_ref, keep_ref, g_ref, v3_ref, bq_ref, sig_ref, h2_ref):
    samples = ts_ref.shape[1]
    sig = sig_ref[0:1]
    q_hi, q_lo = split(bq_ref[0:modes] - bq_ref[modes : 2 * modes] * sig)
    pad = jnp.zeros((LANES - 3 * modes, samples), BF16)
    q3 = jnp.concatenate([q_hi, q_lo, q_hi, pad], axis=0)
    eye = iota((at.stop - at.start,) * 2, 0) == iota((at.stop - at.start,) * 2, 1)
    g_col = jnp.sum(jnp.where(eye, g_ref[:, at], 0.0), axis=1, keepdims=True)
    rest = (ts_ref[at] - g_col * sig) * keep_ref[at].astype(F32) - mm(v3_ref[at], q3)
    rest = rest.astype(BF16)
    return (mm(rest, h2_ref[0:samples]) + mm(rest, h2_ref[samples:])).astype(BF16)


def tile_parts(seg, kblk, digits, all_ref, vec_ref, base_ref, scale_ref, same_ref):
    listed = seg * kblk
    blocks = all_ref.shape[0] * listed // LANES
    per = LANES // listed
    psum = jnp.zeros((LANES, LANES), F32)
    wsum = jnp.zeros((LANES, LANES), F32)
    first = (lax.axis_index("det") * lax.axis_size("tm") + lax.axis_index("tm")) * LANES
    mine = (iota((LANES, LANES), 0) + first).astype(F32)
    for b in range(blocks):
        same = (mine == lane_ids(all_ref, listed, blocks, digits, b)).astype(F32).astype(BF16)
        same_ref[b] = same
        part = all_ref[b * per : (b + 1) * per]
        psum = psum + mm(same, part[:, 0:listed].reshape(LANES, LANES))
        wsum = wsum + mm(same, part[:, listed : 2 * listed].reshape(LANES, LANES))
    wsum = 1.0 + vec_ref[2:3, 0:LANES] * wsum
    scale = jnp.sqrt(wsum) / wsum
    scale_ref[...] = scale
    base_ref[...] = psum * scale


def early_kernel(seg, kblk, digits, modes, ts_ref, keep_ref, g_ref, v3_ref, bq_ref, sig_ref, h2_ref, all_ref, vec_ref,
                 early_ref, base_ref, scale_ref, same_ref):
    rows = slice(0, early_ref.shape[0])
    early_ref[...] = clean_rows(modes, rows, ts_ref, keep_ref, g_ref, v3_ref, bq_ref, sig_ref, h2_ref)
    tile_parts(seg, kblk, digits, all_ref, vec_ref, base_ref, scale_ref, same_ref)


def late_kernel(modes, ts_ref, keep_ref, g_ref, v3_ref, bq_ref, sig_ref, h2_ref, early_ref, after_ref, out_hbm,
                late_ref, sem):
    cut = early_ref.shape[0]
    first = pltpu.make_async_copy(early_ref, out_hbm.at[pl.ds(0, cut)], sem.at[0])
    first.start()
    rows = slice(cut, ts_ref.shape[0])
    late_ref[...] = clean_rows(modes, rows, ts_ref, keep_ref, g_ref, v3_ref, bq_ref, sig_ref, h2_ref)
    second = pltpu.make_async_copy(late_ref, out_hbm.at[pl.ds(cut, late_ref.shape[0])], sem.at[1])
    second.start()
    first.wait()
    second.wait()


def tile_kernel(all2_ref, base_ref, scale_ref, same_ref, out_ref):
    per = LANES // all2_ref.shape[1]
    psum = jnp.zeros((LANES, LANES), F32)
    for b in range(same_ref.shape[0]):
        psum = psum + mm(same_ref[b], all2_ref[b * per : (b + 1) * per].reshape(LANES, LANES))
    out_ref[0] = base_ref[...] + psum * scale_ref[...]


def pair_tile_kernel(send_ref, near_ref, far_ref, mate_ref, base_ref, scale_ref, same_ref, out_ref, all_ref):
    t = lax.axis_index("tm")
    core = t % 2
    far, other = 6 - 2 * core, 4 + 2 * core
    mate = jnp.bitwise_xor(t, 1)
    arrived = [
        (send_ref, t),
        (near_ref, jnp.bitwise_xor(t, 2)),
        (far_ref, jnp.bitwise_xor(t, far)),
        (mate_ref, jnp.bitwise_xor(mate, other)),
    ]
    for ref, at in arrived:
        all_ref[at] = ref[0]
        all_ref[jnp.bitwise_xor(at, 1)] = ref[1]
    blocks, per = same_ref.shape[0], LANES // all_ref.shape[1]
    psum = jnp.zeros((LANES, LANES), F32)
    for b in range(blocks):
        psum = psum + mm(same_ref[b], all_ref[b * per : (b + 1) * per].reshape(LANES, LANES))
    out_ref[0] = base_ref[...] + psum * scale_ref[...]


VM = pl.BlockSpec(memory_space=pltpu.VMEM)
HB = pl.BlockSpec(memory_space=pltpu.HBM)
SM = pl.BlockSpec(memory_space=pltpu.SMEM)
GRANT = pltpu.CompilerParams(vmem_limit_bytes=12 * 2**20)


def shape(dims, dtype=F32):
    return jax.ShapeDtypeStruct(dims, dtype)


def others(x, axis, n):
    if n & (n - 1) == 0:
        pairs = [[(i, i ^ k) for i in range(n)] for k in range(1, n)]
    else:
        pairs = [[(i, (i + k) % n) for i in range(n)] for k in range(1, n)]
    return [lax.ppermute(x, axis, p) for p in pairs]


def shards(n_det, n_tm, timestream, sample_flags, pointing, tile_ids, block_offsets, tile_owner, det_gains,
           mode_vectors, filter_gain):
    dets, samples = timestream.shape
    modes = mode_vectors.shape[1]
    seg, kblk = tile_ids.shape
    listed = seg * kblk
    lane_blocks = n_tm * listed // LANES
    digits = -(-int(tile_owner.shape[0] * LANES - 1).bit_length() // 7)
    id_rows = -(-digits * lane_blocks // 8) * 8
    inputs = (timestream, sample_flags, mode_vectors.T, det_gains.reshape(1, dets))
    msg, ts, keep, vt, g = pl.pallas_call(
        functools.partial(sums_kernel, modes),
        in_specs=[HB] * 4,
        out_specs=[VM] * 5,
        out_shape=[
            shape((2 * modes + MORE, samples), BF16),
            shape((dets, samples)),
            shape((dets, samples), BF16),
            shape((modes, dets)),
            shape((1, dets)),
        ],
        scratch_shapes=[
            pltpu.VMEM((dets, samples), jnp.int32),
            pltpu.SemaphoreType.DMA((4,)),
        ],
        compiler_params=GRANT,
        name="sums",
    )(*(pltpu.with_memory_space_constraint(x, pltpu.HBM) for x in inputs))
    parts_of_all = [msg] + others(msg, "det", n_det)

    rows = -(-filter_gain.shape[0] // LANES) * LANES
    inputs = (tile_ids, block_offsets, tile_owner, jnp.asarray(cosine_table(samples, rows)), pointing)
    h2, toep, pn, pt, v3, geo, own = pl.pallas_call(
        functools.partial(prep_kernel, seg, kblk, lane_blocks, digits),
        in_specs=[HB] * 5 + [VM] * 2,
        out_specs=[VM] * 7,
        out_shape=[
            shape((2 * samples, samples), BF16),
            shape((samples, 2 * LANES), BF16),
            shape((samples, kblk * LANES), BF16),
            shape((kblk * LANES, samples), BF16),
            shape((dets, LANES), BF16),
            shape((listed + id_rows, LANES), BF16),
            shape((listed, LANES)),
        ],
        scratch_shapes=[
            pltpu.SMEM(tile_ids.shape, jnp.int32),
            pltpu.SMEM(block_offsets.shape, jnp.int32),
            pltpu.SMEM(tile_owner.shape, jnp.int32),
            pltpu.VMEM((rows, samples), F32),
            pltpu.VMEM(pointing.shape, BF16),
            pltpu.VMEM((8, rows), F32),
            pltpu.SemaphoreType.DMA((5,)),
        ],
        cost_estimate=pl.CostEstimate(flops=10**8, bytes_accessed=3 * 10**6, transcendentals=0),
        compiler_params=GRANT,
        name="prep",
    )(*(pltpu.with_memory_space_constraint(x, pltpu.HBM) for x in inputs), filter_gain.reshape(1, -1), vt)

    bq, vec, send = pl.pallas_call(
        functools.partial(first_kernel, modes, seg, kblk),
        in_specs=[VM] * 7,
        out_specs=[VM] * 3,
        out_shape=[
            shape((2 * modes, samples)),
            shape((8, samples)),
            shape((n_tm, 2 * listed + id_rows, LANES), BF16),
        ],
        compiler_params=GRANT,
        name="first",
    )(*parts_of_all, toep, pn, geo)
    everyone = lax.all_to_all(send, "tm", 0, 0)

    paired = n_tm == 8
    sig, send = pl.pallas_call(
        functools.partial(second_kernel, seg, kblk, digits),
        in_specs=[VM] * 6,
        out_specs=[VM] * 2,
        out_shape=[shape((8, samples)), shape((1 if paired else n_tm, listed, LANES), BF16)],
        compiler_params=GRANT,
        name="second",
    )(everyone, own, vec, toep, pn, pt)
    mates = [(i, i ^ 1) for i in range(n_tm)]
    if paired:
        mate = lax.ppermute(send, "tm", mates)

    cut = EARLY * dets // 4
    operands = (ts, keep, g, v3, bq, sig, h2)
    early, base, scale, same = pl.pallas_call(
        functools.partial(early_kernel, seg, kblk, digits, modes),
        in_specs=[VM] * 9,
        out_specs=[VM] * 4,
        out_shape=[
            shape((cut, samples), BF16),
            shape((LANES, LANES)),
            shape((LANES, LANES)),
            shape((lane_blocks, LANES, LANES), BF16),
        ],
        cost_estimate=pl.CostEstimate(flops=5 * 10**8, bytes_accessed=2 * 10**6, transcendentals=0),
        compiler_params=GRANT,
        name="early",
    )(*operands, everyone, vec)
    if paired:
        mate, early, base = lax.optimization_barrier((mate, early, base))
        both = jnp.concatenate([send, mate], axis=0)
        near = lax.ppermute(both, "tm", [(i, i ^ 2) for i in range(n_tm)])
        after = lax.ppermute(both, "tm", [(i, i ^ (6 - 2 * (i % 2))) for i in range(n_tm)])
        arrived = (both, near, after, lax.ppermute(after, "tm", mates))
        last, scratch = pair_tile_kernel, [pltpu.VMEM((n_tm, listed, LANES), BF16)]
    else:
        arrived = (lax.all_to_all(send, "tm", 0, 0),)
        after, last, scratch = vec, tile_kernel, []
    cleaned = pl.pallas_call(
        functools.partial(late_kernel, modes),
        in_specs=[VM] * 9,
        out_specs=HB,
        out_shape=shape((dets, samples), BF16),
        scratch_shapes=[pltpu.VMEM((dets - cut, samples), BF16), pltpu.SemaphoreType.DMA((2,))],
        cost_estimate=pl.CostEstimate(flops=5 * 10**8, bytes_accessed=2 * 10**6, transcendentals=0),
        compiler_params=GRANT,
        name="late",
    )(*operands, early, after)

    tile = pl.pallas_call(
        last,
        in_specs=[VM] * (len(arrived) + 3),
        out_specs=VM,
        out_shape=shape((1, LANES, LANES)),
        scratch_shapes=scratch,
        compiler_params=GRANT,
        name="tile",
    )(*arrived, base, scale, same)
    return tile, cleaned


def solution(mesh):
    return jax.shard_map(
        functools.partial(shards, mesh.shape["det"], mesh.shape["tm"]),
        mesh=mesh,
        in_specs=(
            P("det", "tm"),
            P("det", "tm"),
            P("tm", None, None, None),
            P("tm", None),
            P("tm", None),
            P(),
            P("det"),
            P("det", None),
            P(),
        ),
        out_specs=(P(("det", "tm"), None, None), P("det", "tm")),
        check_vma=False,
    )
```

```python
import functools
import math

import jax
import jax.numpy as jnp
import numpy as np
from jax import lax
from jax.experimental import pallas as pl
from jax.experimental.pallas import tpu as pltpu
from jax.sharding import PartitionSpec as P

F32 = jnp.float32
BF16 = jnp.bfloat16
LANES = 128
BASE = 128
EXT = 16
EARLY = 2
MORE = 8
NN = (((1,), (0,)), ((), ()))
NT = (((1,), (1,)), ((), ()))


def mm(a, b, dims=NN):
    return lax.dot_general(a, b, dims, preferred_element_type=F32)


def split(x):
    hi = x.astype(BF16)
    return hi, (x - hi.astype(F32)).astype(BF16)


def iota(shape, axis):
    return lax.broadcasted_iota(jnp.int32, shape, axis)


def cosine_table(flen, rows):
    f = np.arange(rows)[:, None]
    n = np.arange(flen)[None, :]
    scale = np.where((f == 0) | (f == flen // 2), 1.0, 2.0) / flen
    scale = np.where(f <= flen // 2, scale, 0.0)
    return (scale * np.cos(2.0 * math.pi * ((f * n) % flen) / flen)).astype(np.float32)


def sums_kernel(modes, ts_hbm, flag_hbm, v_hbm, g_hbm, msg_ref, ts_ref, keep_ref, v_ref, g_ref, flag_ref, sem):
    dets, samples = ts_ref.shape
    streams = [(v_hbm, v_ref), (g_hbm, g_ref), (flag_hbm, flag_ref), (ts_hbm, ts_ref)]
    copies = [pltpu.make_async_copy(a, b, sem.at[i]) for i, (a, b) in enumerate(streams)]
    for copy in copies:
        copy.start()
    copies[0].wait()
    copies[1].wait()
    vt = v_ref[...]
    g = g_ref[...]
    row = iota((EXT, dets), 0)
    left1 = jnp.concatenate([vt, jnp.where(row < 2, g, 0.0)], axis=0)
    left2 = jnp.concatenate([vt * g, jnp.where((row >= 2) & (row < 4), g * g, 0.0)], axis=0)
    hi1, lo1 = split(left1)
    hi2, lo2 = split(left2)
    left1 = jnp.concatenate([hi1, lo1], axis=0)
    left2 = jnp.concatenate([hi2, lo2], axis=0)
    u = jnp.sum(vt * g, axis=1, keepdims=True)
    square = jnp.sum(g * g, axis=1, keepdims=True)
    lane = iota((modes, samples), 1)
    u = jnp.sum(jnp.where(lane == iota((modes, samples), 0), u, 0.0), axis=0, keepdims=True)
    u = jnp.where(iota((1, samples), 1) == modes, square, u)
    n = modes + EXT
    copies[2].wait()
    keep = (1 - flag_ref[...]).astype(F32)
    keep_ref[...] = keep.astype(BF16)
    both = mm(left2, keep.astype(BF16))
    acc2 = both[:n] + both[n:]
    copies[3].wait()
    x_hi, x_lo = split(ts_ref[...] * keep_ref[...].astype(F32))
    both = mm(left1, x_hi)
    acc1 = both[:n] + both[n:] + mm(hi1, x_lo)
    msg_ref[0:modes] = acc1[0:modes].astype(BF16)
    msg_ref[modes : 2 * modes] = acc2[0:modes].astype(BF16)
    row = iota((MORE, samples), 0)
    ext = acc1[modes : modes + MORE] + acc2[modes : modes + MORE] + jnp.where((row >= 4) & (row < 6), u, 0.0)
    hi = ext.astype(BF16).astype(F32)
    msg_ref[2 * modes :] = jnp.where(row % 2 == 1, ext - hi, hi).astype(BF16)


def prep_kernel(seg, kblk, lane_blocks, digits, tids_hbm, offs_hbm, owner_hbm, cos_hbm, point_hbm, gain_ref, v_ref,
                h2_ref, toep_ref, pnt_ref, v3_ref, geo_ref, own_ref,
                tids_ref, offs_ref, owner_ref, cos_ref, point_ref, wide_ref, sem):
    streams = [(cos_hbm, cos_ref), (point_hbm, point_ref), (tids_hbm, tids_ref), (offs_hbm, offs_ref),
               (owner_hbm, owner_ref)]
    copies = [pltpu.make_async_copy(a, b, sem.at[i]) for i, (a, b) in enumerate(streams)]
    for copy in copies:
        copy.start()
    flen = cos_ref.shape[1]
    vt = v_ref[...]
    vhi = vt.astype(BF16).astype(F32)
    pad = jnp.zeros((LANES - 3 * vt.shape[0], vt.shape[1]), F32)
    v3_ref[...] = jnp.concatenate([vhi, vhi, vt - vhi, pad], axis=0).T.astype(BF16)
    copies[0].wait()
    wide_ref[...] = jnp.zeros_like(wide_ref)
    wide_ref[0:1, 0 : gain_ref.shape[1]] = gain_ref[...]
    h = lax.dot_general(wide_ref[...], cos_ref[...], NN, precision=lax.Precision.HIGHEST, preferred_element_type=F32)
    base = jnp.broadcast_to(h[0:1], (LANES, flen))
    base = pltpu.roll(base, 0, 1, stride=1, stride_axis=0)
    base_hi, base_lo = split(base)
    blocks = flen // LANES
    for a in range(blocks):
        for b in range(blocks):
            c = (b - a) % blocks
            to = slice(b * LANES, (b + 1) * LANES)
            h2_ref[a * LANES : (a + 1) * LANES, to] = base_hi[:, c * LANES : (c + 1) * LANES]
            h2_ref[flen + a * LANES : flen + (a + 1) * LANES, to] = base_lo[:, c * LANES : (c + 1) * LANES]
    for c in range(blocks):
        at = slice(c * LANES, (c + 1) * LANES)
        toep_ref[at, 0:LANES] = base_hi[:, at]
        toep_ref[at, LANES : 2 * LANES] = base_lo[:, at]
    for copy in copies[1:]:
        copy.wait()
    listed = seg * kblk
    row16 = iota((listed, LANES), 0)
    first = lax.axis_index("tm") * listed
    squares = jnp.zeros((listed, LANES), F32)
    ext = geo_ref.shape[0] - listed
    row_x = iota((ext, LANES), 0)
    lane_x = iota((ext, LANES), 1)
    ids = jnp.zeros((ext, LANES), F32)
    own = jnp.zeros((listed, LANES), F32)
    for k in range(kblk):
        for s in range(seg):
            j = k * seg + s
            p = point_ref[s, k]
            span, tile = p.shape
            pnt_ref[s * span : (s + 1) * span, k * tile : (k + 1) * tile] = p
            pnt_ref[flen + k * tile : flen + (k + 1) * tile, s * span : (s + 1) * span] = p.T
            p = p.astype(F32)
            squares = jnp.where(row16 == j, jnp.sum(p * p, axis=0, keepdims=True), squares)
            target = owner_ref[tids_ref[s, k]] * LANES + offs_ref[s, k]
            own = jnp.where(row16 == j, target.astype(F32), own)
            place = first + j
            digit = target
            for d in range(digits):
                at = (row_x == d * lane_blocks + place // LANES) & (lane_x == place % LANES)
                ids = jnp.where(at, (digit % BASE).astype(F32), ids)
                digit = digit // BASE
    geo_ref[0:listed] = squares.astype(BF16)
    geo_ref[listed:] = ids.astype(BF16)
    own_ref[...] = own


def filtered(vectors, toep_ref):
    blocks = vectors[0].shape[1] // LANES
    rows = -(-2 * blocks * len(vectors) // EXT) * EXT
    row = iota((rows, LANES), 0)
    halves = []
    for b in vectors:
        hi, lo = split(b)
        halves += [hi.astype(F32), lo.astype(F32)]
    left = []
    for c in range(blocks):
        block = jnp.zeros((rows, LANES), F32)
        for i, half in enumerate(halves):
            for m in range(blocks):
                to = i * blocks + (m + c) % blocks
                block = jnp.where(row == to, half[:, m * LANES : (m + 1) * LANES], block)
        left.append(block.astype(BF16))
    z = mm(jnp.concatenate(left, axis=1), toep_ref[...])
    z = z[:, 0:LANES] + z[:, LANES:]
    out = []
    for i in range(len(vectors)):
        at = 2 * i * blocks
        out.append(z[at : at + blocks] + z[at + blocks : at + 2 * blocks])
    return out


def project(z, pn, seg, kblk):
    listed = seg * kblk
    hi, lo = split(z)
    hi, lo = hi.astype(F32), lo.astype(F32)
    row = iota((2 * listed, LANES), 0)
    left = []
    for s in range(seg):
        value = jnp.where(row < listed, hi[s : s + 1], lo[s : s + 1])
        left.append(jnp.where(row % seg == s, value, 0.0).astype(BF16))
    out = mm(jnp.concatenate(left, axis=1), pn)
    out = out[:listed] + out[listed:]
    row = iota((listed, LANES), 0)
    proj = out[:, 0:LANES]
    for k in range(1, kblk):
        proj = jnp.where(row // seg == k, out[:, k * LANES : (k + 1) * LANES], proj)
    return proj


def first_kernel(modes, seg, kblk, m0, m1, m2, m3, toep_ref, pnt_ref, geo_ref,
                 bq_ref, vec_ref, send_ref):
    tot = m0[...].astype(F32) + m1[...].astype(F32) + m2[...].astype(F32) + m3[...].astype(F32)
    bq_ref[...] = tot[0 : 2 * modes]
    ext = tot[2 * modes :]
    u_row = ext[4:5, 0:LANES] + ext[5:6, 0:LANES]
    u_col = jnp.sum(jnp.where(iota((modes, LANES), 0) == iota((modes, LANES), 1), u_row, 0.0), axis=1, keepdims=True)
    square = jnp.sum(jnp.where(iota((1, LANES), 1) == modes, u_row, 0.0), axis=1, keepdims=True)
    b1 = ext[0:1] + ext[1:2] - jnp.sum(u_col * tot[0:modes], axis=0, keepdims=True)
    b2 = ext[2:3] + ext[3:4] - jnp.sum(u_col * tot[modes : 2 * modes], axis=0, keepdims=True)
    row = iota((8, b1.shape[1]), 0)
    vec_ref[...] = jnp.where(row == 0, b1, jnp.where(row == 1, b2, jnp.where(row == 2, square, 0.0)))
    (z,) = filtered([b1], toep_ref)
    proj = project(z, pnt_ref[0 : b1.shape[1]], seg, kblk).astype(BF16)
    geo = geo_ref[...]
    listed = seg * kblk
    for t in range(send_ref.shape[0]):
        send_ref[t, 0:listed] = proj
        send_ref[t, listed : listed + geo.shape[0]] = geo
    if send_ref.shape[1] > listed + geo.shape[0]:
        blocks = b1.shape[1] // LANES
        row = iota((4 * blocks, LANES), 0)
        tail = jnp.zeros((4 * blocks, LANES), F32)
        for i, half in enumerate(split(b1) + split(b2)):
            for m in range(blocks):
                tail = jnp.where(row == i * blocks + m, half[:, m * LANES : (m + 1) * LANES].astype(F32), tail)
        send_ref[0, listed + geo.shape[0] :] = tail.astype(BF16)


def lane_ids(all_ref, listed, blocks, digits, b):
    ids = jnp.sum(all_ref[:, 2 * listed :].astype(F32), axis=0)
    out = ids[b : b + 1]
    for d in range(1, digits):
        out = out + float(BASE**d) * ids[d * blocks + b : d * blocks + b + 1]
    return out


def fetch(all_ref, own, vec_ref, listed, blocks, digits):
    per = LANES // listed
    psum = jnp.zeros((own.shape[0], LANES), F32)
    wsum = jnp.zeros((own.shape[0], LANES), F32)
    for b in range(blocks):
        same = (own == lane_ids(all_ref, listed, blocks, digits, b)).astype(F32).astype(BF16)
        part = all_ref[b * per : (b + 1) * per]
        psum = psum + mm(same, part[:, 0:listed].reshape(LANES, LANES))
        wsum = wsum + mm(same, part[:, listed : 2 * listed].reshape(LANES, LANES))
    return (psum / (1.0 + vec_ref[2:3, 0:LANES] * wsum)).astype(BF16).astype(F32)


def signal(fetched, pt, seg, kblk):
    samples = pt.shape[1]
    listed = seg * kblk
    row = iota((listed, LANES), 0)
    wide = [jnp.where(row // seg == k, fetched, 0.0).astype(BF16) for k in range(kblk)]
    spread = mm(jnp.concatenate(wide, axis=1), pt)
    row = iota((listed, samples), 0)
    lane = iota((listed, samples), 1)
    return jnp.sum(jnp.where(lane // (samples // seg) == row % seg, spread, 0.0), axis=0, keepdims=True)


def second_kernel(seg, kblk, digits, all_ref, own_ref, vec_ref, toep_ref, pnt_ref, sig_ref, send_ref):
    listed = seg * kblk
    blocks = all_ref.shape[0] * listed // LANES
    samples = vec_ref.shape[1]
    fetched = fetch(all_ref, own_ref[...], vec_ref, listed, blocks, digits)
    sig = signal(fetched, pnt_ref[samples:], seg, kblk)
    sig_ref[...] = jnp.broadcast_to(sig, sig_ref.shape)
    (z,) = filtered([vec_ref[0:1] - vec_ref[1:2] * sig], toep_ref)
    proj = project(z, pnt_ref[0:samples], seg, kblk).astype(BF16)
    for t in range(send_ref.shape[0]):
        send_ref[t] = proj


def assemble(pair_ref, near_ref, far_ref, cross_ref, all_ref):
    t = lax.axis_index("tm")
    core = t % 2
    far, other = 6 - 2 * core, 4 + 2 * core
    arrived = [
        (pair_ref, t),
        (near_ref, jnp.bitwise_xor(t, 2)),
        (far_ref, jnp.bitwise_xor(t, far)),
        (cross_ref, jnp.bitwise_xor(jnp.bitwise_xor(t, 1), other)),
    ]
    for ref, at in arrived:
        all_ref[at] = ref[0]
        all_ref[jnp.bitwise_xor(at, 1)] = ref[1]


def pair_second_kernel(seg, kblk, digits, pair_ref, near_ref, far_ref, cross_ref, mate_ref, vec_ref, toep_ref, pnt_ref,
                       mate_pnt_ref, all_ref, sig_ref, send_ref):
    assemble(pair_ref, near_ref, far_ref, cross_ref, all_ref)
    listed = seg * kblk
    blocks = all_ref.shape[0] * listed // LANES
    samples = vec_ref.shape[1]
    t = lax.axis_index("tm")
    mate = t + 1 - 2 * (t % 2)
    row = iota((2 * listed, LANES), 0)
    listing = jnp.where(row < listed, t * listed + row, mate * listed + row - listed)
    lane = iota((2 * listed, LANES), 1)
    own = jnp.zeros((2 * listed, 1), F32)
    for b in range(blocks):
        ids = lane_ids(all_ref, listed, blocks, digits, b)
        own = own + jnp.sum(jnp.where(listing == lane + b * LANES, ids, 0.0), axis=1, keepdims=True)
    fetched = fetch(all_ref, own, vec_ref, listed, blocks, digits)
    sig = signal(fetched[0:listed], pnt_ref[samples:], seg, kblk)
    mate_sig = signal(fetched[listed:], mate_pnt_ref[samples:], seg, kblk)
    sig_ref[...] = jnp.broadcast_to(sig, sig_ref.shape)
    rest = vec_ref[0:1] - vec_ref[1:2] * sig
    cuts = samples // LANES
    tail = mate_ref[0, pair_ref.shape[1] :].astype(F32)
    halves = [
        jnp.concatenate([tail[i * cuts + m : i * cuts + m + 1] for m in range(cuts)], axis=1) for i in range(4)
    ]
    mate_rest = halves[0] + halves[1] - (halves[2] + halves[3]) * mate_sig
    z, mate_z = filtered([rest, mate_rest], toep_ref)
    send_ref[0] = project(z, pnt_ref[0:samples], seg, kblk).astype(BF16)
    send_ref[1] = project(mate_z, mate_pnt_ref[0:samples], seg, kblk).astype(BF16)


def clean_rows(modes, at, ts_ref, keep_ref, g_ref, v3_ref, bq_ref, sig_ref, h2_ref):
    samples = ts_ref.shape[1]
    sig = sig_ref[0:1]
    q_hi, q_lo = split(bq_ref[0:modes] - bq_ref[modes : 2 * modes] * sig)
    pad = jnp.zeros((LANES - 3 * modes, samples), BF16)
    q3 = jnp.concatenate([q_hi, q_lo, q_hi, pad], axis=0)
    eye = iota((at.stop - at.start,) * 2, 0) == iota((at.stop - at.start,) * 2, 1)
    g_col = jnp.sum(jnp.where(eye, g_ref[:, at], 0.0), axis=1, keepdims=True)
    rest = (ts_ref[at] - g_col * sig) * keep_ref[at].astype(F32) - mm(v3_ref[at], q3)
    rest = rest.astype(BF16)
    return (mm(rest, h2_ref[0:samples]) + mm(rest, h2_ref[samples:])).astype(BF16)


def tile_parts(seg, kblk, digits, all_ref, vec_ref, base_ref, scale_ref, same_ref):
    listed = seg * kblk
    blocks = all_ref.shape[0] * listed // LANES
    per = LANES // listed
    psum = jnp.zeros((LANES, LANES), F32)
    wsum = jnp.zeros((LANES, LANES), F32)
    first = (lax.axis_index("det") * lax.axis_size("tm") + lax.axis_index("tm")) * LANES
    mine = (iota((LANES, LANES), 0) + first).astype(F32)
    for b in range(blocks):
        same = (mine == lane_ids(all_ref, listed, blocks, digits, b)).astype(F32).astype(BF16)
        same_ref[b] = same
        part = all_ref[b * per : (b + 1) * per]
        psum = psum + mm(same, part[:, 0:listed].reshape(LANES, LANES))
        wsum = wsum + mm(same, part[:, listed : 2 * listed].reshape(LANES, LANES))
    wsum = 1.0 + vec_ref[2:3, 0:LANES] * wsum
    scale = jnp.sqrt(wsum) / wsum
    scale_ref[...] = scale
    base_ref[...] = psum * scale


def early_kernel(seg, kblk, digits, modes, ts_ref, keep_ref, g_ref, v3_ref, bq_ref, sig_ref, h2_ref, all_ref, vec_ref,
                 early_ref, base_ref, scale_ref, same_ref):
    rows = slice(0, early_ref.shape[0])
    early_ref[...] = clean_rows(modes, rows, ts_ref, keep_ref, g_ref, v3_ref, bq_ref, sig_ref, h2_ref)
    tile_parts(seg, kblk, digits, all_ref, vec_ref, base_ref, scale_ref, same_ref)


def late_kernel(modes, ts_ref, keep_ref, g_ref, v3_ref, bq_ref, sig_ref, h2_ref, early_ref, after_ref, out_hbm,
                late_ref, sem):
    cut = early_ref.shape[0]
    first = pltpu.make_async_copy(early_ref, out_hbm.at[pl.ds(0, cut)], sem.at[0])
    first.start()
    rows = slice(cut, ts_ref.shape[0])
    late_ref[...] = clean_rows(modes, rows, ts_ref, keep_ref, g_ref, v3_ref, bq_ref, sig_ref, h2_ref)
    second = pltpu.make_async_copy(late_ref, out_hbm.at[pl.ds(cut, late_ref.shape[0])], sem.at[1])
    second.start()
    first.wait()
    second.wait()


def tile_kernel(all2_ref, base_ref, scale_ref, same_ref, out_ref):
    per = LANES // all2_ref.shape[1]
    psum = jnp.zeros((LANES, LANES), F32)
    for b in range(same_ref.shape[0]):
        psum = psum + mm(same_ref[b], all2_ref[b * per : (b + 1) * per].reshape(LANES, LANES))
    out_ref[0] = base_ref[...] + psum * scale_ref[...]


def pair_tile_kernel(pair_ref, near_ref, far_ref, cross_ref, base_ref, scale_ref, same_ref, out_ref, all_ref):
    assemble(pair_ref, near_ref, far_ref, cross_ref, all_ref)
    blocks, per = same_ref.shape[0], LANES // all_ref.shape[1]
    psum = jnp.zeros((LANES, LANES), F32)
    for b in range(blocks):
        psum = psum + mm(same_ref[b], all_ref[b * per : (b + 1) * per].reshape(LANES, LANES))
    out_ref[0] = base_ref[...] + psum * scale_ref[...]


VM = pl.BlockSpec(memory_space=pltpu.VMEM)
HB = pl.BlockSpec(memory_space=pltpu.HBM)
SM = pl.BlockSpec(memory_space=pltpu.SMEM)
GRANT = pltpu.CompilerParams(vmem_limit_bytes=12 * 2**20)


def shape(dims, dtype=F32):
    return jax.ShapeDtypeStruct(dims, dtype)


def others(x, axis, n):
    if n & (n - 1) == 0:
        pairs = [[(i, i ^ k) for i in range(n)] for k in range(1, n)]
    else:
        pairs = [[(i, (i + k) % n) for i in range(n)] for k in range(1, n)]
    return [lax.ppermute(x, axis, p) for p in pairs]


def shards(n_det, n_tm, timestream, sample_flags, pointing, tile_ids, block_offsets, tile_owner, det_gains,
           mode_vectors, filter_gain):
    dets, samples = timestream.shape
    modes = mode_vectors.shape[1]
    seg, kblk = tile_ids.shape
    listed = seg * kblk
    lane_blocks = n_tm * listed // LANES
    digits = -(-int(tile_owner.shape[0] * LANES - 1).bit_length() // 7)
    id_rows = -(-digits * lane_blocks // 8) * 8
    inputs = (timestream, sample_flags, mode_vectors.T, det_gains.reshape(1, dets))
    msg, ts, keep, vt, g = pl.pallas_call(
        functools.partial(sums_kernel, modes),
        in_specs=[HB] * 4,
        out_specs=[VM] * 5,
        out_shape=[
            shape((2 * modes + MORE, samples), BF16),
            shape((dets, samples)),
            shape((dets, samples), BF16),
            shape((modes, dets)),
            shape((1, dets)),
        ],
        scratch_shapes=[
            pltpu.VMEM((dets, samples), jnp.int32),
            pltpu.SemaphoreType.DMA((4,)),
        ],
        compiler_params=GRANT,
        name="sums",
    )(*(pltpu.with_memory_space_constraint(x, pltpu.HBM) for x in inputs))
    parts_of_all = [msg] + others(msg, "det", n_det)

    rows = -(-filter_gain.shape[0] // LANES) * LANES
    inputs = (tile_ids, block_offsets, tile_owner, jnp.asarray(cosine_table(samples, rows)), pointing)
    h2, toep, pnt, v3, geo, own = pl.pallas_call(
        functools.partial(prep_kernel, seg, kblk, lane_blocks, digits),
        in_specs=[HB] * 5 + [VM] * 2,
        out_specs=[VM] * 6,
        out_shape=[
            shape((2 * samples, samples), BF16),
            shape((samples, 2 * LANES), BF16),
            shape((2 * samples, samples), BF16),
            shape((dets, LANES), BF16),
            shape((listed + id_rows, LANES), BF16),
            shape((listed, LANES)),
        ],
        scratch_shapes=[
            pltpu.SMEM(tile_ids.shape, jnp.int32),
            pltpu.SMEM(block_offsets.shape, jnp.int32),
            pltpu.SMEM(tile_owner.shape, jnp.int32),
            pltpu.VMEM((rows, samples), F32),
            pltpu.VMEM(pointing.shape, BF16),
            pltpu.VMEM((8, rows), F32),
            pltpu.SemaphoreType.DMA((5,)),
        ],
        cost_estimate=pl.CostEstimate(flops=10**8, bytes_accessed=3 * 10**6, transcendentals=0),
        compiler_params=GRANT,
        name="prep",
    )(*(pltpu.with_memory_space_constraint(x, pltpu.HBM) for x in inputs), filter_gain.reshape(1, -1), vt)

    paired = n_tm == 8
    mates = [(i, i ^ 1) for i in range(n_tm)]

    def spread(pair):
        near = lax.ppermute(pair, "tm", [(i, i ^ 2) for i in range(n_tm)])
        far = lax.ppermute(pair, "tm", [(i, i ^ (6 - 2 * (i % 2))) for i in range(n_tm)])
        return pair, near, far, lax.ppermute(far, "tm", mates)

    block = 2 * listed + id_rows
    first_shape = (1, block + 4 * samples // LANES, LANES) if paired else (n_tm, block, LANES)
    bq, vec, send = pl.pallas_call(
        functools.partial(first_kernel, modes, seg, kblk),
        in_specs=[VM] * 7,
        out_specs=[VM] * 3,
        out_shape=[shape((2 * modes, samples)), shape((8, samples)), shape(first_shape, BF16)],
        compiler_params=GRANT,
        name="first",
    )(*parts_of_all, toep, pnt, geo)
    if paired:
        mate = lax.ppermute(send, "tm", mates)
        pair = jnp.concatenate([send[:, :block], mate[:, :block]], axis=0)
        late_pnt, pair = lax.optimization_barrier((pnt, pair))
        arrived = spread(pair)
        mate_pnt = lax.ppermute(late_pnt, "tm", mates)
        everyone, sig, send = pl.pallas_call(
            functools.partial(pair_second_kernel, seg, kblk, digits),
            in_specs=[VM] * 9,
            out_specs=[VM] * 3,
            out_shape=[
                shape((n_tm, block, LANES), BF16),
                shape((8, samples)),
                shape((2, listed, LANES), BF16),
            ],
            compiler_params=GRANT,
            name="second",
        )(*arrived, mate, vec, toep, pnt, mate_pnt)
        arrived = spread(send)
        after = arrived[2]
        last, scratch = pair_tile_kernel, [pltpu.VMEM((n_tm, listed, LANES), BF16)]
    else:
        everyone = lax.all_to_all(send, "tm", 0, 0)
        sig, send = pl.pallas_call(
            functools.partial(second_kernel, seg, kblk, digits),
            in_specs=[VM] * 5,
            out_specs=[VM] * 2,
            out_shape=[shape((8, samples)), shape((n_tm, listed, LANES), BF16)],
            compiler_params=GRANT,
            name="second",
        )(everyone, own, vec, toep, pnt)
        arrived = (lax.all_to_all(send, "tm", 0, 0),)
        after, last, scratch = vec, tile_kernel, []

    cut = EARLY * dets // 4
    operands = (ts, keep, g, v3, bq, sig, h2)
    early, base, scale, same = pl.pallas_call(
        functools.partial(early_kernel, seg, kblk, digits, modes),
        in_specs=[VM] * 9,
        out_specs=[VM] * 4,
        out_shape=[
            shape((cut, samples), BF16),
            shape((LANES, LANES)),
            shape((LANES, LANES)),
            shape((lane_blocks, LANES, LANES), BF16),
        ],
        cost_estimate=pl.CostEstimate(flops=5 * 10**8, bytes_accessed=2 * 10**6, transcendentals=0),
        compiler_params=GRANT,
        name="early",
    )(*operands, everyone, vec)
    cleaned = pl.pallas_call(
        functools.partial(late_kernel, modes),
        in_specs=[VM] * 9,
        out_specs=HB,
        out_shape=shape((dets, samples), BF16),
        scratch_shapes=[pltpu.VMEM((dets - cut, samples), BF16), pltpu.SemaphoreType.DMA((2,))],
        cost_estimate=pl.CostEstimate(flops=5 * 10**8, bytes_accessed=2 * 10**6, transcendentals=0),
        compiler_params=GRANT,
        name="late",
    )(*operands, early, after)

    tile = pl.pallas_call(
        last,
        in_specs=[VM] * (len(arrived) + 3),
        out_specs=VM,
        out_shape=shape((1, LANES, LANES)),
        scratch_shapes=scratch,
        compiler_params=GRANT,
        name="tile",
    )(*arrived, base, scale, same)
    return tile, cleaned


def solution(mesh):
    return jax.shard_map(
        functools.partial(shards, mesh.shape["det"], mesh.shape["tm"]),
        mesh=mesh,
        in_specs=(
            P("det", "tm"),
            P("det", "tm"),
            P("tm", None, None, None),
            P("tm", None),
            P("tm", None),
            P(),
            P("det"),
            P("det", None),
            P(),
        ),
        out_specs=(P(("det", "tm"), None, None), P("det", "tm")),
        check_vma=False,
    )
```

```python
import functools
import math

import jax
import jax.numpy as jnp
import numpy as np
from jax import lax
from jax.experimental import pallas as pl
from jax.experimental.pallas import tpu as pltpu
from jax.sharding import PartitionSpec as P

F32 = jnp.float32
BF16 = jnp.bfloat16
LANES = 128
BASE = 128
EXT = 16
EARLY = 2
MORE = 8
NN = (((1,), (0,)), ((), ()))


def mm(a, b, dims=NN):
    return lax.dot_general(a, b, dims, preferred_element_type=F32)


def split(x):
    hi = x.astype(BF16)
    return hi, (x - hi.astype(F32)).astype(BF16)


def iota(shape, axis):
    return lax.broadcasted_iota(jnp.int32, shape, axis)


def cosine_table(flen, rows):
    f = np.arange(rows)[:, None]
    n = np.arange(flen)[None, :]
    scale = np.where((f == 0) | (f == flen // 2), 1.0, 2.0) / flen
    scale = np.where(f <= flen // 2, scale, 0.0)
    return (scale * np.cos(2.0 * math.pi * ((f * n) % flen) / flen)).astype(np.float32)


def sums_kernel(modes, ts_hbm, flag_hbm, v_hbm, g_hbm, msg_ref, ts_ref, keep_ref, v_ref, g_ref, flag_ref, sem):
    dets, samples = ts_ref.shape
    streams = [(v_hbm, v_ref), (g_hbm, g_ref), (flag_hbm, flag_ref), (ts_hbm, ts_ref)]
    copies = [pltpu.make_async_copy(a, b, sem.at[i]) for i, (a, b) in enumerate(streams)]
    for copy in copies:
        copy.start()
    copies[0].wait()
    copies[1].wait()
    vt = v_ref[...]
    g = g_ref[...]
    row = iota((EXT, dets), 0)
    left1 = jnp.concatenate([vt, jnp.where(row < 2, g, 0.0)], axis=0)
    left2 = jnp.concatenate([vt * g, jnp.where((row >= 2) & (row < 4), g * g, 0.0)], axis=0)
    hi1, lo1 = split(left1)
    hi2, lo2 = split(left2)
    left1 = jnp.concatenate([hi1, lo1], axis=0)
    left2 = jnp.concatenate([hi2, lo2], axis=0)
    u = jnp.sum(vt * g, axis=1, keepdims=True)
    square = jnp.sum(g * g, axis=1, keepdims=True)
    lane = iota((modes, samples), 1)
    u = jnp.sum(jnp.where(lane == iota((modes, samples), 0), u, 0.0), axis=0, keepdims=True)
    u = jnp.where(iota((1, samples), 1) == modes, square, u)
    n = modes + EXT
    copies[2].wait()
    keep = (1 - flag_ref[...]).astype(F32)
    keep_ref[...] = keep.astype(BF16)
    both = mm(left2, keep.astype(BF16))
    acc2 = both[:n] + both[n:]
    copies[3].wait()
    x_hi, x_lo = split(ts_ref[...] * keep_ref[...].astype(F32))
    both = mm(left1, x_hi)
    acc1 = both[:n] + both[n:] + mm(hi1, x_lo)
    msg_ref[0:modes] = acc1[0:modes].astype(BF16)
    msg_ref[modes : 2 * modes] = acc2[0:modes].astype(BF16)
    row = iota((MORE, samples), 0)
    ext = acc1[modes : modes + MORE] + acc2[modes : modes + MORE] + jnp.where((row >= 4) & (row < 6), u, 0.0)
    hi = ext.astype(BF16).astype(F32)
    msg_ref[2 * modes :] = jnp.where(row % 2 == 1, ext - hi, hi).astype(BF16)


def prep_kernel(seg, kblk, digits, tids_hbm, offs_hbm, owner_hbm, cos_hbm, point_hbm, gain_ref, v_ref,
                h2_ref, toep_ref, pnt_ref, v3_ref, geo_ref,
                tids_ref, offs_ref, owner_ref, cos_ref, point_ref, wide_ref, sem):
    streams = [(cos_hbm, cos_ref), (point_hbm, point_ref), (tids_hbm, tids_ref), (offs_hbm, offs_ref),
               (owner_hbm, owner_ref)]
    copies = [pltpu.make_async_copy(a, b, sem.at[i]) for i, (a, b) in enumerate(streams)]
    for copy in copies:
        copy.start()
    flen = cos_ref.shape[1]
    vt = v_ref[...]
    vhi = vt.astype(BF16).astype(F32)
    pad = jnp.zeros((LANES - 3 * vt.shape[0], vt.shape[1]), F32)
    v3_ref[...] = jnp.concatenate([vhi, vhi, vt - vhi, pad], axis=0).T.astype(BF16)
    copies[0].wait()
    wide_ref[...] = jnp.zeros_like(wide_ref)
    wide_ref[0:1, 0 : gain_ref.shape[1]] = gain_ref[...]
    h = lax.dot_general(wide_ref[...], cos_ref[...], NN, precision=lax.Precision.HIGHEST, preferred_element_type=F32)
    base = jnp.broadcast_to(h[0:1], (LANES, flen))
    base = pltpu.roll(base, 0, 1, stride=1, stride_axis=0)
    base_hi, base_lo = split(base)
    blocks = flen // LANES
    for a in range(blocks):
        for b in range(blocks):
            c = (b - a) % blocks
            to = slice(b * LANES, (b + 1) * LANES)
            h2_ref[a * LANES : (a + 1) * LANES, to] = base_hi[:, c * LANES : (c + 1) * LANES]
            h2_ref[flen + a * LANES : flen + (a + 1) * LANES, to] = base_lo[:, c * LANES : (c + 1) * LANES]
    for c in range(blocks):
        at = slice(c * LANES, (c + 1) * LANES)
        toep_ref[at, 0:LANES] = base_hi[:, at]
        toep_ref[at, LANES : 2 * LANES] = base_lo[:, at]
    for copy in copies[1:]:
        copy.wait()
    listed = seg * kblk
    row16 = iota((listed, LANES), 0)
    squares = jnp.zeros((listed, LANES), F32)
    ext = geo_ref.shape[0] - listed
    row_x = iota((ext, LANES), 0)
    lane_x = iota((ext, LANES), 1)
    ids = jnp.zeros((ext, LANES), F32)
    for k in range(kblk):
        for s in range(seg):
            j = k * seg + s
            p = point_ref[s, k]
            span, tile = p.shape
            pnt_ref[s * span : (s + 1) * span, k * tile : (k + 1) * tile] = p
            pnt_ref[flen + k * tile : flen + (k + 1) * tile, s * span : (s + 1) * span] = p.T
            p = p.astype(F32)
            squares = jnp.where(row16 == j, jnp.sum(p * p, axis=0, keepdims=True), squares)
            target = owner_ref[tids_ref[s, k]] * LANES + offs_ref[s, k]
            for d in range(digits):
                ids = jnp.where((row_x == d) & (lane_x == j), (target % BASE).astype(F32), ids)
                target = target // BASE
    geo_ref[0:listed] = squares.astype(BF16)
    geo_ref[listed:] = ids.astype(BF16)


def filtered(vectors, toep_ref):
    blocks = vectors[0].shape[1] // LANES
    rows = -(-2 * blocks * len(vectors) // EXT) * EXT
    row = iota((rows, LANES), 0)
    halves = []
    for b in vectors:
        hi, lo = split(b)
        halves += [hi.astype(F32), lo.astype(F32)]
    left = []
    for c in range(blocks):
        block = jnp.zeros((rows, LANES), F32)
        for i, half in enumerate(halves):
            for m in range(blocks):
                to = i * blocks + (m + c) % blocks
                block = jnp.where(row == to, half[:, m * LANES : (m + 1) * LANES], block)
        left.append(block.astype(BF16))
    z = mm(jnp.concatenate(left, axis=1), toep_ref[...])
    z = z[:, 0:LANES] + z[:, LANES:]
    out = []
    for i in range(len(vectors)):
        at = 2 * i * blocks
        out.append(z[at : at + blocks] + z[at + blocks : at + 2 * blocks])
    return out


def project(z, pn, seg, kblk):
    listed = seg * kblk
    hi, lo = split(z)
    hi, lo = hi.astype(F32), lo.astype(F32)
    row = iota((2 * listed, LANES), 0)
    left = []
    for s in range(seg):
        value = jnp.where(row < listed, hi[s : s + 1], lo[s : s + 1])
        left.append(jnp.where(row % seg == s, value, 0.0).astype(BF16))
    out = mm(jnp.concatenate(left, axis=1), pn)
    out = out[:listed] + out[listed:]
    row = iota((listed, LANES), 0)
    proj = out[:, 0:LANES]
    for k in range(1, kblk):
        proj = jnp.where(row // seg == k, out[:, k * LANES : (k + 1) * LANES], proj)
    return proj


def first_kernel(modes, seg, kblk, m0, m1, m2, m3, toep_ref, pnt_ref, geo_ref,
                 bq_ref, vec_ref, send_ref):
    tot = m0[...].astype(F32) + m1[...].astype(F32) + m2[...].astype(F32) + m3[...].astype(F32)
    bq_ref[...] = tot[0 : 2 * modes]
    ext = tot[2 * modes :]
    u_row = ext[4:5, 0:LANES] + ext[5:6, 0:LANES]
    u_col = jnp.sum(jnp.where(iota((modes, LANES), 0) == iota((modes, LANES), 1), u_row, 0.0), axis=1, keepdims=True)
    square = jnp.sum(jnp.where(iota((1, LANES), 1) == modes, u_row, 0.0), axis=1, keepdims=True)
    b1 = ext[0:1] + ext[1:2] - jnp.sum(u_col * tot[0:modes], axis=0, keepdims=True)
    b2 = ext[2:3] + ext[3:4] - jnp.sum(u_col * tot[modes : 2 * modes], axis=0, keepdims=True)
    row = iota((8, b1.shape[1]), 0)
    vec_ref[...] = jnp.where(row == 0, b1, jnp.where(row == 1, b2, jnp.where(row == 2, square, 0.0)))
    (z,) = filtered([b1], toep_ref)
    proj = project(z, pnt_ref[0 : b1.shape[1]], seg, kblk).astype(BF16)
    geo = geo_ref[...]
    listed = seg * kblk
    for t in range(send_ref.shape[0]):
        send_ref[t, 0:listed] = proj
        send_ref[t, listed : listed + geo.shape[0]] = geo
    if send_ref.shape[1] > listed + geo.shape[0]:
        blocks = b1.shape[1] // LANES
        row = iota((4 * blocks, LANES), 0)
        tail = jnp.zeros((4 * blocks, LANES), F32)
        for i, half in enumerate(split(b1) + split(b2)):
            for m in range(blocks):
                tail = jnp.where(row == i * blocks + m, half[:, m * LANES : (m + 1) * LANES].astype(F32), tail)
        send_ref[0, listed + geo.shape[0] :] = tail.astype(BF16)


def row_ids(ext, digits):
    ext = ext.astype(F32)
    ids = ext[0:1]
    for d in range(1, digits):
        ids = ids + float(BASE**d) * ext[d : d + 1]
    return ids


def groups(refs, listed, digits):
    per = LANES // listed
    slots = [(ref, i) for ref in refs for i in range(ref.shape[0])]
    for b in range(len(slots) // per):
        part = slots[b * per : (b + 1) * per]
        row = iota((per, LANES), 0)
        ids = jnp.zeros((per, LANES), F32)
        for n, (ref, i) in enumerate(part):
            ids = jnp.where(row == n, row_ids(ref[i, 2 * listed :], digits), ids)
        ids = pltpu.roll(ids, 0, 1, stride=listed, stride_axis=0)
        ids = jnp.sum(ids, axis=0, keepdims=True)
        sums = jnp.concatenate([ref[i, 0:listed] for ref, i in part], axis=0)
        squares = jnp.concatenate([ref[i, listed : 2 * listed] for ref, i in part], axis=0)
        yield ids, sums, squares


def upright(ids, count):
    eye = iota((count, LANES), 0) == iota((count, LANES), 1)
    return jnp.sum(jnp.where(eye, ids, 0.0), axis=1, keepdims=True)


def fetch(parts, own, vec_ref):
    psum = jnp.zeros((own.shape[0], LANES), F32)
    wsum = jnp.zeros((own.shape[0], LANES), F32)
    for ids, sums, squares in parts:
        same = (own == ids).astype(F32).astype(BF16)
        psum = psum + mm(same, sums)
        wsum = wsum + mm(same, squares)
    return (psum / (1.0 + vec_ref[2:3, 0:LANES] * wsum)).astype(BF16).astype(F32)


def signal(fetched, pt, seg, kblk):
    samples = pt.shape[1]
    listed = seg * kblk
    row = iota((listed, LANES), 0)
    wide = [jnp.where(row // seg == k, fetched, 0.0).astype(BF16) for k in range(kblk)]
    spread = mm(jnp.concatenate(wide, axis=1), pt)
    row = iota((listed, samples), 0)
    lane = iota((listed, samples), 1)
    return jnp.sum(jnp.where(lane // (samples // seg) == row % seg, spread, 0.0), axis=0, keepdims=True)


def second_kernel(seg, kblk, digits, all_ref, geo_ref, vec_ref, toep_ref, pnt_ref, sig_ref, send_ref):
    listed = seg * kblk
    samples = vec_ref.shape[1]
    own = upright(row_ids(geo_ref[listed:], digits), listed)
    fetched = fetch(list(groups([all_ref], listed, digits)), own, vec_ref)
    sig = signal(fetched, pnt_ref[samples:], seg, kblk)
    sig_ref[...] = jnp.broadcast_to(sig, sig_ref.shape)
    (z,) = filtered([vec_ref[0:1] - vec_ref[1:2] * sig], toep_ref)
    proj = project(z, pnt_ref[0:samples], seg, kblk).astype(BF16)
    for t in range(send_ref.shape[0]):
        send_ref[t] = proj


def pair_second_kernel(seg, kblk, digits, pair_ref, near_ref, far_ref, cross_ref, mate_ref, vec_ref, toep_ref, pnt_ref,
                       mate_pnt_ref, sig_ref, send_ref):
    listed = seg * kblk
    samples = vec_ref.shape[1]
    parts = list(groups([pair_ref, near_ref, far_ref, cross_ref], listed, digits))
    fetched = fetch(parts, upright(parts[0][0], 2 * listed), vec_ref)
    sig = signal(fetched[0:listed], pnt_ref[samples:], seg, kblk)
    mate_sig = signal(fetched[listed:], mate_pnt_ref[samples:], seg, kblk)
    sig_ref[...] = jnp.broadcast_to(sig, sig_ref.shape)
    rest = vec_ref[0:1] - vec_ref[1:2] * sig
    cuts = samples // LANES
    tail = mate_ref[0, pair_ref.shape[1] :].astype(F32)
    halves = [
        jnp.concatenate([tail[i * cuts + m : i * cuts + m + 1] for m in range(cuts)], axis=1) for i in range(4)
    ]
    mate_rest = halves[0] + halves[1] - (halves[2] + halves[3]) * mate_sig
    z, mate_z = filtered([rest, mate_rest], toep_ref)
    send_ref[0] = project(z, pnt_ref[0:samples], seg, kblk).astype(BF16)
    send_ref[1] = project(mate_z, mate_pnt_ref[0:samples], seg, kblk).astype(BF16)


def clean_rows(modes, at, ts_ref, keep_ref, g_ref, v3_ref, bq_ref, sig_ref, h2_ref):
    samples = ts_ref.shape[1]
    sig = sig_ref[0:1]
    q_hi, q_lo = split(bq_ref[0:modes] - bq_ref[modes : 2 * modes] * sig)
    pad = jnp.zeros((LANES - 3 * modes, samples), BF16)
    q3 = jnp.concatenate([q_hi, q_lo, q_hi, pad], axis=0)
    count = at.stop - at.start
    eye = iota((count, count), 0) == iota((count, count), 1)
    g_col = jnp.sum(jnp.where(eye, g_ref[:, at], 0.0), axis=1, keepdims=True)
    rest = (ts_ref[at] - g_col * sig) * keep_ref[at].astype(F32) - mm(v3_ref[at], q3)
    rest = rest.astype(BF16)
    return (mm(rest, h2_ref[0:samples]) + mm(rest, h2_ref[samples:])).astype(BF16)


def early_kernel(seg, kblk, digits, modes, *refs):
    operands, vec_ref, all_refs, (early_ref, base_ref, scale_ref, same_ref) = refs[:7], refs[7], refs[8:-4], refs[-4:]
    early_ref[...] = clean_rows(modes, slice(0, early_ref.shape[0]), *operands)
    psum = jnp.zeros((LANES, LANES), F32)
    wsum = jnp.zeros((LANES, LANES), F32)
    first = (lax.axis_index("det") * lax.axis_size("tm") + lax.axis_index("tm")) * LANES
    mine = (iota((LANES, LANES), 0) + first).astype(F32)
    for b, (ids, sums, squares) in enumerate(groups(all_refs, seg * kblk, digits)):
        same = (mine == ids).astype(F32).astype(BF16)
        same_ref[b] = same
        psum = psum + mm(same, sums)
        wsum = wsum + mm(same, squares)
    wsum = 1.0 + vec_ref[2:3, 0:LANES] * wsum
    scale = jnp.sqrt(wsum) / wsum
    scale_ref[...] = scale
    base_ref[...] = psum * scale


def late_kernel(modes, *refs):
    operands, early_ref, (out_hbm, late_ref, sem) = refs[:7], refs[7], refs[-3:]
    cut, dets = early_ref.shape[0], operands[0].shape[0]
    copies = [
        pltpu.make_async_copy(early_ref, out_hbm.at[pl.ds(0, cut)], sem.at[0]),
        pltpu.make_async_copy(late_ref, out_hbm.at[pl.ds(cut, dets - cut)], sem.at[1]),
    ]
    copies[0].start()
    late_ref[...] = clean_rows(modes, slice(cut, dets), *operands)
    copies[1].start()
    for copy in copies:
        copy.wait()


def tile_kernel(*refs):
    all_refs, (base_ref, scale_ref, same_ref, out_ref) = refs[:-4], refs[-4:]
    slots = [ref[i] for ref in all_refs for i in range(ref.shape[0])]
    per = LANES // slots[0].shape[0]
    psum = jnp.zeros((LANES, LANES), F32)
    for b in range(same_ref.shape[0]):
        psum = psum + mm(same_ref[b], jnp.concatenate(slots[b * per : (b + 1) * per], axis=0))
    out_ref[0] = base_ref[...] + psum * scale_ref[...]


VM = pl.BlockSpec(memory_space=pltpu.VMEM)
HB = pl.BlockSpec(memory_space=pltpu.HBM)
SM = pl.BlockSpec(memory_space=pltpu.SMEM)
GRANT = pltpu.CompilerParams(vmem_limit_bytes=12 * 2**20)


def shape(dims, dtype=F32):
    return jax.ShapeDtypeStruct(dims, dtype)


def others(x, axis, n):
    if n & (n - 1) == 0:
        pairs = [[(i, i ^ k) for i in range(n)] for k in range(1, n)]
    else:
        pairs = [[(i, (i + k) % n) for i in range(n)] for k in range(1, n)]
    return [lax.ppermute(x, axis, p) for p in pairs]


def shards(n_det, n_tm, timestream, sample_flags, pointing, tile_ids, block_offsets, tile_owner, det_gains,
           mode_vectors, filter_gain):
    dets, samples = timestream.shape
    modes = mode_vectors.shape[1]
    seg, kblk = tile_ids.shape
    listed = seg * kblk
    lane_blocks = n_tm * listed // LANES
    digits = -(-int(tile_owner.shape[0] * LANES - 1).bit_length() // 7)
    id_rows = 8
    inputs = (timestream, sample_flags, mode_vectors.T, det_gains.reshape(1, dets))
    msg, ts, keep, vt, g = pl.pallas_call(
        functools.partial(sums_kernel, modes),
        in_specs=[HB] * 4,
        out_specs=[VM] * 5,
        out_shape=[
            shape((2 * modes + MORE, samples), BF16),
            shape((dets, samples)),
            shape((dets, samples), BF16),
            shape((modes, dets)),
            shape((1, dets)),
        ],
        scratch_shapes=[
            pltpu.VMEM((dets, samples), jnp.int32),
            pltpu.SemaphoreType.DMA((4,)),
        ],
        compiler_params=GRANT,
        name="sums",
    )(*(pltpu.with_memory_space_constraint(x, pltpu.HBM) for x in inputs))
    parts_of_all = [msg] + others(msg, "det", n_det)

    rows = -(-filter_gain.shape[0] // LANES) * LANES
    inputs = (tile_ids, block_offsets, tile_owner, jnp.asarray(cosine_table(samples, rows)), pointing)
    h2, toep, pnt, v3, geo = pl.pallas_call(
        functools.partial(prep_kernel, seg, kblk, digits),
        in_specs=[HB] * 5 + [VM] * 2,
        out_specs=[VM] * 5,
        out_shape=[
            shape((2 * samples, samples), BF16),
            shape((samples, 2 * LANES), BF16),
            shape((2 * samples, samples), BF16),
            shape((dets, LANES), BF16),
            shape((listed + id_rows, LANES), BF16),
        ],
        scratch_shapes=[
            pltpu.SMEM(tile_ids.shape, jnp.int32),
            pltpu.SMEM(block_offsets.shape, jnp.int32),
            pltpu.SMEM(tile_owner.shape, jnp.int32),
            pltpu.VMEM((rows, samples), F32),
            pltpu.VMEM(pointing.shape, BF16),
            pltpu.VMEM((8, rows), F32),
            pltpu.SemaphoreType.DMA((5,)),
        ],
        cost_estimate=pl.CostEstimate(flops=10**8, bytes_accessed=3 * 10**6, transcendentals=0),
        compiler_params=GRANT,
        name="prep",
    )(*(pltpu.with_memory_space_constraint(x, pltpu.HBM) for x in inputs), filter_gain.reshape(1, -1), vt)

    paired = n_tm == 8
    mates = [(i, i ^ 1) for i in range(n_tm)]

    nears = [(i, i ^ 2) for i in range(n_tm)]
    fars = [(i, i ^ (4 + 2 * (i % 2))) for i in range(n_tm)]
    block = 2 * listed + id_rows
    first_shape = (1, block + 4 * samples // LANES, LANES) if paired else (n_tm, block, LANES)
    bq, vec, send = pl.pallas_call(
        functools.partial(first_kernel, modes, seg, kblk),
        in_specs=[VM] * 7,
        out_specs=[VM] * 3,
        out_shape=[shape((2 * modes, samples)), shape((8, samples)), shape(first_shape, BF16)],
        compiler_params=GRANT,
        name="first",
    )(*parts_of_all, toep, pnt, geo)
    if paired:
        mate_pnt = lax.ppermute(pnt, "tm", mates)
        mate = lax.ppermute(send, "tm", mates)
        pair = jnp.concatenate([send[:, :block], mate[:, :block]], axis=0)
        near = lax.ppermute(pair, "tm", nears)
        far = lax.ppermute(pair, "tm", fars)
        arrived1 = (pair, near, far, lax.ppermute(far, "tm", mates))
        sig, send = pl.pallas_call(
            functools.partial(pair_second_kernel, seg, kblk, digits),
            in_specs=[VM] * 9,
            out_specs=[VM] * 2,
            out_shape=[shape((8, samples)), shape((2, listed, LANES), BF16)],
            compiler_params=GRANT,
            name="second",
        )(*arrived1, mate, vec, toep, pnt, mate_pnt)
        near = lax.ppermute(send, "tm", nears)
        far = lax.ppermute(send, "tm", fars)
    else:
        arrived1 = (lax.all_to_all(send, "tm", 0, 0),)
        sig, send = pl.pallas_call(
            functools.partial(second_kernel, seg, kblk, digits),
            in_specs=[VM] * 5,
            out_specs=[VM] * 2,
            out_shape=[shape((8, samples)), shape((n_tm, listed, LANES), BF16)],
            compiler_params=GRANT,
            name="second",
        )(*arrived1, geo, vec, toep, pnt)
        arrived2 = (lax.all_to_all(send, "tm", 0, 0),)

    cut = EARLY * dets // 4
    operands = (ts, keep, g, v3, bq, sig, h2)
    early, base, scale, same = pl.pallas_call(
        functools.partial(early_kernel, seg, kblk, digits, modes),
        in_specs=[VM] * (8 + len(arrived1)),
        out_specs=[VM] * 4,
        out_shape=[
            shape((cut, samples), BF16),
            shape((LANES, LANES)),
            shape((LANES, LANES)),
            shape((lane_blocks, LANES, LANES), BF16),
        ],
        cost_estimate=pl.CostEstimate(flops=5 * 10**8, bytes_accessed=2 * 10**6, transcendentals=0),
        compiler_params=GRANT,
        name="early",
    )(*operands, vec, *arrived1)
    after = vec
    if paired:
        far, base = lax.optimization_barrier((far, base))
        arrived2 = (send, near, far, lax.ppermute(far, "tm", mates))
        after = far
    cleaned = pl.pallas_call(
        functools.partial(late_kernel, modes),
        in_specs=[VM] * 9,
        out_specs=HB,
        out_shape=shape((dets, samples), BF16),
        scratch_shapes=[pltpu.VMEM((dets - cut, samples), BF16), pltpu.SemaphoreType.DMA((2,))],
        cost_estimate=pl.CostEstimate(flops=5 * 10**8, bytes_accessed=2 * 10**6, transcendentals=0),
        compiler_params=GRANT,
        name="late",
    )(*operands, early, after)

    tile = pl.pallas_call(
        tile_kernel,
        in_specs=[VM] * (len(arrived2) + 3),
        out_specs=VM,
        out_shape=shape((1, LANES, LANES)),
        compiler_params=GRANT,
        name="tile",
    )(*arrived2, base, scale, same)
    return tile, cleaned


def solution(mesh):
    def step(*args):
        return shards(mesh.shape["det"], mesh.shape["tm"], *args)

    step = jax.shard_map(
        step,
        mesh=mesh,
        in_specs=(
            P("det", "tm"),
            P("det", "tm"),
            P("tm", None, None, None),
            P("tm", None),
            P("tm", None),
            P(),
            P("det"),
            P("det", None),
            P(),
        ),
        out_specs=(P(("det", "tm"), None, None), P("det", "tm")),
        check_vma=False,
    )
    return step
```

```python
import functools
import math

import jax
import jax.numpy as jnp
import numpy as np
from jax import lax
from jax.experimental import pallas as pl
from jax.experimental.pallas import tpu as pltpu
from jax.sharding import PartitionSpec as P

F32 = jnp.float32
BF16 = jnp.bfloat16
LANES = 128
BASE = 128
EXT = 16
EARLY = 3
MORE = 8
NN = (((1,), (0,)), ((), ()))


def mm(a, b, dims=NN):
    return lax.dot_general(a, b, dims, preferred_element_type=F32)


def split(x):
    hi = x.astype(BF16)
    return hi, (x - hi.astype(F32)).astype(BF16)


def iota(shape, axis):
    return lax.broadcasted_iota(jnp.int32, shape, axis)


def cosine_table(flen, rows):
    f = np.arange(rows)[:, None]
    n = np.arange(flen)[None, :]
    scale = np.where((f == 0) | (f == flen // 2), 1.0, 2.0) / flen
    scale = np.where(f <= flen // 2, scale, 0.0)
    return (scale * np.cos(2.0 * math.pi * ((f * n) % flen) / flen)).astype(np.float32)


def sums_kernel(modes, ts_hbm, flag_hbm, v_hbm, g_hbm, msg_ref, ts_ref, keep_ref, v_ref, g_ref, flag_ref, sem):
    dets, samples = ts_ref.shape
    streams = [(v_hbm, v_ref), (g_hbm, g_ref), (flag_hbm, flag_ref), (ts_hbm, ts_ref)]
    copies = [pltpu.make_async_copy(a, b, sem.at[i]) for i, (a, b) in enumerate(streams)]
    for copy in copies:
        copy.start()
    copies[0].wait()
    copies[1].wait()
    vt = v_ref[...]
    g = g_ref[...]
    row = iota((EXT, dets), 0)
    left1 = jnp.concatenate([vt, jnp.where(row < 2, g, 0.0)], axis=0)
    left2 = jnp.concatenate([vt * g, jnp.where((row >= 2) & (row < 4), g * g, 0.0)], axis=0)
    hi1, lo1 = split(left1)
    hi2, lo2 = split(left2)
    left1 = jnp.concatenate([hi1, lo1], axis=0)
    left2 = jnp.concatenate([hi2, lo2], axis=0)
    u = jnp.sum(vt * g, axis=1, keepdims=True)
    square = jnp.sum(g * g, axis=1, keepdims=True)
    lane = iota((modes, samples), 1)
    u = jnp.sum(jnp.where(lane == iota((modes, samples), 0), u, 0.0), axis=0, keepdims=True)
    u = jnp.where(iota((1, samples), 1) == modes, square, u)
    n = modes + EXT
    copies[2].wait()
    keep = (1 - flag_ref[...]).astype(F32)
    keep_ref[...] = keep.astype(BF16)
    both = mm(left2, keep.astype(BF16))
    acc2 = both[:n] + both[n:]
    copies[3].wait()
    x_hi, x_lo = split(ts_ref[...] * keep_ref[...].astype(F32))
    both = mm(left1, x_hi)
    acc1 = both[:n] + both[n:] + mm(hi1, x_lo)
    msg_ref[0:modes] = acc1[0:modes].astype(BF16)
    msg_ref[modes : 2 * modes] = acc2[0:modes].astype(BF16)
    row = iota((MORE, samples), 0)
    ext = acc1[modes : modes + MORE] + acc2[modes : modes + MORE] + jnp.where((row >= 4) & (row < 6), u, 0.0)
    hi = ext.astype(BF16).astype(F32)
    msg_ref[2 * modes :] = jnp.where(row % 2 == 1, ext - hi, hi).astype(BF16)


def prep_kernel(seg, kblk, digits, tids_hbm, offs_hbm, owner_hbm, cos_hbm, point_hbm, gain_ref, v_ref,
                h2_ref, toep_ref, pnt_ref, v3_ref, geo_ref,
                tids_ref, offs_ref, owner_ref, cos_ref, point_ref, wide_ref, sem):
    streams = [(cos_hbm, cos_ref), (point_hbm, point_ref), (tids_hbm, tids_ref), (offs_hbm, offs_ref),
               (owner_hbm, owner_ref)]
    copies = [pltpu.make_async_copy(a, b, sem.at[i]) for i, (a, b) in enumerate(streams)]
    for copy in copies:
        copy.start()
    flen = cos_ref.shape[1]
    vt = v_ref[...]
    vhi = vt.astype(BF16).astype(F32)
    pad = jnp.zeros((LANES - 3 * vt.shape[0], vt.shape[1]), F32)
    v3_ref[...] = jnp.concatenate([vhi, vhi, vt - vhi, pad], axis=0).T.astype(BF16)
    copies[0].wait()
    wide_ref[...] = jnp.zeros_like(wide_ref)
    wide_ref[0:1, 0 : gain_ref.shape[1]] = gain_ref[...]
    h = lax.dot_general(wide_ref[...], cos_ref[...], NN, precision=lax.Precision.HIGHEST, preferred_element_type=F32)
    base = jnp.broadcast_to(h[0:1], (LANES, flen))
    base = pltpu.roll(base, 0, 1, stride=1, stride_axis=0)
    base_hi, base_lo = split(base)
    blocks = flen // LANES
    for a in range(blocks):
        for b in range(blocks):
            c = (b - a) % blocks
            to = slice(b * LANES, (b + 1) * LANES)
            h2_ref[a * LANES : (a + 1) * LANES, to] = base_hi[:, c * LANES : (c + 1) * LANES]
            h2_ref[flen + a * LANES : flen + (a + 1) * LANES, to] = base_lo[:, c * LANES : (c + 1) * LANES]
    for c in range(blocks):
        at = slice(c * LANES, (c + 1) * LANES)
        toep_ref[at, 0:LANES] = base_hi[:, at]
        toep_ref[at, LANES : 2 * LANES] = base_lo[:, at]
    for copy in copies[1:]:
        copy.wait()
    listed = seg * kblk
    row16 = iota((listed, LANES), 0)
    squares = jnp.zeros((listed, LANES), F32)
    ext = geo_ref.shape[0] - listed
    row_x = iota((ext, LANES), 0)
    lane_x = iota((ext, LANES), 1)
    ids = jnp.zeros((ext, LANES), F32)
    for k in range(kblk):
        for s in range(seg):
            j = k * seg + s
            p = point_ref[s, k]
            span, tile = p.shape
            pnt_ref[s * span : (s + 1) * span, k * tile : (k + 1) * tile] = p
            pnt_ref[flen + k * tile : flen + (k + 1) * tile, s * span : (s + 1) * span] = p.T
            p = p.astype(F32)
            squares = jnp.where(row16 == j, jnp.sum(p * p, axis=0, keepdims=True), squares)
            target = owner_ref[tids_ref[s, k]] * LANES + offs_ref[s, k]
            for d in range(digits):
                ids = jnp.where((row_x == d) & (lane_x % listed == j), (target % BASE).astype(F32), ids)
                target = target // BASE
    geo_ref[0:listed] = squares.astype(BF16)
    geo_ref[listed:] = ids.astype(BF16)


def filtered(vectors, toep_ref):
    blocks = vectors[0].shape[1] // LANES
    rows = -(-2 * blocks * len(vectors) // EXT) * EXT
    row = iota((rows, LANES), 0)
    halves = []
    for b in vectors:
        hi, lo = split(b)
        halves += [hi.astype(F32), lo.astype(F32)]
    left = []
    for c in range(blocks):
        block = jnp.zeros((rows, LANES), F32)
        for i, half in enumerate(halves):
            for m in range(blocks):
                to = i * blocks + (m + c) % blocks
                block = jnp.where(row == to, half[:, m * LANES : (m + 1) * LANES], block)
        left.append(block.astype(BF16))
    z = mm(jnp.concatenate(left, axis=1), toep_ref[...])
    z = z[:, 0:LANES] + z[:, LANES:]
    out = []
    for i in range(len(vectors)):
        at = 2 * i * blocks
        out.append(z[at : at + blocks] + z[at + blocks : at + 2 * blocks])
    return out


def project(z, pn, seg, kblk):
    listed = seg * kblk
    hi, lo = split(z)
    hi, lo = hi.astype(F32), lo.astype(F32)
    row = iota((2 * listed, LANES), 0)
    left = []
    for s in range(seg):
        value = jnp.where(row < listed, hi[s : s + 1], lo[s : s + 1])
        left.append(jnp.where(row % seg == s, value, 0.0).astype(BF16))
    out = mm(jnp.concatenate(left, axis=1), pn)
    out = out[:listed] + out[listed:]
    row = iota((listed, LANES), 0)
    proj = out[:, 0:LANES]
    for k in range(1, kblk):
        proj = jnp.where(row // seg == k, out[:, k * LANES : (k + 1) * LANES], proj)
    return proj


def first_kernel(modes, seg, kblk, m0, m1, m2, m3, toep_ref, pnt_ref, geo_ref,
                 bq_ref, vec_ref, send_ref):
    tot = m0[...].astype(F32) + m1[...].astype(F32) + m2[...].astype(F32) + m3[...].astype(F32)
    bq_ref[...] = tot[0 : 2 * modes]
    ext = tot[2 * modes :]
    u_row = ext[4:5, 0:LANES] + ext[5:6, 0:LANES]
    u_col = jnp.sum(jnp.where(iota((modes, LANES), 0) == iota((modes, LANES), 1), u_row, 0.0), axis=1, keepdims=True)
    square = jnp.sum(jnp.where(iota((1, LANES), 1) == modes, u_row, 0.0), axis=1, keepdims=True)
    b1 = ext[0:1] + ext[1:2] - jnp.sum(u_col * tot[0:modes], axis=0, keepdims=True)
    b2 = ext[2:3] + ext[3:4] - jnp.sum(u_col * tot[modes : 2 * modes], axis=0, keepdims=True)
    row = iota((8, b1.shape[1]), 0)
    vec_ref[...] = jnp.where(row == 0, b1, jnp.where(row == 1, b2, jnp.where(row == 2, square, 0.0)))
    (z,) = filtered([b1], toep_ref)
    proj = project(z, pnt_ref[0 : b1.shape[1]], seg, kblk).astype(BF16)
    geo = geo_ref[...]
    listed = seg * kblk
    for t in range(send_ref.shape[0]):
        send_ref[t, 0:listed] = proj
        send_ref[t, listed : listed + geo.shape[0]] = geo
    if send_ref.shape[1] > listed + geo.shape[0]:
        blocks = b1.shape[1] // LANES
        row = iota((4 * blocks, LANES), 0)
        tail = jnp.zeros((4 * blocks, LANES), F32)
        for i, half in enumerate(split(b1) + split(b2)):
            for m in range(blocks):
                tail = jnp.where(row == i * blocks + m, half[:, m * LANES : (m + 1) * LANES].astype(F32), tail)
        send_ref[0, listed + geo.shape[0] :] = tail.astype(BF16)


def row_ids(ext, digits):
    ext = ext.astype(F32)
    ids = ext[0:1]
    for d in range(1, digits):
        ids = ids + float(BASE**d) * ext[d : d + 1]
    return ids


def groups(refs, listed, digits):
    per = LANES // listed
    slots = [(ref, i) for ref in refs for i in range(ref.shape[0])]
    for b in range(len(slots) // per):
        part = slots[b * per : (b + 1) * per]
        lane = iota((1, LANES), 1)
        ids = jnp.zeros((1, LANES), F32)
        for n, (ref, i) in enumerate(part):
            ids = jnp.where(lane // listed == n, row_ids(ref[i, 2 * listed :], digits), ids)
        sums = jnp.concatenate([ref[i, 0:listed] for ref, i in part], axis=0)
        squares = jnp.concatenate([ref[i, listed : 2 * listed] for ref, i in part], axis=0)
        yield ids, sums, squares


def upright(ids, count):
    eye = iota((count, LANES), 0) == iota((count, LANES), 1)
    return jnp.sum(jnp.where(eye, ids, 0.0), axis=1, keepdims=True)


def fetch(parts, own, vec_ref):
    psum = jnp.zeros((own.shape[0], LANES), F32)
    wsum = jnp.zeros((own.shape[0], LANES), F32)
    for ids, sums, squares in parts:
        same = (own == ids).astype(F32).astype(BF16)
        psum = psum + mm(same, sums)
        wsum = wsum + mm(same, squares)
    return (psum / (1.0 + vec_ref[2:3, 0:LANES] * wsum)).astype(BF16).astype(F32)


def signal(fetched, pt, seg, kblk):
    samples = pt.shape[1]
    listed = seg * kblk
    row = iota((listed, LANES), 0)
    wide = [jnp.where(row // seg == k, fetched, 0.0).astype(BF16) for k in range(kblk)]
    spread = mm(jnp.concatenate(wide, axis=1), pt)
    row = iota((listed, samples), 0)
    lane = iota((listed, samples), 1)
    return jnp.sum(jnp.where(lane // (samples // seg) == row % seg, spread, 0.0), axis=0, keepdims=True)


def second_kernel(seg, kblk, digits, all_ref, geo_ref, vec_ref, toep_ref, pnt_ref, sig_ref, send_ref):
    listed = seg * kblk
    samples = vec_ref.shape[1]
    own = upright(row_ids(geo_ref[listed:], digits), listed)
    fetched = fetch(list(groups([all_ref], listed, digits)), own, vec_ref)
    sig = signal(fetched, pnt_ref[samples:], seg, kblk)
    sig_ref[...] = jnp.broadcast_to(sig, sig_ref.shape)
    (z,) = filtered([vec_ref[0:1] - vec_ref[1:2] * sig], toep_ref)
    proj = project(z, pnt_ref[0:samples], seg, kblk).astype(BF16)
    for t in range(send_ref.shape[0]):
        send_ref[t] = proj


def pair_second_kernel(seg, kblk, digits, pair_ref, near_ref, far_ref, cross_ref, mate_ref, vec_ref, toep_ref, pnt_ref,
                       mate_pnt_ref, sig_ref, send_ref):
    listed = seg * kblk
    samples = vec_ref.shape[1]
    parts = list(groups([pair_ref, near_ref, far_ref, cross_ref], listed, digits))
    fetched = fetch(parts, upright(parts[0][0], 2 * listed), vec_ref)
    sig = signal(fetched[0:listed], pnt_ref[samples:], seg, kblk)
    mate_sig = signal(fetched[listed:], mate_pnt_ref[samples:], seg, kblk)
    sig_ref[...] = jnp.broadcast_to(sig, sig_ref.shape)
    rest = vec_ref[0:1] - vec_ref[1:2] * sig
    cuts = samples // LANES
    tail = mate_ref[0, pair_ref.shape[1] :].astype(F32)
    halves = [
        jnp.concatenate([tail[i * cuts + m : i * cuts + m + 1] for m in range(cuts)], axis=1) for i in range(4)
    ]
    mate_rest = halves[0] + halves[1] - (halves[2] + halves[3]) * mate_sig
    z, mate_z = filtered([rest, mate_rest], toep_ref)
    send_ref[0] = project(z, pnt_ref[0:samples], seg, kblk).astype(BF16)
    send_ref[1] = project(mate_z, mate_pnt_ref[0:samples], seg, kblk).astype(BF16)


def stacked_modes(modes, bq_ref, sig_ref):
    q_hi, q_lo = split(bq_ref[0:modes] - bq_ref[modes : 2 * modes] * sig_ref[0:1])
    pad = jnp.zeros((LANES - 3 * modes, q_hi.shape[1]), BF16)
    return jnp.concatenate([q_hi, q_lo, q_hi, pad], axis=0)


def clean_rows(at, q3, ts_ref, keep_ref, g_ref, v3_ref, sig_ref, h2_ref):
    samples = ts_ref.shape[1]
    sig = sig_ref[0:1]
    count = at.stop - at.start
    eye = iota((count, count), 0) == iota((count, count), 1)
    g_col = jnp.sum(jnp.where(eye, g_ref[:, at], 0.0), axis=1, keepdims=True)
    rest = (ts_ref[at] - g_col * sig) * keep_ref[at].astype(F32) - mm(v3_ref[at], q3)
    rest = rest.astype(BF16)
    return (mm(rest, h2_ref[0:samples]) + mm(rest, h2_ref[samples:])).astype(BF16)


def early_kernel(seg, kblk, digits, modes, *refs):
    operands, bq_ref, vec_ref, all_refs = refs[:6], refs[6], refs[7], refs[8:-5]
    early_ref, q3_ref, base_ref, scale_ref, same_ref = refs[-5:]
    q3 = stacked_modes(modes, bq_ref, operands[4])
    q3_ref[...] = q3
    early_ref[...] = clean_rows(slice(0, early_ref.shape[0]), q3, *operands)
    psum = jnp.zeros((LANES, LANES), F32)
    wsum = jnp.zeros((LANES, LANES), F32)
    first = (lax.axis_index("det") * lax.axis_size("tm") + lax.axis_index("tm")) * LANES
    mine = (iota((LANES, LANES), 0) + first).astype(F32)
    for b, (ids, sums, squares) in enumerate(groups(all_refs, seg * kblk, digits)):
        same = (mine == ids).astype(F32).astype(BF16)
        same_ref[b] = same
        psum = psum + mm(same, sums)
        wsum = wsum + mm(same, squares)
    wsum = 1.0 + vec_ref[2:3, 0:LANES] * wsum
    scale = jnp.sqrt(wsum) / wsum
    scale_ref[...] = scale
    base_ref[...] = psum * scale


def late_kernel(*refs):
    operands, q3_ref, early_ref, (out_hbm, late_ref, sem) = refs[:6], refs[6], refs[7], refs[-3:]
    cut, dets = early_ref.shape[0], operands[0].shape[0]
    copies = [
        pltpu.make_async_copy(early_ref, out_hbm.at[pl.ds(0, cut)], sem.at[0]),
        pltpu.make_async_copy(late_ref, out_hbm.at[pl.ds(cut, dets - cut)], sem.at[1]),
    ]
    copies[0].start()
    late_ref[...] = clean_rows(slice(cut, dets), q3_ref[...], *operands)
    copies[1].start()
    for copy in copies:
        copy.wait()


def tile_kernel(*refs):
    all_refs, (base_ref, scale_ref, same_ref, out_ref) = refs[:-4], refs[-4:]
    slots = [ref[i] for ref in all_refs for i in range(ref.shape[0])]
    per = LANES // slots[0].shape[0]
    psum = jnp.zeros((LANES, LANES), F32)
    for b in range(same_ref.shape[0]):
        psum = psum + mm(same_ref[b], jnp.concatenate(slots[b * per : (b + 1) * per], axis=0))
    out_ref[0] = base_ref[...] + psum * scale_ref[...]


VM = pl.BlockSpec(memory_space=pltpu.VMEM)
HB = pl.BlockSpec(memory_space=pltpu.HBM)
SM = pl.BlockSpec(memory_space=pltpu.SMEM)
GRANT = pltpu.CompilerParams(vmem_limit_bytes=12 * 2**20)


def shape(dims, dtype=F32):
    return jax.ShapeDtypeStruct(dims, dtype)


def others(x, axis, n):
    if n & (n - 1) == 0:
        pairs = [[(i, i ^ k) for i in range(n)] for k in range(1, n)]
    else:
        pairs = [[(i, (i + k) % n) for i in range(n)] for k in range(1, n)]
    return [lax.ppermute(x, axis, p) for p in pairs]


def shards(n_det, n_tm, timestream, sample_flags, pointing, tile_ids, block_offsets, tile_owner, det_gains,
           mode_vectors, filter_gain):
    dets, samples = timestream.shape
    modes = mode_vectors.shape[1]
    seg, kblk = tile_ids.shape
    listed = seg * kblk
    lane_blocks = n_tm * listed // LANES
    digits = -(-int(tile_owner.shape[0] * LANES - 1).bit_length() // 7)
    id_rows = 8
    inputs = (timestream, sample_flags, mode_vectors.T, det_gains.reshape(1, dets))
    msg, ts, keep, vt, g = pl.pallas_call(
        functools.partial(sums_kernel, modes),
        in_specs=[HB] * 4,
        out_specs=[VM] * 5,
        out_shape=[
            shape((2 * modes + MORE, samples), BF16),
            shape((dets, samples)),
            shape((dets, samples), BF16),
            shape((modes, dets)),
            shape((1, dets)),
        ],
        scratch_shapes=[
            pltpu.VMEM((dets, samples), jnp.int32),
            pltpu.SemaphoreType.DMA((4,)),
        ],
        compiler_params=GRANT,
        name="sums",
    )(*(pltpu.with_memory_space_constraint(x, pltpu.HBM) for x in inputs))
    parts_of_all = [msg] + others(msg, "det", n_det)

    rows = -(-filter_gain.shape[0] // LANES) * LANES
    inputs = (tile_ids, block_offsets, tile_owner, jnp.asarray(cosine_table(samples, rows)), pointing)
    h2, toep, pnt, v3, geo = pl.pallas_call(
        functools.partial(prep_kernel, seg, kblk, digits),
        in_specs=[HB] * 5 + [VM] * 2,
        out_specs=[VM] * 5,
        out_shape=[
            shape((2 * samples, samples), BF16),
            shape((samples, 2 * LANES), BF16),
            shape((2 * samples, samples), BF16),
            shape((dets, LANES), BF16),
            shape((listed + id_rows, LANES), BF16),
        ],
        scratch_shapes=[
            pltpu.SMEM(tile_ids.shape, jnp.int32),
            pltpu.SMEM(block_offsets.shape, jnp.int32),
            pltpu.SMEM(tile_owner.shape, jnp.int32),
            pltpu.VMEM((rows, samples), F32),
            pltpu.VMEM(pointing.shape, BF16),
            pltpu.VMEM((8, rows), F32),
            pltpu.SemaphoreType.DMA((5,)),
        ],
        cost_estimate=pl.CostEstimate(flops=10**8, bytes_accessed=3 * 10**6, transcendentals=0),
        compiler_params=GRANT,
        name="prep",
    )(*(pltpu.with_memory_space_constraint(x, pltpu.HBM) for x in inputs), filter_gain.reshape(1, -1), vt)

    paired = n_tm == 8
    mates = [(i, i ^ 1) for i in range(n_tm)]

    nears = [(i, i ^ 2) for i in range(n_tm)]
    fars = [(i, i ^ (4 + 2 * (i % 2))) for i in range(n_tm)]
    block = 2 * listed + id_rows
    first_shape = (1, block + 4 * samples // LANES, LANES) if paired else (n_tm, block, LANES)
    bq, vec, send = pl.pallas_call(
        functools.partial(first_kernel, modes, seg, kblk),
        in_specs=[VM] * 7,
        out_specs=[VM] * 3,
        out_shape=[shape((2 * modes, samples)), shape((8, samples)), shape(first_shape, BF16)],
        compiler_params=GRANT,
        name="first",
    )(*parts_of_all, toep, pnt, geo)
    if paired:
        mate_pnt = lax.ppermute(pnt, "tm", mates)
        mate = lax.ppermute(send, "tm", mates)
        pair = jnp.concatenate([send[:, :block], mate[:, :block]], axis=0)
        near = lax.ppermute(pair, "tm", nears)
        far = lax.ppermute(pair, "tm", fars)
        arrived1 = (pair, near, far, lax.ppermute(far, "tm", mates))
        sig, send = pl.pallas_call(
            functools.partial(pair_second_kernel, seg, kblk, digits),
            in_specs=[VM] * 9,
            out_specs=[VM] * 2,
            out_shape=[shape((8, samples)), shape((2, listed, LANES), BF16)],
            compiler_params=GRANT,
            name="second",
        )(*arrived1, mate, vec, toep, pnt, mate_pnt)
        near = lax.ppermute(send, "tm", nears)
        far = lax.ppermute(send, "tm", fars)
    else:
        arrived1 = (lax.all_to_all(send, "tm", 0, 0),)
        sig, send = pl.pallas_call(
            functools.partial(second_kernel, seg, kblk, digits),
            in_specs=[VM] * 5,
            out_specs=[VM] * 2,
            out_shape=[shape((8, samples)), shape((n_tm, listed, LANES), BF16)],
            compiler_params=GRANT,
            name="second",
        )(*arrived1, geo, vec, toep, pnt)
        arrived2 = (lax.all_to_all(send, "tm", 0, 0),)

    cut = EARLY * dets // 4
    operands = (ts, keep, g, v3, sig, h2)
    early, q3, base, scale, same = pl.pallas_call(
        functools.partial(early_kernel, seg, kblk, digits, modes),
        in_specs=[VM] * (8 + len(arrived1)),
        out_specs=[VM] * 5,
        out_shape=[
            shape((cut, samples), BF16),
            shape((LANES, samples), BF16),
            shape((LANES, LANES)),
            shape((LANES, LANES)),
            shape((lane_blocks, LANES, LANES), BF16),
        ],
        cost_estimate=pl.CostEstimate(flops=5 * 10**8, bytes_accessed=2 * 10**6, transcendentals=0),
        compiler_params=GRANT,
        name="early",
    )(*operands, bq, vec, *arrived1)
    after = vec
    if paired:
        far, base = lax.optimization_barrier((far, base))
        arrived2 = (send, near, far, lax.ppermute(far, "tm", mates))
        after = far
    cleaned = pl.pallas_call(
        late_kernel,
        in_specs=[VM] * 9,
        out_specs=HB,
        out_shape=shape((dets, samples), BF16),
        scratch_shapes=[pltpu.VMEM((dets - cut, samples), BF16), pltpu.SemaphoreType.DMA((2,))],
        cost_estimate=pl.CostEstimate(flops=5 * 10**8, bytes_accessed=2 * 10**6, transcendentals=0),
        compiler_params=GRANT,
        name="late",
    )(*operands, q3, early, after)

    tile = pl.pallas_call(
        tile_kernel,
        in_specs=[VM] * (len(arrived2) + 3),
        out_specs=VM,
        out_shape=shape((1, LANES, LANES)),
        compiler_params=GRANT,
        name="tile",
    )(*arrived2, base, scale, same)
    return tile, cleaned


def solution(mesh):
    def step(*args):
        return shards(mesh.shape["det"], mesh.shape["tm"], *args)

    step = jax.shard_map(
        step,
        mesh=mesh,
        in_specs=(
            P("det", "tm"),
            P("det", "tm"),
            P("tm", None, None, None),
            P("tm", None),
            P("tm", None),
            P(),
            P("det"),
            P("det", None),
            P(),
        ),
        out_specs=(P(("det", "tm"), None, None), P("det", "tm")),
        check_vma=False,
    )
    return step
```

```python
import functools
import math

import jax
import jax.numpy as jnp
import numpy as np
from jax import lax
from jax.experimental import pallas as pl
from jax.experimental.pallas import tpu as pltpu
from jax.sharding import PartitionSpec as P

F32 = jnp.float32
BF16 = jnp.bfloat16
LANES = 128
BASE = 128
EXT = 16
EARLY = 3
MORE = 8
NN = (((1,), (0,)), ((), ()))


def mm(a, b, dims=NN):
    return lax.dot_general(a, b, dims, preferred_element_type=F32)


def split(x):
    hi = x.astype(BF16)
    return hi, (x - hi.astype(F32)).astype(BF16)


def iota(shape, axis):
    return lax.broadcasted_iota(jnp.int32, shape, axis)


def cosine_table(flen, rows):
    f = np.arange(rows)[:, None]
    n = np.arange(flen)[None, :]
    scale = np.where((f == 0) | (f == flen // 2), 1.0, 2.0) / flen
    scale = np.where(f <= flen // 2, scale, 0.0)
    return (scale * np.cos(2.0 * math.pi * ((f * n) % flen) / flen)).astype(np.float32)


def sums_kernel(modes, ts_hbm, flag_hbm, v_hbm, g_hbm, msg_ref, ts_ref, keep_ref, v_ref, g_ref, flag_ref, sem):
    dets, samples = ts_ref.shape
    streams = [(v_hbm, v_ref), (g_hbm, g_ref), (flag_hbm, flag_ref), (ts_hbm, ts_ref)]
    copies = [pltpu.make_async_copy(a, b, sem.at[i]) for i, (a, b) in enumerate(streams)]
    for copy in copies:
        copy.start()
    copies[0].wait()
    copies[1].wait()
    vt = v_ref[...]
    g = g_ref[...]
    row = iota((EXT, dets), 0)
    left1 = jnp.concatenate([vt, jnp.where(row < 2, g, 0.0)], axis=0)
    left2 = jnp.concatenate([vt * g, jnp.where((row >= 2) & (row < 4), g * g, 0.0)], axis=0)
    hi1, lo1 = split(left1)
    hi2, lo2 = split(left2)
    left1 = jnp.concatenate([hi1, lo1], axis=0)
    left2 = jnp.concatenate([hi2, lo2], axis=0)
    u = jnp.sum(vt * g, axis=1, keepdims=True)
    square = jnp.sum(g * g, axis=1, keepdims=True)
    lane = iota((modes, samples), 1)
    u = jnp.sum(jnp.where(lane == iota((modes, samples), 0), u, 0.0), axis=0, keepdims=True)
    u = jnp.where(iota((1, samples), 1) == modes, square, u)
    n = modes + EXT
    copies[2].wait()
    keep = (1 - flag_ref[...]).astype(F32)
    keep_ref[...] = keep.astype(BF16)
    both = mm(left2, keep.astype(BF16))
    acc2 = both[:n] + both[n:]
    copies[3].wait()
    x_hi, x_lo = split(ts_ref[...] * keep_ref[...].astype(F32))
    both = mm(left1, x_hi)
    acc1 = both[:n] + both[n:] + mm(hi1, x_lo)
    msg_ref[0:modes] = acc1[0:modes].astype(BF16)
    msg_ref[modes : 2 * modes] = acc2[0:modes].astype(BF16)
    row = iota((MORE, samples), 0)
    ext = acc1[modes : modes + MORE] + acc2[modes : modes + MORE] + jnp.where((row >= 4) & (row < 6), u, 0.0)
    hi = ext.astype(BF16).astype(F32)
    msg_ref[2 * modes :] = jnp.where(row % 2 == 1, ext - hi, hi).astype(BF16)


def prep_kernel(seg, kblk, digits, tids_hbm, offs_hbm, owner_hbm, cos_hbm, point_hbm, gain_ref, v_ref,
                h2_ref, toep_ref, pnt_ref, v3_ref, geo_ref,
                tids_ref, offs_ref, owner_ref, cos_ref, point_ref, wide_ref, sem):
    streams = [(cos_hbm, cos_ref), (point_hbm, point_ref), (tids_hbm, tids_ref), (offs_hbm, offs_ref),
               (owner_hbm, owner_ref)]
    copies = [pltpu.make_async_copy(a, b, sem.at[i]) for i, (a, b) in enumerate(streams)]
    for copy in copies:
        copy.start()
    flen = cos_ref.shape[1]
    vt = v_ref[...]
    vhi = vt.astype(BF16).astype(F32)
    pad = jnp.zeros((LANES - 3 * vt.shape[0], vt.shape[1]), F32)
    v3_ref[...] = jnp.concatenate([vhi, vhi, vt - vhi, pad], axis=0).T.astype(BF16)
    copies[0].wait()
    wide_ref[...] = jnp.zeros_like(wide_ref)
    wide_ref[0:1, 0 : gain_ref.shape[1]] = gain_ref[...]
    h = lax.dot_general(wide_ref[...], cos_ref[...], NN, precision=lax.Precision.HIGHEST, preferred_element_type=F32)
    base = jnp.broadcast_to(h[0:1], (LANES, flen))
    base = pltpu.roll(base, 0, 1, stride=1, stride_axis=0)
    base_hi, base_lo = split(base)
    blocks = flen // LANES
    for a in range(blocks):
        for b in range(blocks):
            c = (b - a) % blocks
            to = slice(b * LANES, (b + 1) * LANES)
            h2_ref[a * LANES : (a + 1) * LANES, to] = base_hi[:, c * LANES : (c + 1) * LANES]
            h2_ref[flen + a * LANES : flen + (a + 1) * LANES, to] = base_lo[:, c * LANES : (c + 1) * LANES]
    for c in range(blocks):
        at = slice(c * LANES, (c + 1) * LANES)
        toep_ref[at, 0:LANES] = base_hi[:, at]
        toep_ref[at, LANES : 2 * LANES] = base_lo[:, at]
    for copy in copies[1:]:
        copy.wait()
    listed = seg * kblk
    row16 = iota((listed, LANES), 0)
    squares = jnp.zeros((listed, LANES), F32)
    ext = geo_ref.shape[0] - listed
    row_x = iota((ext, LANES), 0)
    lane_x = iota((ext, LANES), 1)
    ids = jnp.zeros((ext, LANES), F32)
    for k in range(kblk):
        for s in range(seg):
            j = k * seg + s
            p = point_ref[s, k]
            span, tile = p.shape
            pnt_ref[s * span : (s + 1) * span, k * tile : (k + 1) * tile] = p
            pnt_ref[flen + k * tile : flen + (k + 1) * tile, s * span : (s + 1) * span] = p.T
            p = p.astype(F32)
            squares = jnp.where(row16 == j, jnp.sum(p * p, axis=0, keepdims=True), squares)
            target = owner_ref[tids_ref[s, k]] * LANES + offs_ref[s, k]
            for d in range(digits):
                ids = jnp.where((row_x == d) & (lane_x % listed == j), (target % BASE).astype(F32), ids)
                target = target // BASE
    geo_ref[0:listed] = squares.astype(BF16)
    geo_ref[listed:] = ids.astype(BF16)


def filtered(vectors, toep_ref):
    blocks = vectors[0].shape[1] // LANES
    rows = -(-2 * blocks * len(vectors) // EXT) * EXT
    row = iota((rows, LANES), 0)
    halves = []
    for b in vectors:
        hi, lo = split(b)
        halves += [hi.astype(F32), lo.astype(F32)]
    left = []
    for c in range(blocks):
        block = jnp.zeros((rows, LANES), F32)
        for i, half in enumerate(halves):
            for m in range(blocks):
                to = i * blocks + (m + c) % blocks
                block = jnp.where(row == to, half[:, m * LANES : (m + 1) * LANES], block)
        left.append(block.astype(BF16))
    z = mm(jnp.concatenate(left, axis=1), toep_ref[...])
    z = z[:, 0:LANES] + z[:, LANES:]
    out = []
    for i in range(len(vectors)):
        at = 2 * i * blocks
        out.append(z[at : at + blocks] + z[at + blocks : at + 2 * blocks])
    return out


def project(z, pn, seg, kblk):
    listed = seg * kblk
    hi, lo = split(z)
    hi, lo = hi.astype(F32), lo.astype(F32)
    row = iota((2 * listed, LANES), 0)
    left = []
    for s in range(seg):
        value = jnp.where(row < listed, hi[s : s + 1], lo[s : s + 1])
        left.append(jnp.where(row % seg == s, value, 0.0).astype(BF16))
    out = mm(jnp.concatenate(left, axis=1), pn)
    out = out[:listed] + out[listed:]
    row = iota((listed, LANES), 0)
    proj = out[:, 0:LANES]
    for k in range(1, kblk):
        proj = jnp.where(row // seg == k, out[:, k * LANES : (k + 1) * LANES], proj)
    return proj


def first_kernel(modes, seg, kblk, m0, m1, m2, m3, toep_ref, pnt_ref, geo_ref,
                 vec_ref, send_ref):
    tot = m0[...].astype(F32) + m1[...].astype(F32) + m2[...].astype(F32) + m3[...].astype(F32)
    ext = tot[2 * modes :]
    u_row = ext[4:5, 0:LANES] + ext[5:6, 0:LANES]
    u_col = jnp.sum(jnp.where(iota((modes, LANES), 0) == iota((modes, LANES), 1), u_row, 0.0), axis=1, keepdims=True)
    square = jnp.sum(jnp.where(iota((1, LANES), 1) == modes, u_row, 0.0), axis=1, keepdims=True)
    b1 = ext[0:1] + ext[1:2] - jnp.sum(u_col * tot[0:modes], axis=0, keepdims=True)
    b2 = ext[2:3] + ext[3:4] - jnp.sum(u_col * tot[modes : 2 * modes], axis=0, keepdims=True)
    row = iota((8, b1.shape[1]), 0)
    vec_ref[...] = jnp.where(row == 0, b1, jnp.where(row == 1, b2, jnp.where(row == 2, square, 0.0)))
    (z,) = filtered([b1], toep_ref)
    proj = project(z, pnt_ref[0 : b1.shape[1]], seg, kblk).astype(BF16)
    geo = geo_ref[...]
    listed = seg * kblk
    for t in range(send_ref.shape[0]):
        send_ref[t, 0:listed] = proj
        send_ref[t, listed : listed + geo.shape[0]] = geo
    if send_ref.shape[1] > listed + geo.shape[0]:
        blocks = b1.shape[1] // LANES
        row = iota((4 * blocks, LANES), 0)
        tail = jnp.zeros((4 * blocks, LANES), F32)
        for i, half in enumerate(split(b1) + split(b2)):
            for m in range(blocks):
                tail = jnp.where(row == i * blocks + m, half[:, m * LANES : (m + 1) * LANES].astype(F32), tail)
        send_ref[0, listed + geo.shape[0] :] = tail.astype(BF16)


def row_ids(ext, digits):
    ext = ext.astype(F32)
    ids = ext[0:1]
    for d in range(1, digits):
        ids = ids + float(BASE**d) * ext[d : d + 1]
    return ids


def groups(refs, listed, digits):
    per = LANES // listed
    slots = [(ref, i) for ref in refs for i in range(ref.shape[0])]
    for b in range(len(slots) // per):
        part = slots[b * per : (b + 1) * per]
        lane = iota((1, LANES), 1)
        ids = jnp.zeros((1, LANES), F32)
        for n, (ref, i) in enumerate(part):
            ids = jnp.where(lane // listed == n, row_ids(ref[i, 2 * listed :], digits), ids)
        sums = jnp.concatenate([ref[i, 0:listed] for ref, i in part], axis=0)
        squares = jnp.concatenate([ref[i, listed : 2 * listed] for ref, i in part], axis=0)
        yield ids, sums, squares


def upright(ids, count):
    eye = iota((count, LANES), 0) == iota((count, LANES), 1)
    return jnp.sum(jnp.where(eye, ids, 0.0), axis=1, keepdims=True)


def fetch(parts, own, vec_ref):
    psum = jnp.zeros((own.shape[0], LANES), F32)
    wsum = jnp.zeros((own.shape[0], LANES), F32)
    for ids, sums, squares in parts:
        same = (own == ids).astype(F32).astype(BF16)
        psum = psum + mm(same, sums)
        wsum = wsum + mm(same, squares)
    return (psum / (1.0 + vec_ref[2:3, 0:LANES] * wsum)).astype(BF16).astype(F32)


def signal(fetched, pt, seg, kblk):
    samples = pt.shape[1]
    listed = seg * kblk
    row = iota((listed, LANES), 0)
    wide = [jnp.where(row // seg == k, fetched, 0.0).astype(BF16) for k in range(kblk)]
    spread = mm(jnp.concatenate(wide, axis=1), pt)
    row = iota((listed, samples), 0)
    lane = iota((listed, samples), 1)
    return jnp.sum(jnp.where(lane // (samples // seg) == row % seg, spread, 0.0), axis=0, keepdims=True)


def second_kernel(seg, kblk, digits, all_ref, geo_ref, vec_ref, toep_ref, pnt_ref, sig_ref, send_ref):
    listed = seg * kblk
    samples = vec_ref.shape[1]
    own = upright(row_ids(geo_ref[listed:], digits), listed)
    fetched = fetch(list(groups([all_ref], listed, digits)), own, vec_ref)
    sig = signal(fetched, pnt_ref[samples:], seg, kblk)
    sig_ref[...] = jnp.broadcast_to(sig, sig_ref.shape)
    (z,) = filtered([vec_ref[0:1] - vec_ref[1:2] * sig], toep_ref)
    proj = project(z, pnt_ref[0:samples], seg, kblk).astype(BF16)
    for t in range(send_ref.shape[0]):
        send_ref[t] = proj


def pair_second_kernel(seg, kblk, digits, pair_ref, near_ref, far_ref, cross_ref, mate_ref, vec_ref, toep_ref, pnt_ref,
                       mate_pnt_ref, sig_ref, send_ref):
    listed = seg * kblk
    samples = vec_ref.shape[1]
    parts = list(groups([pair_ref, near_ref, far_ref, cross_ref], listed, digits))
    fetched = fetch(parts, upright(parts[0][0], 2 * listed), vec_ref)
    sig = signal(fetched[0:listed], pnt_ref[samples:], seg, kblk)
    mate_sig = signal(fetched[listed:], mate_pnt_ref[samples:], seg, kblk)
    sig_ref[...] = jnp.broadcast_to(sig, sig_ref.shape)
    rest = vec_ref[0:1] - vec_ref[1:2] * sig
    cuts = samples // LANES
    tail = mate_ref[0, pair_ref.shape[1] :].astype(F32)
    halves = [
        jnp.concatenate([tail[i * cuts + m : i * cuts + m + 1] for m in range(cuts)], axis=1) for i in range(4)
    ]
    mate_rest = halves[0] + halves[1] - (halves[2] + halves[3]) * mate_sig
    z, mate_z = filtered([rest, mate_rest], toep_ref)
    send_ref[0] = project(z, pnt_ref[0:samples], seg, kblk).astype(BF16)
    send_ref[1] = project(mate_z, mate_pnt_ref[0:samples], seg, kblk).astype(BF16)


def stacked_modes(modes, messages, sig_ref):
    tot = sum(message[0 : 2 * modes].astype(F32) for message in messages)
    q_hi, q_lo = split(tot[0:modes] - tot[modes:] * sig_ref[0:1])
    pad = jnp.zeros((LANES - 3 * modes, q_hi.shape[1]), BF16)
    return jnp.concatenate([q_hi, q_lo, q_hi, pad], axis=0)


def clean_rows(at, q3, ts_ref, keep_ref, g_ref, v3_ref, sig_ref, h2_ref):
    samples = ts_ref.shape[1]
    sig = sig_ref[0:1]
    count = at.stop - at.start
    eye = iota((count, count), 0) == iota((count, count), 1)
    g_col = jnp.sum(jnp.where(eye, g_ref[:, at], 0.0), axis=1, keepdims=True)
    rest = (ts_ref[at] - g_col * sig) * keep_ref[at].astype(F32) - mm(v3_ref[at], q3)
    rest = rest.astype(BF16)
    return (mm(rest, h2_ref[0:samples]) + mm(rest, h2_ref[samples:])).astype(BF16)


def early_kernel(seg, kblk, digits, modes, count, *refs):
    operands, messages, vec_ref, all_refs = refs[:6], refs[6 : 6 + count], refs[6 + count], refs[7 + count : -5]
    early_ref, q3_ref, base_ref, scale_ref, same_ref = refs[-5:]
    q3 = stacked_modes(modes, messages, operands[4])
    q3_ref[...] = q3
    early_ref[...] = clean_rows(slice(0, early_ref.shape[0]), q3, *operands)
    psum = jnp.zeros((LANES, LANES), F32)
    wsum = jnp.zeros((LANES, LANES), F32)
    first = (lax.axis_index("det") * lax.axis_size("tm") + lax.axis_index("tm")) * LANES
    mine = (iota((LANES, LANES), 0) + first).astype(F32)
    for b, (ids, sums, squares) in enumerate(groups(all_refs, seg * kblk, digits)):
        same = (mine == ids).astype(F32).astype(BF16)
        same_ref[b] = same
        psum = psum + mm(same, sums)
        wsum = wsum + mm(same, squares)
    wsum = 1.0 + vec_ref[2:3, 0:LANES] * wsum
    scale = jnp.sqrt(wsum) / wsum
    scale_ref[...] = scale
    base_ref[...] = psum * scale


def late_kernel(*refs):
    operands, q3_ref, early_ref, (out_hbm, late_ref, sem) = refs[:6], refs[6], refs[7], refs[-3:]
    cut, dets = early_ref.shape[0], operands[0].shape[0]
    copies = [
        pltpu.make_async_copy(early_ref, out_hbm.at[pl.ds(0, cut)], sem.at[0]),
        pltpu.make_async_copy(late_ref, out_hbm.at[pl.ds(cut, dets - cut)], sem.at[1]),
    ]
    copies[0].start()
    late_ref[...] = clean_rows(slice(cut, dets), q3_ref[...], *operands)
    copies[1].start()
    for copy in copies:
        copy.wait()


def tile_kernel(*refs):
    all_refs, (base_ref, scale_ref, same_ref, out_ref) = refs[:-4], refs[-4:]
    slots = [ref[i] for ref in all_refs for i in range(ref.shape[0])]
    per = LANES // slots[0].shape[0]
    psum = jnp.zeros((LANES, LANES), F32)
    for b in range(same_ref.shape[0]):
        psum = psum + mm(same_ref[b], jnp.concatenate(slots[b * per : (b + 1) * per], axis=0))
    out_ref[0] = base_ref[...] + psum * scale_ref[...]


VM = pl.BlockSpec(memory_space=pltpu.VMEM)
HB = pl.BlockSpec(memory_space=pltpu.HBM)
SM = pl.BlockSpec(memory_space=pltpu.SMEM)
GRANT = pltpu.CompilerParams(vmem_limit_bytes=12 * 2**20)


def shape(dims, dtype=F32):
    return jax.ShapeDtypeStruct(dims, dtype)


def others(x, axis, n):
    if n & (n - 1) == 0:
        pairs = [[(i, i ^ k) for i in range(n)] for k in range(1, n)]
    else:
        pairs = [[(i, (i + k) % n) for i in range(n)] for k in range(1, n)]
    return [lax.ppermute(x, axis, p) for p in pairs]


def shards(n_det, n_tm, timestream, sample_flags, pointing, tile_ids, block_offsets, tile_owner, det_gains,
           mode_vectors, filter_gain):
    dets, samples = timestream.shape
    modes = mode_vectors.shape[1]
    seg, kblk = tile_ids.shape
    listed = seg * kblk
    lane_blocks = n_tm * listed // LANES
    digits = -(-int(tile_owner.shape[0] * LANES - 1).bit_length() // 7)
    id_rows = 8
    inputs = (timestream, sample_flags, mode_vectors.T, det_gains.reshape(1, dets))
    msg, ts, keep, vt, g = pl.pallas_call(
        functools.partial(sums_kernel, modes),
        in_specs=[HB] * 4,
        out_specs=[VM] * 5,
        out_shape=[
            shape((2 * modes + MORE, samples), BF16),
            shape((dets, samples)),
            shape((dets, samples), BF16),
            shape((modes, dets)),
            shape((1, dets)),
        ],
        scratch_shapes=[
            pltpu.VMEM((dets, samples), jnp.int32),
            pltpu.SemaphoreType.DMA((4,)),
        ],
        compiler_params=GRANT,
        name="sums",
    )(*(pltpu.with_memory_space_constraint(x, pltpu.HBM) for x in inputs))
    parts_of_all = [msg] + others(msg, "det", n_det)

    rows = -(-filter_gain.shape[0] // LANES) * LANES
    inputs = (tile_ids, block_offsets, tile_owner, jnp.asarray(cosine_table(samples, rows)), pointing)
    h2, toep, pnt, v3, geo = pl.pallas_call(
        functools.partial(prep_kernel, seg, kblk, digits),
        in_specs=[HB] * 5 + [VM] * 2,
        out_specs=[VM] * 5,
        out_shape=[
            shape((2 * samples, samples), BF16),
            shape((samples, 2 * LANES), BF16),
            shape((2 * samples, samples), BF16),
            shape((dets, LANES), BF16),
            shape((listed + id_rows, LANES), BF16),
        ],
        scratch_shapes=[
            pltpu.SMEM(tile_ids.shape, jnp.int32),
            pltpu.SMEM(block_offsets.shape, jnp.int32),
            pltpu.SMEM(tile_owner.shape, jnp.int32),
            pltpu.VMEM((rows, samples), F32),
            pltpu.VMEM(pointing.shape, BF16),
            pltpu.VMEM((8, rows), F32),
            pltpu.SemaphoreType.DMA((5,)),
        ],
        cost_estimate=pl.CostEstimate(flops=10**8, bytes_accessed=3 * 10**6, transcendentals=0),
        compiler_params=GRANT,
        name="prep",
    )(*(pltpu.with_memory_space_constraint(x, pltpu.HBM) for x in inputs), filter_gain.reshape(1, -1), vt)

    paired = n_tm == 8
    mates = [(i, i ^ 1) for i in range(n_tm)]

    nears = [(i, i ^ 2) for i in range(n_tm)]
    fars = [(i, i ^ (4 + 2 * (i % 2))) for i in range(n_tm)]
    block = 2 * listed + id_rows
    first_shape = (1, block + 4 * samples // LANES, LANES) if paired else (n_tm, block, LANES)
    vec, send = pl.pallas_call(
        functools.partial(first_kernel, modes, seg, kblk),
        in_specs=[VM] * 7,
        out_specs=[VM] * 2,
        out_shape=[shape((8, samples)), shape(first_shape, BF16)],
        compiler_params=GRANT,
        name="first",
    )(*parts_of_all, toep, pnt, geo)
    if paired:
        mate_pnt = lax.ppermute(pnt, "tm", mates)
        mate = lax.ppermute(send, "tm", mates)
        pair = jnp.concatenate([send[:, :block], mate[:, :block]], axis=0)
        near = lax.ppermute(pair, "tm", nears)
        far = lax.ppermute(pair, "tm", fars)
        arrived1 = (pair, near, far, lax.ppermute(far, "tm", mates))
        sig, send = pl.pallas_call(
            functools.partial(pair_second_kernel, seg, kblk, digits),
            in_specs=[VM] * 9,
            out_specs=[VM] * 2,
            out_shape=[shape((8, samples)), shape((2, listed, LANES), BF16)],
            compiler_params=GRANT,
            name="second",
        )(*arrived1, mate, vec, toep, pnt, mate_pnt)
        near = lax.ppermute(send, "tm", nears)
        far = lax.ppermute(send, "tm", fars)
    else:
        arrived1 = (lax.all_to_all(send, "tm", 0, 0),)
        sig, send = pl.pallas_call(
            functools.partial(second_kernel, seg, kblk, digits),
            in_specs=[VM] * 5,
            out_specs=[VM] * 2,
            out_shape=[shape((8, samples)), shape((n_tm, listed, LANES), BF16)],
            compiler_params=GRANT,
            name="second",
        )(*arrived1, geo, vec, toep, pnt)
        arrived2 = (lax.all_to_all(send, "tm", 0, 0),)

    cut = EARLY * dets // 4
    operands = (ts, keep, g, v3, sig, h2)
    early, q3, base, scale, same = pl.pallas_call(
        functools.partial(early_kernel, seg, kblk, digits, modes, len(parts_of_all)),
        in_specs=[VM] * (7 + len(parts_of_all) + len(arrived1)),
        out_specs=[VM] * 5,
        out_shape=[
            shape((cut, samples), BF16),
            shape((LANES, samples), BF16),
            shape((LANES, LANES)),
            shape((LANES, LANES)),
            shape((lane_blocks, LANES, LANES), BF16),
        ],
        cost_estimate=pl.CostEstimate(flops=5 * 10**8, bytes_accessed=2 * 10**6, transcendentals=0),
        compiler_params=GRANT,
        name="early",
    )(*operands, *parts_of_all, vec, *arrived1)
    after = vec
    if paired:
        far, base = lax.optimization_barrier((far, base))
        arrived2 = (send, near, far, lax.ppermute(far, "tm", mates))
        after = far
    cleaned = pl.pallas_call(
        late_kernel,
        in_specs=[VM] * 9,
        out_specs=HB,
        out_shape=shape((dets, samples), BF16),
        scratch_shapes=[pltpu.VMEM((dets - cut, samples), BF16), pltpu.SemaphoreType.DMA((2,))],
        cost_estimate=pl.CostEstimate(flops=5 * 10**8, bytes_accessed=2 * 10**6, transcendentals=0),
        compiler_params=GRANT,
        name="late",
    )(*operands, q3, early, after)

    tile = pl.pallas_call(
        tile_kernel,
        in_specs=[VM] * (len(arrived2) + 3),
        out_specs=VM,
        out_shape=shape((1, LANES, LANES)),
        compiler_params=GRANT,
        name="tile",
    )(*arrived2, base, scale, same)
    return tile, cleaned


def solution(mesh):
    def step(*args):
        return shards(mesh.shape["det"], mesh.shape["tm"], *args)

    step = jax.shard_map(
        step,
        mesh=mesh,
        in_specs=(
            P("det", "tm"),
            P("det", "tm"),
            P("tm", None, None, None),
            P("tm", None),
            P("tm", None),
            P(),
            P("det"),
            P("det", None),
            P(),
        ),
        out_specs=(P(("det", "tm"), None, None), P("det", "tm")),
        check_vma=False,
    )
    return step
```

```python
import functools
import math

import jax
import jax.numpy as jnp
import numpy as np
from jax import lax
from jax.experimental import pallas as pl
from jax.experimental.pallas import tpu as pltpu
from jax.sharding import PartitionSpec as P

F32 = jnp.float32
BF16 = jnp.bfloat16
LANES = 128
BASE = 128
EXT = 16
EARLY = 3
MORE = 8
NN = (((1,), (0,)), ((), ()))


def mm(a, b, dims=NN):
    return lax.dot_general(a, b, dims, preferred_element_type=F32)


def split(x):
    hi = x.astype(BF16)
    return hi, (x - hi.astype(F32)).astype(BF16)


def iota(shape, axis):
    return lax.broadcasted_iota(jnp.int32, shape, axis)


def cosine_table(flen, rows):
    f = np.arange(rows)[:, None]
    n = np.arange(flen)[None, :]
    scale = np.where((f == 0) | (f == flen // 2), 1.0, 2.0) / flen
    scale = np.where(f <= flen // 2, scale, 0.0)
    return (scale * np.cos(2.0 * math.pi * ((f * n) % flen) / flen)).astype(np.float32)


def sums_kernel(modes, ts_hbm, flag_hbm, v_hbm, g_hbm, msg_ref, ts_ref, keep_ref, v_ref, g_ref, flag_ref, sem):
    dets, samples = ts_ref.shape
    streams = [(v_hbm, v_ref), (g_hbm, g_ref), (flag_hbm, flag_ref), (ts_hbm, ts_ref)]
    copies = [pltpu.make_async_copy(a, b, sem.at[i]) for i, (a, b) in enumerate(streams)]
    for copy in copies:
        copy.start()
    copies[0].wait()
    copies[1].wait()
    vt = v_ref[...]
    g = g_ref[...]
    row = iota((EXT, dets), 0)
    left1 = jnp.concatenate([vt, jnp.where(row < 2, g, 0.0)], axis=0)
    left2 = jnp.concatenate([vt * g, jnp.where((row >= 2) & (row < 4), g * g, 0.0)], axis=0)
    hi1, lo1 = split(left1)
    hi2, lo2 = split(left2)
    left1 = jnp.concatenate([hi1, lo1], axis=0)
    left2 = jnp.concatenate([hi2, lo2], axis=0)
    u = jnp.sum(vt * g, axis=1, keepdims=True)
    square = jnp.sum(g * g, axis=1, keepdims=True)
    lane = iota((modes, samples), 1)
    u = jnp.sum(jnp.where(lane == iota((modes, samples), 0), u, 0.0), axis=0, keepdims=True)
    u = jnp.where(iota((1, samples), 1) == modes, square, u)
    n = modes + EXT
    copies[2].wait()
    keep = (1 - flag_ref[...]).astype(F32)
    keep_ref[...] = keep.astype(BF16)
    both = mm(left2, keep.astype(BF16))
    acc2 = both[:n] + both[n:]
    copies[3].wait()
    x_hi, x_lo = split(ts_ref[...] * keep_ref[...].astype(F32))
    both = mm(left1, x_hi)
    acc1 = both[:n] + both[n:] + mm(hi1, x_lo)
    msg_ref[0:modes] = acc1[0:modes].astype(BF16)
    msg_ref[modes : 2 * modes] = acc2[0:modes].astype(BF16)
    row = iota((MORE, samples), 0)
    ext = acc1[modes : modes + MORE] + acc2[modes : modes + MORE] + jnp.where((row >= 4) & (row < 6), u, 0.0)
    hi = ext.astype(BF16).astype(F32)
    msg_ref[2 * modes :] = jnp.where(row % 2 == 1, ext - hi, hi).astype(BF16)


def prep_kernel(seg, kblk, digits, tids_hbm, offs_hbm, owner_hbm, cos_hbm, point_hbm, gain_ref, v_ref,
                h2_ref, toep_ref, pnt_ref, v3_ref, geo_ref,
                tids_ref, offs_ref, owner_ref, cos_ref, point_ref, wide_ref, sem):
    streams = [(cos_hbm, cos_ref), (point_hbm, point_ref), (tids_hbm, tids_ref), (offs_hbm, offs_ref),
               (owner_hbm, owner_ref)]
    copies = [pltpu.make_async_copy(a, b, sem.at[i]) for i, (a, b) in enumerate(streams)]
    for copy in copies:
        copy.start()
    flen = cos_ref.shape[1]
    vt = v_ref[...]
    vhi = vt.astype(BF16).astype(F32)
    pad = jnp.zeros((LANES - 3 * vt.shape[0], vt.shape[1]), F32)
    v3_ref[...] = jnp.concatenate([vhi, vhi, vt - vhi, pad], axis=0).T.astype(BF16)
    copies[0].wait()
    wide_ref[...] = jnp.zeros_like(wide_ref)
    wide_ref[0:1, 0 : gain_ref.shape[1]] = gain_ref[...]
    h = lax.dot_general(wide_ref[...], cos_ref[...], NN, precision=lax.Precision.HIGHEST, preferred_element_type=F32)
    base = jnp.broadcast_to(h[0:1], (LANES, flen))
    base = pltpu.roll(base, 0, 1, stride=1, stride_axis=0)
    base_hi, base_lo = split(base)
    blocks = flen // LANES
    for a in range(blocks):
        for b in range(blocks):
            c = (b - a) % blocks
            to = slice(b * LANES, (b + 1) * LANES)
            h2_ref[a * LANES : (a + 1) * LANES, to] = base_hi[:, c * LANES : (c + 1) * LANES]
            h2_ref[flen + a * LANES : flen + (a + 1) * LANES, to] = base_lo[:, c * LANES : (c + 1) * LANES]
    for c in range(blocks):
        at = slice(c * LANES, (c + 1) * LANES)
        toep_ref[at, 0:LANES] = base_hi[:, at]
        toep_ref[at, LANES : 2 * LANES] = base_lo[:, at]
    for copy in copies[1:]:
        copy.wait()
    listed = seg * kblk
    row16 = iota((listed, LANES), 0)
    squares = jnp.zeros((listed, LANES), F32)
    ext = geo_ref.shape[0] - listed
    row_x = iota((ext, LANES), 0)
    lane_x = iota((ext, LANES), 1)
    ids = jnp.zeros((ext, LANES), F32)
    for k in range(kblk):
        for s in range(seg):
            j = k * seg + s
            p = point_ref[s, k]
            span, tile = p.shape
            pnt_ref[s * span : (s + 1) * span, k * tile : (k + 1) * tile] = p
            pnt_ref[flen + k * tile : flen + (k + 1) * tile, s * span : (s + 1) * span] = p.T
            p = p.astype(F32)
            squares = jnp.where(row16 == j, jnp.sum(p * p, axis=0, keepdims=True), squares)
            target = owner_ref[tids_ref[s, k]] * LANES + offs_ref[s, k]
            for d in range(digits):
                ids = jnp.where((row_x == d) & (lane_x % listed == j), (target % BASE).astype(F32), ids)
                target = target // BASE
    geo_ref[0:listed] = squares.astype(BF16)
    geo_ref[listed:] = ids.astype(BF16)


def filtered(vectors, toep_ref):
    blocks = vectors[0].shape[1] // LANES
    rows = -(-2 * blocks * len(vectors) // EXT) * EXT
    row = iota((rows, LANES), 0)
    halves = []
    for b in vectors:
        hi, lo = split(b)
        halves += [hi.astype(F32), lo.astype(F32)]
    left = []
    for c in range(blocks):
        block = jnp.zeros((rows, LANES), F32)
        for i, half in enumerate(halves):
            for m in range(blocks):
                to = i * blocks + (m + c) % blocks
                block = jnp.where(row == to, half[:, m * LANES : (m + 1) * LANES], block)
        left.append(block.astype(BF16))
    z = mm(jnp.concatenate(left, axis=1), toep_ref[...])
    z = z[:, 0:LANES] + z[:, LANES:]
    out = []
    for i in range(len(vectors)):
        at = 2 * i * blocks
        out.append(z[at : at + blocks] + z[at + blocks : at + 2 * blocks])
    return out


def project(z, pn, seg, kblk):
    listed = seg * kblk
    hi, lo = split(z)
    hi, lo = hi.astype(F32), lo.astype(F32)
    row = iota((2 * listed, LANES), 0)
    left = []
    for s in range(seg):
        value = jnp.where(row < listed, hi[s : s + 1], lo[s : s + 1])
        left.append(jnp.where(row % seg == s, value, 0.0).astype(BF16))
    out = mm(jnp.concatenate(left, axis=1), pn)
    out = out[:listed] + out[listed:]
    row = iota((listed, LANES), 0)
    proj = out[:, 0:LANES]
    for k in range(1, kblk):
        proj = jnp.where(row // seg == k, out[:, k * LANES : (k + 1) * LANES], proj)
    return proj


def first_kernel(modes, seg, kblk, m0, m1, m2, m3, toep_ref, pnt_ref, geo_ref,
                 vec_ref, send_ref):
    tot = m0[...].astype(F32) + m1[...].astype(F32) + m2[...].astype(F32) + m3[...].astype(F32)
    ext = tot[2 * modes :]
    u_row = ext[4:5, 0:LANES] + ext[5:6, 0:LANES]
    u_col = jnp.sum(jnp.where(iota((modes, LANES), 0) == iota((modes, LANES), 1), u_row, 0.0), axis=1, keepdims=True)
    square = jnp.sum(jnp.where(iota((1, LANES), 1) == modes, u_row, 0.0), axis=1, keepdims=True)
    b1 = ext[0:1] + ext[1:2] - jnp.sum(u_col * tot[0:modes], axis=0, keepdims=True)
    b2 = ext[2:3] + ext[3:4] - jnp.sum(u_col * tot[modes : 2 * modes], axis=0, keepdims=True)
    row = iota((8, b1.shape[1]), 0)
    vec_ref[...] = jnp.where(row == 0, b1, jnp.where(row == 1, b2, jnp.where(row == 2, square, 0.0)))
    (z,) = filtered([b1], toep_ref)
    proj = project(z, pnt_ref[0 : b1.shape[1]], seg, kblk).astype(BF16)
    geo = geo_ref[...]
    listed = seg * kblk
    for t in range(send_ref.shape[0]):
        send_ref[t, 0:listed] = proj
        send_ref[t, listed : listed + geo.shape[0]] = geo
    if send_ref.shape[1] > listed + geo.shape[0]:
        blocks = b1.shape[1] // LANES
        row = iota((4 * blocks, LANES), 0)
        tail = jnp.zeros((4 * blocks, LANES), F32)
        for i, half in enumerate(split(b1) + split(b2)):
            for m in range(blocks):
                tail = jnp.where(row == i * blocks + m, half[:, m * LANES : (m + 1) * LANES].astype(F32), tail)
        send_ref[0, listed + geo.shape[0] :] = tail.astype(BF16)


def row_ids(ext, digits):
    ext = ext.astype(F32)
    ids = ext[0:1]
    for d in range(1, digits):
        ids = ids + float(BASE**d) * ext[d : d + 1]
    return ids


def groups(refs, listed, digits):
    per = LANES // listed
    slots = [(ref, i) for ref in refs for i in range(ref.shape[0])]
    for b in range(len(slots) // per):
        part = slots[b * per : (b + 1) * per]
        lane = iota((1, LANES), 1)
        ids = jnp.zeros((1, LANES), F32)
        for n, (ref, i) in enumerate(part):
            ids = jnp.where(lane // listed == n, row_ids(ref[i, 2 * listed :], digits), ids)
        sums = jnp.concatenate([ref[i, 0:listed] for ref, i in part], axis=0)
        squares = jnp.concatenate([ref[i, listed : 2 * listed] for ref, i in part], axis=0)
        yield ids, sums, squares


def upright(ids, count):
    eye = iota((count, LANES), 0) == iota((count, LANES), 1)
    return jnp.sum(jnp.where(eye, ids, 0.0), axis=1, keepdims=True)


def fetch(parts, own, vec_ref):
    psum = jnp.zeros((own.shape[0], LANES), F32)
    wsum = jnp.zeros((own.shape[0], LANES), F32)
    for ids, sums, squares in parts:
        same = (own == ids).astype(F32).astype(BF16)
        psum = psum + mm(same, sums)
        wsum = wsum + mm(same, squares)
    return (psum / (1.0 + vec_ref[2:3, 0:LANES] * wsum)).astype(BF16).astype(F32)


def signal(fetched, pt, seg, kblk):
    samples = pt.shape[1]
    listed = seg * kblk
    row = iota((listed, LANES), 0)
    wide = [jnp.where(row // seg == k, fetched, 0.0).astype(BF16) for k in range(kblk)]
    spread = mm(jnp.concatenate(wide, axis=1), pt)
    row = iota((listed, samples), 0)
    lane = iota((listed, samples), 1)
    return jnp.sum(jnp.where(lane // (samples // seg) == row % seg, spread, 0.0), axis=0, keepdims=True)


def second_kernel(seg, kblk, digits, all_ref, geo_ref, vec_ref, toep_ref, pnt_ref, sig_ref, send_ref):
    listed = seg * kblk
    samples = vec_ref.shape[1]
    own = upright(row_ids(geo_ref[listed:], digits), listed)
    fetched = fetch(list(groups([all_ref], listed, digits)), own, vec_ref)
    sig = signal(fetched, pnt_ref[samples:], seg, kblk)
    sig_ref[...] = jnp.broadcast_to(sig, sig_ref.shape)
    (z,) = filtered([vec_ref[0:1] - vec_ref[1:2] * sig], toep_ref)
    proj = project(z, pnt_ref[0:samples], seg, kblk).astype(BF16)
    for t in range(send_ref.shape[0]):
        send_ref[t] = proj


def pair_second_kernel(seg, kblk, digits, pair_ref, near_ref, far_ref, cross_ref, mate_ref, vec_ref, toep_ref, pnt_ref,
                       mate_pnt_ref, sig_ref, send_ref):
    listed = seg * kblk
    samples = vec_ref.shape[1]
    parts = list(groups([pair_ref, near_ref, far_ref, cross_ref], listed, digits))
    fetched = fetch(parts, upright(parts[0][0], 2 * listed), vec_ref)
    sig = signal(fetched[0:listed], pnt_ref[samples:], seg, kblk)
    mate_sig = signal(fetched[listed:], mate_pnt_ref[samples:], seg, kblk)
    sig_ref[...] = jnp.broadcast_to(sig, sig_ref.shape)
    rest = vec_ref[0:1] - vec_ref[1:2] * sig
    cuts = samples // LANES
    tail = mate_ref[0, pair_ref.shape[1] :].astype(F32)
    halves = [
        jnp.concatenate([tail[i * cuts + m : i * cuts + m + 1] for m in range(cuts)], axis=1) for i in range(4)
    ]
    mate_rest = halves[0] + halves[1] - (halves[2] + halves[3]) * mate_sig
    z, mate_z = filtered([rest, mate_rest], toep_ref)
    send_ref[0] = project(z, pnt_ref[0:samples], seg, kblk).astype(BF16)
    send_ref[1] = project(mate_z, mate_pnt_ref[0:samples], seg, kblk).astype(BF16)


def stacked_modes(modes, messages, sig_ref):
    tot = sum(message[0 : 2 * modes].astype(F32) for message in messages)
    q_hi, q_lo = split(tot[0:modes] - tot[modes:] * sig_ref[0:1])
    pad = jnp.zeros((LANES - 3 * modes, q_hi.shape[1]), BF16)
    return jnp.concatenate([q_hi, q_lo, q_hi, pad], axis=0)


def clean_rows(at, q3, ts_ref, keep_ref, g_ref, v3_ref, sig_ref, h2_ref):
    samples = ts_ref.shape[1]
    sig = sig_ref[0:1]
    count = at.stop - at.start
    eye = iota((count, count), 0) == iota((count, count), 1)
    g_col = jnp.sum(jnp.where(eye, g_ref[:, at], 0.0), axis=1, keepdims=True)
    rest = (ts_ref[at] - g_col * sig) * keep_ref[at].astype(F32) - mm(v3_ref[at], q3)
    rest = rest.astype(BF16)
    return (mm(rest, h2_ref[0:samples]) + mm(rest, h2_ref[samples:])).astype(BF16)


def early_kernel(seg, kblk, digits, modes, count, *refs):
    operands, messages, vec_ref, all_refs = refs[:6], refs[6 : 6 + count], refs[6 + count], refs[7 + count : -5]
    early_ref, q3_ref, base_ref, scale_ref, same_ref = refs[-5:]
    q3 = stacked_modes(modes, messages, operands[4])
    q3_ref[...] = q3
    early_ref[...] = clean_rows(slice(0, early_ref.shape[0]), q3, *operands)
    psum = jnp.zeros((LANES, LANES), F32)
    wsum = jnp.zeros((LANES, LANES), F32)
    first = (lax.axis_index("det") * lax.axis_size("tm") + lax.axis_index("tm")) * LANES
    mine = (iota((LANES, LANES), 0) + first).astype(F32)
    for b, (ids, sums, squares) in enumerate(groups(all_refs, seg * kblk, digits)):
        same = (mine == ids).astype(F32).astype(BF16)
        same_ref[b] = same
        psum = psum + mm(same, sums)
        wsum = wsum + mm(same, squares)
    wsum = 1.0 + vec_ref[2:3, 0:LANES] * wsum
    scale = jnp.sqrt(wsum) / wsum
    scale_ref[...] = scale
    base_ref[...] = psum * scale


def late_kernel(*refs):
    operands, q3_ref, early_ref, (out_hbm, late_ref, sem) = refs[:6], refs[6], refs[7], refs[-3:]
    cut, dets = early_ref.shape[0], operands[0].shape[0]
    copies = [
        pltpu.make_async_copy(early_ref, out_hbm.at[pl.ds(0, cut)], sem.at[0]),
        pltpu.make_async_copy(late_ref, out_hbm.at[pl.ds(cut, dets - cut)], sem.at[1]),
    ]
    copies[0].start()
    late_ref[...] = clean_rows(slice(cut, dets), q3_ref[...], *operands)
    copies[1].start()
    for copy in copies:
        copy.wait()


def tile_kernel(*refs):
    all_refs, (base_ref, scale_ref, same_ref, out_ref) = refs[:-4], refs[-4:]
    slots = [ref[i] for ref in all_refs for i in range(ref.shape[0])]
    per = LANES // slots[0].shape[0]
    psum = jnp.zeros((LANES, LANES), F32)
    for b in range(same_ref.shape[0]):
        psum = psum + mm(same_ref[b], jnp.concatenate(slots[b * per : (b + 1) * per], axis=0))
    out_ref[0] = base_ref[...] + psum * scale_ref[...]


VM = pl.BlockSpec(memory_space=pltpu.VMEM)
HB = pl.BlockSpec(memory_space=pltpu.HBM)
SM = pl.BlockSpec(memory_space=pltpu.SMEM)
GRANT = pltpu.CompilerParams(vmem_limit_bytes=12 * 2**20)


def shape(dims, dtype=F32):
    return jax.ShapeDtypeStruct(dims, dtype)


def others(x, axis, n):
    if n & (n - 1) == 0:
        pairs = [[(i, i ^ k) for i in range(n)] for k in range(1, n)]
    else:
        pairs = [[(i, (i + k) % n) for i in range(n)] for k in range(1, n)]
    return [lax.ppermute(x, axis, p) for p in pairs]


def shards(n_det, n_tm, timestream, sample_flags, pointing, tile_ids, block_offsets, tile_owner, det_gains,
           mode_vectors, filter_gain):
    dets, samples = timestream.shape
    modes = mode_vectors.shape[1]
    seg, kblk = tile_ids.shape
    listed = seg * kblk
    lane_blocks = n_tm * listed // LANES
    digits = -(-int(tile_owner.shape[0] * LANES - 1).bit_length() // 7)
    id_rows = 8
    inputs = (timestream, sample_flags, mode_vectors.T, det_gains.reshape(1, dets))
    msg, ts, keep, vt, g = pl.pallas_call(
        functools.partial(sums_kernel, modes),
        in_specs=[HB] * 4,
        out_specs=[VM] * 5,
        out_shape=[
            shape((2 * modes + MORE, samples), BF16),
            shape((dets, samples)),
            shape((dets, samples), BF16),
            shape((modes, dets)),
            shape((1, dets)),
        ],
        scratch_shapes=[
            pltpu.VMEM((dets, samples), jnp.int32),
            pltpu.SemaphoreType.DMA((4,)),
        ],
        compiler_params=GRANT,
        name="sums",
    )(*(pltpu.with_memory_space_constraint(x, pltpu.HBM) for x in inputs))
    if n_det == 4:
        parts_of_all = [msg]
        for ks in ((1, 2), (2, 1), (3, 3)):
            hops = [(d * n_tm + t, (d ^ ks[t % 2]) * n_tm + t) for d in range(n_det) for t in range(n_tm)]
            parts_of_all.append(lax.ppermute(msg, ("det", "tm"), hops))
    else:
        parts_of_all = [msg] + others(msg, "det", n_det)

    rows = -(-filter_gain.shape[0] // LANES) * LANES
    inputs = (tile_ids, block_offsets, tile_owner, jnp.asarray(cosine_table(samples, rows)), pointing)
    h2, toep, pnt, v3, geo = pl.pallas_call(
        functools.partial(prep_kernel, seg, kblk, digits),
        in_specs=[HB] * 5 + [VM] * 2,
        out_specs=[VM] * 5,
        out_shape=[
            shape((2 * samples, samples), BF16),
            shape((samples, 2 * LANES), BF16),
            shape((2 * samples, samples), BF16),
            shape((dets, LANES), BF16),
            shape((listed + id_rows, LANES), BF16),
        ],
        scratch_shapes=[
            pltpu.SMEM(tile_ids.shape, jnp.int32),
            pltpu.SMEM(block_offsets.shape, jnp.int32),
            pltpu.SMEM(tile_owner.shape, jnp.int32),
            pltpu.VMEM((rows, samples), F32),
            pltpu.VMEM(pointing.shape, BF16),
            pltpu.VMEM((8, rows), F32),
            pltpu.SemaphoreType.DMA((5,)),
        ],
        cost_estimate=pl.CostEstimate(flops=10**8, bytes_accessed=3 * 10**6, transcendentals=0),
        compiler_params=GRANT,
        name="prep",
    )(*(pltpu.with_memory_space_constraint(x, pltpu.HBM) for x in inputs), filter_gain.reshape(1, -1), vt)

    paired = n_tm == 8
    mates = [(i, i ^ 1) for i in range(n_tm)]

    nears = [(i, i ^ 2) for i in range(n_tm)]
    fars = [(i, i ^ (4 + 2 * (i % 2))) for i in range(n_tm)]
    block = 2 * listed + id_rows
    first_shape = (1, block + 4 * samples // LANES, LANES) if paired else (n_tm, block, LANES)
    vec, send = pl.pallas_call(
        functools.partial(first_kernel, modes, seg, kblk),
        in_specs=[VM] * 7,
        out_specs=[VM] * 2,
        out_shape=[shape((8, samples)), shape(first_shape, BF16)],
        compiler_params=GRANT,
        name="first",
    )(*parts_of_all, toep, pnt, geo)
    if paired:
        mate_pnt = lax.ppermute(pnt, "tm", mates)
        mate = lax.ppermute(send, "tm", mates)
        pair = jnp.concatenate([send[:, :block], mate[:, :block]], axis=0)
        near = lax.ppermute(pair, "tm", nears)
        far = lax.ppermute(pair, "tm", fars)
        arrived1 = (pair, near, far, lax.ppermute(far, "tm", mates))
        sig, send = pl.pallas_call(
            functools.partial(pair_second_kernel, seg, kblk, digits),
            in_specs=[VM] * 9,
            out_specs=[VM] * 2,
            out_shape=[shape((8, samples)), shape((2, listed, LANES), BF16)],
            compiler_params=GRANT,
            name="second",
        )(*arrived1, mate, vec, toep, pnt, mate_pnt)
        near = lax.ppermute(send, "tm", nears)
        far = lax.ppermute(send, "tm", fars)
    else:
        arrived1 = (lax.all_to_all(send, "tm", 0, 0),)
        sig, send = pl.pallas_call(
            functools.partial(second_kernel, seg, kblk, digits),
            in_specs=[VM] * 5,
            out_specs=[VM] * 2,
            out_shape=[shape((8, samples)), shape((n_tm, listed, LANES), BF16)],
            compiler_params=GRANT,
            name="second",
        )(*arrived1, geo, vec, toep, pnt)
        arrived2 = (lax.all_to_all(send, "tm", 0, 0),)

    cut = EARLY * dets // 4
    operands = (ts, keep, g, v3, sig, h2)
    early, q3, base, scale, same = pl.pallas_call(
        functools.partial(early_kernel, seg, kblk, digits, modes, len(parts_of_all)),
        in_specs=[VM] * (7 + len(parts_of_all) + len(arrived1)),
        out_specs=[VM] * 5,
        out_shape=[
            shape((cut, samples), BF16),
            shape((LANES, samples), BF16),
            shape((LANES, LANES)),
            shape((LANES, LANES)),
            shape((lane_blocks, LANES, LANES), BF16),
        ],
        cost_estimate=pl.CostEstimate(flops=5 * 10**8, bytes_accessed=2 * 10**6, transcendentals=0),
        compiler_params=GRANT,
        name="early",
    )(*operands, *parts_of_all, vec, *arrived1)
    after = vec
    if paired:
        far, base = lax.optimization_barrier((far, base))
        arrived2 = (send, near, far, lax.ppermute(far, "tm", mates))
        after = far
    cleaned = pl.pallas_call(
        late_kernel,
        in_specs=[VM] * 9,
        out_specs=HB,
        out_shape=shape((dets, samples), BF16),
        scratch_shapes=[pltpu.VMEM((dets - cut, samples), BF16), pltpu.SemaphoreType.DMA((2,))],
        cost_estimate=pl.CostEstimate(flops=5 * 10**8, bytes_accessed=2 * 10**6, transcendentals=0),
        compiler_params=GRANT,
        name="late",
    )(*operands, q3, early, after)

    tile = pl.pallas_call(
        tile_kernel,
        in_specs=[VM] * (len(arrived2) + 3),
        out_specs=VM,
        out_shape=shape((1, LANES, LANES)),
        compiler_params=GRANT,
        name="tile",
    )(*arrived2, base, scale, same)
    return tile, cleaned


def solution(mesh):
    def step(*args):
        return shards(mesh.shape["det"], mesh.shape["tm"], *args)

    step = jax.shard_map(
        step,
        mesh=mesh,
        in_specs=(
            P("det", "tm"),
            P("det", "tm"),
            P("tm", None, None, None),
            P("tm", None),
            P("tm", None),
            P(),
            P("det"),
            P("det", None),
            P(),
        ),
        out_specs=(P(("det", "tm"), None, None), P("det", "tm")),
        check_vma=False,
    )
    return step
```
